32 devices in a mesh: dp: 8 (over z, x), row: 2 (over y), col: 2 (over core).
Axes of the slice: x: 2, y: 2, z: 4, core: 2. Of those that a mesh axis runs over, the one named last changes fastest.
Arguments:
- layer_input: bfloat16 [512, 16, 1024], P(None, ('dp', 'row'), 'col'), may hold values from -6 to 6
- cotangent: bfloat16 [512, 16, 1024], P(None, ('dp', 'row'), 'col'), may hold values from -6 to 6
- lengths: int32 [32], replicated, may hold values from 16 to 976, as said below
- dealing: int32 [32], replicated, may hold values from 0 to 31, as said below
- w_query: bfloat16 [1024, 1024], P(None, 'col'), may hold values from -0.1875 to 0.1875
- w_key: bfloat16 [1024, 1024], P(None, 'col'), may hold values from -0.1875 to 0.1875
- w_value: bfloat16 [1024, 1024], P(None, 'col'), may hold values from -0.1875 to 0.1875
- bias_query: float32 [1024], P('col'), may hold values from -3 to 3
- bias_value: float32 [1024], P('col'), may hold values from -3 to 3
- w_out: bfloat16 [1024, 1024], P('col'), may hold values from -0.1875 to 0.1875
- bias_out: float32 [1024], P('col'), may hold values from -3 to 3
- w_up: bfloat16 [1024, 4096], P(None, 'col'), may hold values from -0.1875 to 0.1875
- bias_up: float32 [4096], P('col'), may hold values from -3 to 3
- w_down: bfloat16 [4096, 1024], P('col'), may hold values from -0.09375 to 0.09375
- bias_down: float32 [1024], P('col'), may hold values from -3 to 3
- gain_attention_in: float32 [1024], P('col'), may hold values from 0.5 to 1.5
- shift_attention_in: float32 [1024], P('col'), may hold values from -2 to 2
- gain_attention_out: float32 [1024], P('col'), may hold values from 0.5 to 1.5
- shift_attention_out: float32 [1024], P('col'), may hold values from -2 to 2
- gain_ffn_in: float32 [1024], P('col'), may hold values from 0.5 to 1.5
- shift_ffn_in: float32 [1024], P('col'), may hold values from -2 to 2
- gain_ffn_out: float32 [1024], P('col'), may hold values from 0.5 to 1.5
- shift_ffn_out: float32 [1024], P('col'), may hold values from -2 to 2
Outputs:
- output: bfloat16 [512, 16, 1024], P(None, ('dp', 'row'), 'col')
- input_grad: bfloat16 [512, 16, 1024], P(None, ('dp', 'row'), 'col')
- grad_w_query: float32 [1024, 1024], P('row', 'col')
- grad_w_key: float32 [1024, 1024], P('row', 'col')
- grad_w_value: float32 [1024, 1024], P('row', 'col')
- grad_bias_query: float32 [1024], P('col')
- grad_bias_value: float32 [1024], P('col')
- grad_w_out: float32 [1024, 1024], P('col', 'row')
- grad_bias_out: float32 [1024], P('col')
- grad_w_up: float32 [1024, 4096], P('row', 'col')
- grad_bias_up: float32 [4096], P('col')
- grad_w_down: float32 [4096, 1024], P('col', 'row')
- grad_bias_down: float32 [1024], P('col')
- grad_gain_attention_in: float32 [1024], P('col')
- grad_shift_attention_in: float32 [1024], P('col')
- grad_gain_attention_out: float32 [1024], P('col')
- grad_shift_attention_out: float32 [1024], P('col')
- grad_gain_ffn_in: float32 [1024], P('col')
- grad_shift_ffn_in: float32 [1024], P('col')
- grad_gain_ffn_out: float32 [1024], P('col')
- grad_shift_ffn_out: float32 [1024], P('col')
The draws below stay inside these ranges and needn't reach their ends.
Inputs may be any that keep to these rules, and one draw needn't show every extreme that they name: Every length is a multiple of 16; for every group g the lengths of sequences dealing[g * 4] to dealing[g * 4 + 3] sum to 1024. `dealing`: A permutation of the 32 sequences.
All inputs are finite; a program needn't handle non-finite values.
Results may differ from the reference program's by a relative error of at most 0.023.
Values may be sent and summed in bfloat16 or wider, within the bound.
No kernel may reach another device: no remote copies, remote signals or barrier semaphores. Data moves between devices by JAX's collectives and lax.ppermute only.
A program may use at most 128 MiB of HBM per device.

```python
import math
import jax
import jax.numpy as jnp
from jax import lax

D = 1024
HEADS = 16
DH = 64
FF = 4096
TOK_GRP = 1024
SEQ_GRP = 4
GRAIN = 16
NSEQ = 32
TOKENS = 8192
N_DP = 8


def deal_tables(key):
    base = jax.random.fold_in(key, 11)
    key_perm, key_cut, key_big, key_roll = jax.random.split(base, 4)
    groups = NSEQ // SEQ_GRP
    units = TOK_GRP // GRAIN

    def cuts_for(sub_key):
        picks = jax.random.permutation(sub_key, units - 1)[:SEQ_GRP - 1].astype(jnp.int32) + 1
        edges = jnp.concatenate([jnp.zeros((1,), jnp.int32), jnp.sort(picks), jnp.full((1,), units, jnp.int32)])
        return edges[1:] - edges[:-1]
    parts = jax.vmap(cuts_for)(jax.random.split(key_cut, groups))
    big_group = jax.random.randint(key_big, (), 0, groups)
    roll_by = jax.random.randint(key_roll, (), 0, SEQ_GRP)
    big_row = jnp.roll(jnp.concatenate([jnp.full((1,), units - SEQ_GRP + 1, jnp.int32), jnp.ones((SEQ_GRP - 1,), jnp.int32)]), roll_by)
    parts = jnp.where((lax.iota(jnp.int32, groups) == big_group)[:, None], big_row[None, :], parts)
    slot_len = (parts * GRAIN).reshape(-1).astype(jnp.int32)
    dealing = jax.random.permutation(key_perm, NSEQ).astype(jnp.int32)
    lengths = jnp.zeros((NSEQ,), jnp.int32).at[dealing].set(slot_len)
    return (lengths, dealing)


def draw_lengths(key, part):
    return deal_tables(key)[0]


def draw_dealing(key, part):
    return deal_tables(key)[1]


def shard_levels(rng, shape, cuts, smallest, high):
    factor_of = 1.0
    for position, blocks in cuts:
        heights = jax.random.uniform(jax.random.fold_in(jax.random.fold_in(rng, 6), position), (blocks,), jnp.float32, smallest / len(cuts), high / len(cuts))
        factor_of = factor_of * jnp.repeat(jnp.exp(heights), shape[position] // blocks).reshape((-1,) + (1,) * (len(shape) - 1 - position))
    return factor_of


def scatter_about(own_key, shape, width, bound, shards=(), kind=jnp.bfloat16):
    result = jax.random.normal(own_key, shape, jnp.float32) * width
    if len(shards) > 0:
        result = shard_levels(own_key, shape, shards, -0.22, 0.18) * result
    return jnp.clip(result, min=-bound, max=bound).astype(kind)


def setup_inputs(seed: int = 0) -> dict:
    streams_of = jax.random.split(jax.random.key(seed), 24)
    return {
        "layer_input": scatter_about(streams_of[0], (TOKENS // GRAIN, GRAIN, D), 1.0, 6.0, ((1, 16), (2, 2))),
        "cotangent": scatter_about(streams_of[1], (TOKENS // GRAIN, GRAIN, D), 1.0, 6.0, ((1, 16), (2, 2))),
        "lengths": draw_lengths(jax.random.fold_in(streams_of[23], 71), 0),
        "dealing": draw_dealing(jax.random.fold_in(streams_of[23], 71), 0),
        "w_query": scatter_about(streams_of[4], (D, D), D ** -0.5, 0.1875, ((1, 2),)),
        "w_key": scatter_about(streams_of[5], (D, D), D ** -0.5, 0.1875, ((1, 2),)),
        "w_value": scatter_about(streams_of[6], (D, D), D ** -0.5, 0.1875, ((1, 2),)),
        "bias_query": scatter_about(streams_of[7], (D,), 0.5, 3.0, ((0, 2),), jnp.float32),
        "bias_value": scatter_about(streams_of[8], (D,), 0.5, 3.0, ((0, 2),), jnp.float32),
        "w_out": scatter_about(streams_of[9], (D, D), D ** -0.5, 0.1875, ((0, 2),)),
        "bias_out": scatter_about(streams_of[10], (D,), 0.5, 3.0, ((0, 2),), jnp.float32),
        "w_up": scatter_about(streams_of[11], (D, FF), D ** -0.5, 0.1875, ((1, 2),)),
        "bias_up": scatter_about(streams_of[12], (FF,), 0.5, 3.0, ((0, 2),), jnp.float32),
        "w_down": scatter_about(streams_of[13], (FF, D), FF ** -0.5, 0.09375, ((0, 2),)),
        "bias_down": scatter_about(streams_of[14], (D,), 0.5, 3.0, ((0, 2),), jnp.float32),
        "gain_attention_in": jnp.clip(1.0 + 0.1 * jax.random.normal(streams_of[15], (D,), jnp.float32), 0.5, 1.5),
        "shift_attention_in": scatter_about(streams_of[16], (D,), 0.3, 2.0, ((0, 2),), jnp.float32),
        "gain_attention_out": jnp.clip(1.0 + 0.1 * jax.random.normal(streams_of[17], (D,), jnp.float32), 0.5, 1.5),
        "shift_attention_out": scatter_about(streams_of[18], (D,), 0.3, 2.0, ((0, 2),), jnp.float32),
        "gain_ffn_in": jnp.clip(1.0 + 0.1 * jax.random.normal(streams_of[19], (D,), jnp.float32), 0.5, 1.5),
        "shift_ffn_in": scatter_about(streams_of[20], (D,), 0.3, 2.0, ((0, 2),), jnp.float32),
        "gain_ffn_out": jnp.clip(1.0 + 0.1 * jax.random.normal(streams_of[21], (D,), jnp.float32), 0.5, 1.5),
        "shift_ffn_out": scatter_about(streams_of[22], (D,), 0.3, 2.0, ((0, 2),), jnp.float32),
    }


EPSILON = 1e-05
RELAXATION = 32.0
MASKED = -1e+30

@jax.custom_vjp
def low(v):
    return lax.optimization_barrier(v.astype(jnp.bfloat16)).astype(jnp.float32)

@jax.custom_vjp
def low_back(v):
    return v

def low_keep(v):
    return (low(v), None)

def low_pass(kept, grad):
    return (grad,)

def back_keep(v):
    return (v, None)

def back_low(kept, grad):
    return (low(grad),)
low.defvjp(low_keep, low_pass)
low_back.defvjp(back_keep, back_low)

def highest(left, right):
    return jnp.dot(left, right, precision=lax.Precision.HIGHEST)

def normalize(values, gain, shift):
    average = lax.optimization_barrier(jnp.mean(values, axis=-1, keepdims=True))
    second = lax.optimization_barrier(jnp.mean(values * values, axis=-1, keepdims=True)) - average * average
    return (values - average) * lax.rsqrt(second + EPSILON) * gain + shift

def attention(queries, key_rows, value_rows, segment):
    group_rows = queries.shape[0]
    tile_rows = min(512, group_rows)
    tiles = group_rows // tile_rows
    positions = lax.iota(jnp.int32, group_rows)
    key_heads = key_rows.reshape(group_rows, HEADS, DH)
    value_heads = value_rows.reshape(group_rows, HEADS, DH)
    query_tiles = queries.reshape(tiles, tile_rows, HEADS, DH)

    @jax.checkpoint
    def one_tile(pieces):
        query_tile, query_pos, query_seg = pieces
        raw_dot = jnp.einsum('qhd,khd->hqk', query_tile, key_heads, precision=lax.Precision.HIGHEST)
        scores = raw_dot * (1.0 / (RELAXATION * math.sqrt(DH)))
        allowed = (positions[None, :] <= query_pos[:, None]) & (segment[None, :] == query_seg[:, None])
        scores = jnp.where(allowed[None], scores, MASKED)
        relaxed = low_back((scores - lax.optimization_barrier(jnp.max(scores, axis=2, keepdims=True))) * RELAXATION)
        expo = jnp.exp(relaxed)
        probability = expo / lax.optimization_barrier(jnp.sum(expo, axis=2, keepdims=True))
        return jnp.einsum('hqk,khd->qhd', low(probability), value_heads, precision=lax.Precision.HIGHEST)
    outputs = lax.map(one_tile, (query_tiles, positions.reshape(tiles, tile_rows), segment.reshape(tiles, tile_rows)))
    return outputs.reshape(group_rows, HEADS * DH)

def layer(stream, segment, params):
    w_query, w_key, w_value, bias_query, bias_value, w_out, bias_out, w_up, bias_up, w_down, bias_down, gain_attention_in, shift_attention_in, gain_attention_out, shift_attention_out, gain_ffn_in, shift_ffn_in, gain_ffn_out, shift_ffn_out = params
    norm_in = low(normalize(stream, gain_attention_in, shift_attention_in))
    queries = low(low_back(highest(norm_in, w_query) + bias_query))
    key_rows = low(low_back(highest(norm_in, w_key)))
    value_rows = low(low_back(highest(norm_in, w_value) + bias_value))
    attended = low(low_back(attention(queries, key_rows, value_rows, segment)))
    branch = low_back(highest(attended, w_out) + bias_out)
    middle = stream + normalize(branch, gain_attention_out, shift_attention_out)
    norm_mid = low(normalize(middle, gain_ffn_in, shift_ffn_in))
    hidden_pre = low_back(highest(norm_mid, w_up) + bias_up)
    hidden = low(jax.nn.gelu(hidden_pre, approximate=True))
    ffn_sum = low_back(highest(hidden, w_down) + bias_down)
    return middle + normalize(ffn_sum, gain_ffn_out, shift_ffn_out)

def group_tables(lengths, dealing):
    in_start = (jnp.cumsum(lengths) - lengths).astype(jnp.int32)
    slot_len = lengths[dealing].reshape(N_DP, SEQ_GRP)
    slot_ofs = (jnp.cumsum(slot_len, axis=1) - slot_len).astype(jnp.int32)
    positions = lax.iota(jnp.int32, TOK_GRP)
    segment = lax.optimization_barrier(jnp.sum((positions[None, :, None] >= slot_ofs[:, None, 1:]).astype(jnp.int32), axis=2)).astype(jnp.int32)
    ofs_at = jnp.take_along_axis(slot_ofs, segment, axis=1)
    seq_at = jnp.take_along_axis(dealing.reshape(N_DP, SEQ_GRP), segment, axis=1)
    source_rows = (in_start[seq_at] + positions[None, :] - ofs_at).astype(jnp.int32)
    return (source_rows, segment)

def reference(layer_input, cotangent, lengths, dealing, w_query, w_key, w_value, bias_query, bias_value, w_out, bias_out, w_up, bias_up, w_down, bias_down, gain_attention_in, shift_attention_in, gain_attention_out, shift_attention_out, gain_ffn_in, shift_ffn_in, gain_ffn_out, shift_ffn_out):
    source_rows, segment = group_tables(lengths, dealing)
    flat_rows = source_rows.reshape(-1)
    back_rows = jnp.zeros_like(flat_rows).at[flat_rows].set(lax.iota(jnp.int32, flat_rows.shape[0]))
    stream_in = layer_input.reshape(-1, D).astype(jnp.float32)
    params = tuple((weight_arg.astype(jnp.float32) for weight_arg in (w_query, w_key, w_value, bias_query, bias_value, w_out, bias_out, w_up, bias_up, w_down, bias_down, gain_attention_in, shift_attention_in, gain_attention_out, shift_attention_out, gain_ffn_in, shift_ffn_in, gain_ffn_out, shift_ffn_out)))
    checked_layer = jax.checkpoint(layer)

    def forward(stream_all, param_set):
        grouped = stream_all[source_rows]

        def one_group(carry_value, pieces):
            return (carry_value, checked_layer(pieces[0], pieces[1], param_set))
        _, results = lax.scan(one_group, jnp.zeros((), jnp.float32), (grouped, segment))
        return results.reshape(-1, D)[back_rows]
    out_rows, pullback = jax.vjp(forward, stream_in, params)
    grad_stream, grads = pullback(cotangent.reshape(-1, D).astype(jnp.float32))
    full_shape = layer_input.shape
    return (out_rows.reshape(full_shape).astype(jnp.bfloat16), grad_stream.reshape(full_shape).astype(jnp.bfloat16), grads[0], grads[1], grads[2], grads[3], grads[4], grads[5], grads[6], grads[7], grads[8], grads[9], grads[10], grads[11], grads[12], grads[13], grads[14], grads[15], grads[16], grads[17], grads[18])
```

```python
import functools
import math

import jax
import jax.numpy as jnp
from jax import lax
from jax.experimental import pallas as pl
from jax.experimental.pallas import tpu as pltpu
from jax.sharding import PartitionSpec as P

D = 1024
DH = 64
SEQ_GRP = 4
PAIR = 2 * DH
EPSILON = 1e-05
MASKED = -1e30
LOW = jnp.bfloat16
F32 = jnp.float32


def swap(values, axis, bit):
    size = lax.axis_size(axis)
    return lax.ppermute(values, axis, [(i, i ^ (1 << bit)) for i in range(size)])


def bits_of(axis):
    return range(lax.axis_size(axis).bit_length() - 1)


def bit_at(axis, bit):
    return (lax.axis_index(axis) >> bit) & 1


def col_pieces(own):
    pieces = [own]
    for bit in bits_of("col"):
        pieces = pieces + [swap(piece, "col", bit) for piece in pieces]
    return pieces


def by_column(pieces):
    for bit in bits_of("col"):
        flip = bit_at("col", bit) == 1
        pieces = [jnp.where(flip, pieces[k ^ (1 << bit)], pieces[k]) for k in range(len(pieces))]
    return pieces


def joined(pieces):
    return jnp.concatenate(by_column(pieces), axis=1)


def col_sum(partial):
    for bit in bits_of("col"):
        partial = partial + swap(partial.astype(LOW), "col", bit).astype(F32)
    return by_column(jnp.split(partial, lax.axis_size("col"), axis=1))


def total(parts):
    return functools.reduce(lambda a, b: a + b, parts)


def row_mean(pieces):
    return total([jnp.sum(p, axis=1, keepdims=True) for p in pieces]) * (1.0 / D)


def normalize(pieces):
    average = row_mean(pieces)
    inverse = lax.rsqrt(row_mean([p * p for p in pieces]) - average * average + EPSILON)
    return [(p - average) * inverse for p in pieces], inverse


def affine(scaled, gains, shifts):
    return [s * g + b for s, g, b in zip(scaled, gains, shifts)]


def normalize_back(grads, scaled, inverse, gains):
    pushed = [e * g for e, g in zip(grads, gains)]
    mean_push = row_mean(pushed)
    mean_dot = row_mean([f * n for f, n in zip(pushed, scaled)])
    result = [inverse * (f - mean_push - n * mean_dot) for f, n in zip(pushed, scaled)]
    return result, jnp.sum(grads[0] * scaled[0], axis=0), jnp.sum(grads[0], axis=0)


def dot(left, right):
    return jnp.dot(left, right, preferred_element_type=F32)


def dot_back(left, right):
    return lax.dot_general(left, right, (((1,), (1,)), ((), ())), preferred_element_type=F32)


def dot_tokens(left, right):
    return lax.dot_general(left, right, (((0,), (0,)), ((), ())), preferred_element_type=F32)


def route_tables(lengths, dealing, groups, half_rows, shard_count, row_count):
    seq_count = lengths.shape[0]
    per_group = seq_count // groups
    seq_ids = lax.iota(jnp.int32, seq_count)
    units = lengths // shard_count
    starts = jnp.sum(jnp.where(seq_ids[None, :] < seq_ids[:, None], units[None, :], 0), axis=1)
    chosen = dealing[:, None] == seq_ids[None, :]
    slot_len = jnp.sum(jnp.where(chosen, units[None, :], 0), axis=1)
    slot_in = jnp.sum(jnp.where(chosen, starts[None, :], 0), axis=1)
    earlier = (seq_ids[None, :] < seq_ids[:, None]) & (
        seq_ids[None, :] // per_group == seq_ids[:, None] // per_group
    )
    slot_ofs = jnp.sum(jnp.where(earlier, slot_len[None, :], 0), axis=1)
    grid_ofs = slot_ofs.reshape(groups, per_group)
    grid_anchor = (slot_in - slot_ofs).reshape(groups, per_group)
    places = half_rows // shard_count
    unit = (
        lax.broadcasted_iota(jnp.int32, (places, groups, row_count), 2) * places
        + lax.broadcasted_iota(jnp.int32, (places, groups, row_count), 0)
    )
    anchor = jnp.broadcast_to(grid_anchor[None, :, :1], unit.shape)
    for k in range(1, per_group):
        anchor = jnp.where(
            unit >= grid_ofs[None, :, k : k + 1], grid_anchor[None, :, k : k + 1], anchor
        )
    return (anchor + unit).reshape(half_rows), grid_ofs * shard_count


def head_lanes(shape, dim, head):
    lane = lax.broadcasted_iota(jnp.int32, shape, dim)
    return (lane >= head * DH) & (lane < (head + 1) * DH)


def masked_head(values, dim, head):
    return jnp.where(head_lanes(values.shape, dim, head), values, jnp.zeros_like(values))


def fill_bias(bias_ref, begin_ref, base):
    keys, queries = bias_ref.shape
    key_pos = lax.broadcasted_iota(jnp.int32, (keys, queries), 0) + base
    query_pos = lax.broadcasted_iota(jnp.int32, (keys, queries), 1)
    allowed = (key_pos <= query_pos) & (key_pos >= begin_ref[...])
    bias_ref[...] = jnp.where(allowed, 0.0, MASKED)


def query_blocks(rows, own):
    step = min(256, rows)
    return [(at, step, at + step if own else rows) for at in range(0, rows, step)]


def forward_own_kernel(begin_ref, q_ref, k_ref, v_ref, top_ref, sum_ref, acc_ref, bias_ref):
    @pl.when(pl.program_id(0) == 0)
    def _():
        fill_bias(bias_ref, begin_ref, 0)

    values = v_ref[...].T
    for at, size, keys in query_blocks(q_ref.shape[0], True):
        here = slice(at, at + size)
        for head in range(2):
            query = masked_head(q_ref[here, :], 1, head)
            scores = dot_back(k_ref[:keys, :], query) + bias_ref[:keys, here]
            top = jnp.max(scores, axis=0, keepdims=True)
            weights = jnp.exp(scores - top)
            top_ref[0, head : head + 1, here] = top
            sum_ref[0, head : head + 1, here] = jnp.sum(weights, axis=0, keepdims=True)
            part = dot(values[head * DH : (head + 1) * DH, :keys], weights.astype(LOW))
            acc_ref[head * DH : (head + 1) * DH, here] = part


def forward_low_kernel(
    begin_ref, q_ref, k_ref, v_ref, top_ref, sum_ref, acc_ref, out_ref, out_t_ref, log_ref, bias_ref
):
    rows = k_ref.shape[0]

    @pl.when(pl.program_id(0) == 0)
    def _():
        fill_bias(bias_ref, begin_ref, -rows)

    values = v_ref[...].T
    for at, size, keys in query_blocks(q_ref.shape[0], False):
        here = slice(at, at + size)
        for head in range(2):
            query = masked_head(q_ref[here, :], 1, head)
            scores = dot_back(k_ref[...], query) + bias_ref[:, here]
            old_top = top_ref[0, head : head + 1, here]
            top = jnp.maximum(old_top, jnp.max(scores, axis=0, keepdims=True))
            weights = jnp.exp(scores - top)
            scale = jnp.exp(old_top - top)
            norm = sum_ref[0, head : head + 1, here] * scale
            norm = norm + jnp.sum(weights, axis=0, keepdims=True)
            part = dot(values[head * DH : (head + 1) * DH, :], weights.astype(LOW))
            lanes = slice(head * DH, (head + 1) * DH)
            out_t_ref[lanes, here] = (acc_ref[lanes, here] * scale + part) / norm
            log_ref[0, head : head + 1, here] = top + jnp.log(norm)
    out_ref[...] = out_t_ref[...].T.astype(LOW)


def backward_kernel(
    own, begin_ref, q_ref, k_ref, v_ref, g_ref, out_t_ref, log_ref, dq_ref, dk_ref, dv_ref, bias_ref
):
    rows = k_ref.shape[0]

    @pl.when(pl.program_id(0) == 0)
    def _():
        fill_bias(bias_ref, begin_ref, 0 if own else -rows)

    dots = g_ref[...].T.astype(F32) * out_t_ref[...]
    keys_t = k_ref[...].T
    dk = [None] * (q_ref.shape[0] // query_blocks(q_ref.shape[0], own)[0][1])
    dv = list(dk)
    for block, (at, size, keys) in enumerate(query_blocks(q_ref.shape[0], own)):
        here = slice(at, at + size)
        for head in range(2):
            lanes = slice(head * DH, (head + 1) * DH)
            query = masked_head(q_ref[here, :], 1, head)
            grad = masked_head(g_ref[here, :], 1, head)
            scores = dot_back(k_ref[:keys, :], query) + bias_ref[:keys, here]
            prob = jnp.exp(scores - log_ref[0, head : head + 1, here])
            grad_prob = dot_back(v_ref[:keys, :], grad)
            row_dot = jnp.sum(dots[lanes, here], axis=0, keepdims=True)
            grad_score = (prob * (grad_prob - row_dot)).astype(LOW)
            dq_ref[lanes, here] = dot(keys_t[lanes, :keys], grad_score)
            new_dk = dot(grad_score, query)
            new_dv = dot(prob.astype(LOW), grad)
            dk[block] = new_dk if dk[block] is None else dk[block] + new_dk
            dv[block] = new_dv if dv[block] is None else dv[block] + new_dv
    for ref, parts in ((dk_ref, dk), (dv_ref, dv)):
        ref[...] = jnp.zeros(ref.shape, F32)
        for part in parts:
            ref[: part.shape[0], :] += part


def pair_spec(rows):
    return pl.BlockSpec((rows, PAIR), lambda i: (0, i))


def pair_t_spec(rows):
    return pl.BlockSpec((PAIR, rows), lambda i: (i, 0))


def stat_spec(rows):
    return pl.BlockSpec((1, 2, rows), lambda i: (i, 0, 0))


def attention_cost(rows, width, dots, other):
    return pl.CostEstimate(
        flops=2 * rows * rows * width * dots,
        bytes_accessed=rows * width * other,
        transcendentals=rows * rows * width // DH,
    )


def attend_call(kernel, rows, width, ins, outs, cost):
    pairs = width // PAIR
    shapes = {
        "rows": (pair_spec(rows), (rows, width)),
        "cols": (pair_t_spec(rows), (width, rows)),
        "stat": (stat_spec(rows), (pairs, 2, rows)),
        "line": (pl.BlockSpec((1, rows), lambda i: (0, 0)), (1, rows)),
    }
    return pl.pallas_call(
        kernel,
        grid=(pairs,),
        in_specs=[shapes[kind][0] for kind in ins],
        out_specs=[shapes[kind][0] for kind, _ in outs],
        out_shape=[jax.ShapeDtypeStruct(shapes[kind][1], dtype) for kind, dtype in outs],
        scratch_shapes=[pltpu.VMEM((rows, rows), F32)],
        cost_estimate=cost,
    )


def pick(values, index, dim):
    size = values.shape[dim] // 2
    return lax.dynamic_slice_in_dim(values, index * size, size, dim)


def phase_of(phase):
    if phase == "y":
        return "row", 0
    return "dp", phase


def reduce_grad(by_rows, left, right, order):
    tokens = left.shape[0]

    def operands(phase, index):
        if phase == "y":
            if by_rows:
                return pick(left, index, 1), right
            return left, pick(right, index, 1)
        if not by_rows:
            return pick(left, index, 1), right
        halves = left.reshape(tokens, 2, left.shape[1] // 2)
        return pick(halves, index, 2).reshape(tokens, left.shape[1] // 2), right

    def half(values, phase, index, row_done):
        if phase == "y":
            return pick(values, index, 0 if by_rows else 1)
        if row_done or not by_rows:
            return pick(values, index, 0)
        rows, columns = values.shape
        grid = values.reshape(2, rows // 2, columns)
        return pick(grid, index, 1).reshape(rows // 2, columns)

    axis, bit = phase_of(order[0])
    mine = bit_at(axis, bit)
    sent = dot_tokens(*operands(order[0], 1 - mine)).astype(LOW)
    kept = dot_tokens(*operands(order[0], mine))
    held = kept + swap(sent, axis, bit).astype(F32)
    row_done = order[0] == "y"
    for phase in order[1:-1]:
        axis, bit = phase_of(phase)
        mine = bit_at(axis, bit)
        sent = half(held, phase, 1 - mine, row_done).astype(LOW)
        kept = half(held, phase, mine, row_done)
        held = kept + swap(sent, axis, bit).astype(F32)
        row_done = row_done or phase == "y"
    axis, bit = phase_of(order[-1])
    low = held.astype(LOW)
    low = (low.astype(F32) + swap(low, axis, bit).astype(F32)).astype(LOW)
    for phase in reversed(order[:-1]):
        if phase == "y":
            continue
        axis, bit = phase_of(phase)
        flip = bit_at(axis, bit) == 1
        other = swap(low, axis, bit)
        low = jnp.concatenate([jnp.where(flip, other, low), jnp.where(flip, low, other)], axis=0)
    return low.astype(F32)


def reduce_small(vectors):
    sizes = [v.shape[0] for v in vectors]
    packed = jnp.concatenate(vectors).reshape(-1, 128)
    for axis in ("row", "dp"):
        for bit in bits_of(axis):
            packed = packed + swap(packed, axis, bit)
    flat = packed.reshape(-1)
    ends = [sum(sizes[: i + 1]) for i in range(len(sizes))]
    return [flat[e - s : e] for s, e in zip(sizes, ends)]


def body(
    layer_input,
    cotangent,
    lengths,
    dealing,
    w_query,
    w_key,
    w_value,
    bias_query,
    bias_value,
    w_out,
    bias_out,
    w_up,
    bias_up,
    w_down,
    bias_down,
    gain_attention_in,
    shift_attention_in,
    gain_attention_out,
    shift_attention_out,
    gain_ffn_in,
    shift_ffn_in,
    gain_ffn_out,
    shift_ffn_out,
):
    row_count = lax.axis_size("row")
    groups = lax.axis_size("dp")
    shard_count = groups * row_count
    row_index = lax.axis_index("row")
    group_index = lax.axis_index("dp")
    rows = layer_input.shape[0]
    local_width = layer_input.shape[2]
    places = rows // shard_count
    group_rows = rows * row_count

    routes, grid_ofs = route_tables(lengths, dealing, groups, rows, shard_count, row_count)
    place = (routes[:, None] == lax.iota(jnp.int32, rows)[None, :]).astype(LOW)

    def deal(values):
        sent = dot(place, values.reshape(rows, local_width)).astype(LOW)
        sent = sent.reshape(places, shard_count, local_width)
        got = lax.all_to_all(sent, ("dp", "row"), split_axis=1, concat_axis=1, tiled=True)
        return got.reshape(rows, local_width)

    def undo_deal(values):
        sent = values.astype(LOW).reshape(places, shard_count, local_width)
        got = lax.all_to_all(sent, ("dp", "row"), split_axis=1, concat_axis=1, tiled=True)
        got = got.reshape(rows, local_width)
        return dot_tokens(place, got).astype(LOW).reshape(rows, 1, local_width)

    own_ofs = jnp.sum(
        jnp.where((lax.iota(jnp.int32, groups) == group_index)[:, None], grid_ofs, 0), axis=0
    )
    positions = row_index * rows + lax.iota(jnp.int32, rows)
    begin = jnp.max(
        jnp.where(positions[:, None] >= own_ofs[None, :], own_ofs[None, :], 0), axis=1
    )
    begin = (begin - row_index * rows).reshape(1, rows)

    packed = jnp.stack(
        [
            gain_attention_in,
            shift_attention_in,
            gain_attention_out,
            shift_attention_out,
            gain_ffn_in,
            shift_ffn_in,
            gain_ffn_out,
            shift_ffn_out,
            bias_out,
            bias_down,
        ]
    )
    packed_all = col_pieces(packed)
    vectors = [[piece[i : i + 1, :] for piece in packed_all] for i in range(10)]
    gain1, shift1, gain2, shift2, gain3, shift3, gain4, shift4, bias_o, bias_d = vectors

    x_own = deal(layer_input)
    x_low_own = lax.ppermute(x_own, "row", [(0, 1)])
    g_own = deal(cotangent)
    x = [piece.astype(F32) for piece in col_pieces(x_own)]
    n1, r1 = normalize(x)
    h1 = joined([piece.astype(LOW) for piece in affine(n1, gain1, shift1)])
    queries = ((dot(h1, w_query) + bias_query) * (1.0 / math.sqrt(DH))).astype(LOW)
    keys = dot(h1, w_key).astype(LOW)
    values = (dot(h1, w_value) + bias_value).astype(LOW)

    width = queries.shape[1]
    top, norm, acc = attend_call(
        forward_own_kernel,
        rows,
        width,
        ["line", "rows", "rows", "rows"],
        [("stat", F32), ("stat", F32), ("cols", F32)],
        attention_cost(rows, width, 3, 10),
    )(begin, queries, keys, values)

    x_low = [piece.astype(F32) for piece in col_pieces(x_low_own)]
    n_low, _ = normalize(x_low)
    h_low = joined([piece.astype(LOW) for piece in affine(n_low, gain1, shift1)])
    keys_low = dot(h_low, w_key).astype(LOW)
    values_low = (dot(h_low, w_value) + bias_value).astype(LOW)
    attended, attended_t, log_total = attend_call(
        forward_low_kernel,
        rows,
        width,
        ["line", "rows", "rows", "rows", "stat", "stat", "cols"],
        [("rows", LOW), ("cols", F32), ("stat", F32)],
        attention_cost(rows, width, 4, 16),
    )(begin, queries, keys_low, values_low, top, norm, acc)

    branch = [p + b for p, b in zip(col_sum(dot(attended, w_out)), bias_o)]
    n2, r2 = normalize(branch)
    middle = [a + b for a, b in zip(x, affine(n2, gain2, shift2))]
    n3, r3 = normalize(middle)
    h2 = joined([piece.astype(LOW) for piece in affine(n3, gain3, shift3)])
    pre = dot(h2, w_up) + bias_up
    cube = math.sqrt(2.0 / math.pi)
    bend = jnp.tanh(cube * (pre + 0.044715 * pre * pre * pre))
    hidden = (0.5 * pre * (1.0 + bend)).astype(LOW)
    slope = 0.5 * (1.0 + bend) + 0.5 * pre * (1.0 - bend * bend) * cube * (
        1.0 + 3.0 * 0.044715 * pre * pre
    )
    slope = slope.astype(LOW)
    ffn = [p + b for p, b in zip(col_sum(dot(hidden, w_down)), bias_d)]
    n4, r4 = normalize(ffn)
    result = middle[0] + affine(n4[:1], gain4[:1], shift4[:1])[0]
    output = undo_deal(result)

    g = [piece.astype(F32) for piece in col_pieces(g_own)]
    d_ffn, g_gain4, g_shift4 = normalize_back(g, n4, r4, gain4)
    d_ffn_low = [piece.astype(LOW) for piece in d_ffn]
    d_ffn_all = joined(d_ffn_low)
    d_pre = (dot_back(d_ffn_all, w_down) * slope.astype(F32)).astype(LOW)
    bits = list(bits_of("dp"))
    spin = bits[1:2] + bits[:1] + bits[2:]
    grad_down = reduce_grad(False, hidden, d_ffn_all, ["y"] + bits)
    grad_up = reduce_grad(True, h2, d_pre, bits[:1] + ["y"] + bits[1:])
    d_h2 = col_sum(dot_back(d_pre, w_up))
    back3, g_gain3, g_shift3 = normalize_back(d_h2, n3, r3, gain3)
    d_middle = [a + b for a, b in zip(g, back3)]
    d_branch, g_gain2, g_shift2 = normalize_back(d_middle, n2, r2, gain2)
    d_branch_low = [piece.astype(LOW) for piece in d_branch]
    d_branch_all = joined(d_branch_low)
    d_attended = dot_back(d_branch_all, w_out).astype(LOW)

    back_ins = ["line", "rows", "rows", "rows", "rows", "cols", "stat"]
    back_outs = [("cols", F32), ("rows", F32), ("rows", F32)]
    dq_low, dk_low, dv_low = attend_call(
        functools.partial(backward_kernel, False),
        rows,
        width,
        back_ins,
        back_outs,
        attention_cost(rows, width, 10, 24),
    )(begin, queries, keys_low, values_low, d_attended, attended_t, log_total)
    kv_low = jnp.concatenate([dk_low.astype(LOW), dv_low.astype(LOW)], axis=1)
    kv_back = lax.ppermute(kv_low, "row", [(1, 0)]).astype(F32)
    dq_own, dk_own, dv_own = attend_call(
        functools.partial(backward_kernel, True),
        rows,
        width,
        back_ins,
        back_outs,
        attention_cost(rows, width, 8, 24),
    )(begin, queries, keys, values, d_attended, attended_t, log_total)
    d_query = ((dq_low + dq_own) * (1.0 / math.sqrt(DH))).T.astype(LOW)
    d_key = (dk_own + kv_back[:, :width]).astype(LOW)
    d_value = (dv_own + kv_back[:, width:]).astype(LOW)

    grad_out = reduce_grad(False, attended, d_branch_all, spin[:1] + ["y"] + spin[1:])
    grad_query = reduce_grad(True, h1, d_query, ["y"] + bits)
    grad_key = reduce_grad(True, h1, d_key, bits[:1] + ["y"] + bits[1:])
    grad_value = reduce_grad(True, h1, d_value, spin[:1] + ["y"] + spin[1:])

    d_h1 = col_sum(
        dot_back(d_query, w_query) + dot_back(d_key, w_key) + dot_back(d_value, w_value)
    )
    back1, g_gain1, g_shift1 = normalize_back(d_h1, n1, r1, gain1)
    input_grad = undo_deal(d_middle[0] + back1[0])

    def summed(values):
        return jnp.sum(values.astype(F32), axis=0)

    smalls = reduce_small(
        [
            summed(d_query),
            summed(d_value),
            summed(d_branch_low[0]),
            summed(d_pre),
            summed(d_ffn_low[0]),
            g_gain1,
            g_shift1,
            g_gain2,
            g_shift2,
            g_gain3,
            g_shift3,
            g_gain4,
            g_shift4,
        ]
    )
    return (
        output,
        input_grad,
        grad_query,
        grad_key,
        grad_value,
        smalls[0],
        smalls[1],
        grad_out,
        smalls[2],
        grad_up,
        smalls[3],
        grad_down,
        smalls[4],
        *smalls[5:],
    )


def solution(mesh):
    shards = P(None, ("dp", "row"), "col")
    by_col = P("col")
    vectors = (by_col,) * 8
    return jax.shard_map(
        body,
        mesh=mesh,
        in_specs=(
            shards,
            shards,
            P(),
            P(),
            P(None, "col"),
            P(None, "col"),
            P(None, "col"),
            by_col,
            by_col,
            P("col", None),
            by_col,
            P(None, "col"),
            by_col,
            P("col", None),
            by_col,
            *vectors,
        ),
        out_specs=(
            shards,
            shards,
            P("row", "col"),
            P("row", "col"),
            P("row", "col"),
            by_col,
            by_col,
            P("col", "row"),
            by_col,
            P("row", "col"),
            by_col,
            P("col", "row"),
            by_col,
            *vectors,
        ),
        check_vma=False,
    )
```

```python
import functools
import math

import jax
import jax.numpy as jnp
from jax import lax
from jax.experimental import pallas as pl
from jax.experimental.pallas import tpu as pltpu
from jax.sharding import PartitionSpec as P

D = 1024
DH = 64
PAIR = 2 * DH
EPSILON = 1e-05
MASKED = -1e30
LOW = jnp.bfloat16
F32 = jnp.float32


def swap(values, axis, bit):
    size = lax.axis_size(axis)
    return lax.ppermute(values, axis, [(i, i ^ (1 << bit)) for i in range(size)])


def bits_of(axis):
    return range(lax.axis_size(axis).bit_length() - 1)


def bit_at(phase):
    if phase == ROW:
        return lax.axis_index("row")
    return (lax.axis_index("dp") >> phase) & 1


ROW = "row"


def swap_phase(values, phases):
    sizes = [lax.axis_size(axis) for axis in ("dp", "row", "col")]
    pairs = []
    for dp in range(sizes[0]):
        for row in range(sizes[1]):
            for col in range(sizes[2]):
                phase = phases[col % 2]
                there = (dp, row ^ 1) if phase == ROW else (dp ^ (1 << phase), row)
                pairs.append(
                    (
                        (dp * sizes[1] + row) * sizes[2] + col,
                        (there[0] * sizes[1] + there[1]) * sizes[2] + col,
                    )
                )
    return lax.ppermute(values, ("dp", "row", "col"), pairs)


def per_core(even, odd):
    return jnp.where(lax.axis_index("col") % 2 == 0, even, odd)


def col_pieces(own):
    pieces = [own]
    for bit in bits_of("col"):
        pieces = pieces + [swap(piece, "col", bit) for piece in pieces]
    return pieces


def col_parts(partial):
    bits = list(bits_of("col"))
    for bit in bits[:-1]:
        partial = (partial.astype(F32) + swap(partial, "col", bit).astype(F32)).astype(LOW)
    return [partial, swap(partial, "col", bits[-1])]


def after(values, *earlier):
    return lax.optimization_barrier((values, *earlier))[0]


def part(values, index, dim):
    size = values.shape[dim] // 2
    return lax.slice_in_dim(values, index * size, (index + 1) * size, axis=dim)


def dot(left, right):
    return jnp.dot(left, right, preferred_element_type=F32)


def dot_back(left, right):
    return lax.dot_general(left, right, (((1,), (1,)), ((), ())), preferred_element_type=F32)


def dot_tokens(left, right):
    return lax.dot_general(left, right, (((0,), (0,)), ((), ())), preferred_element_type=F32)


BLOCKS = 8
GAIN1, SHIFT1, GAIN2, SHIFT2, GAIN3, SHIFT3, GAIN4, SHIFT4, BIAS_OUT, BIAS_DOWN = range(10)


def total(parts):
    return functools.reduce(lambda a, b: a + b, parts)


def row_mean(pieces):
    return total([jnp.sum(p, axis=1, keepdims=True) for p in pieces]) * (1.0 / D)


def normalize(pieces):
    average = row_mean(pieces)
    inverse = lax.rsqrt(row_mean([p * p for p in pieces]) - average * average + EPSILON)
    return [(p - average) * inverse for p in pieces], inverse


def normalize_back(grads, scaled, inverse, gains):
    pushed = [e * g for e, g in zip(grads, gains)]
    mean_push = row_mean(pushed)
    mean_dot = row_mean([f * n for f, n in zip(pushed, scaled)])
    return [inverse * (f - mean_push - n * mean_dot) for f, n in zip(pushed, scaled)]


def span(column, k, width):
    return pl.ds(pl.multiple_of((column ^ k) * width, 128), width)


def load_pieces(refs):
    return [ref[...].astype(F32) for ref in refs]


def load_ordered(refs, column, count):
    width = refs[0].shape[1] // count
    return [
        total([ref[:, span(column, k, width)].astype(F32) for ref in refs]) for k in range(count)
    ]


def store_ordered(ref, column, pieces):
    width = ref.shape[1] // len(pieces)
    for k, piece in enumerate(pieces):
        ref[:, span(column, k, width)] = piece


def store_blocks(ref, table, column, pieces):
    size = ref.shape[1] // BLOCKS
    width = ref.shape[1] // len(pieces)
    for k, piece in enumerate(pieces):
        first = (column ^ k) * (width // size)
        for j in range(width // size):
            place = pl.multiple_of(table[first + j] * size, 128)
            ref[:, pl.ds(place, size)] = piece[:, j * size : (j + 1) * size]


def column_sums(ref, rows):
    @pl.when(pl.program_id(0) == 0)
    def _():
        ref[...] = jnp.zeros(ref.shape, F32)

    for at, values in enumerate(rows):
        ref[at : at + 1, :] += jnp.sum(values, axis=0, keepdims=True)


def vector_of(vector_refs, index):
    return [ref[index : index + 1, :] for ref in vector_refs]


def plus(pieces, vectors):
    return [p + v for p, v in zip(pieces, vectors)]


def affine(scaled, gains, shifts):
    return [s * g + b for s, g, b in zip(scaled, gains, shifts)]


def norm_in_kernel(scalars, vec, x, h, h_blocks=None):
    scaled, _ = normalize(load_pieces(x))
    out = affine(scaled, vector_of(vec, GAIN1), vector_of(vec, SHIFT1))
    out = [p.astype(LOW) for p in out]
    store_ordered(h[0], scalars[0], out)
    if h_blocks is not None:
        store_blocks(h_blocks[0], scalars.table(), scalars[0], out)


def middle_of(column, vec, branch, x):
    held = plus(load_ordered(branch, column, len(x)), vector_of(vec, BIAS_OUT))
    scaled, inverse = normalize(held)
    out = affine(scaled, vector_of(vec, GAIN2), vector_of(vec, SHIFT2))
    return scaled, inverse, [a + b for a, b in zip(load_pieces(x), out)]


def norm_mid_kernel(scalars, vec, branch, x, h, h_blocks, y):
    column = scalars[0]
    _, _, middle = middle_of(column, vec, branch, x)
    y[0][...] = middle[0]
    scaled, _ = normalize(middle)
    out = affine(scaled, vector_of(vec, GAIN3), vector_of(vec, SHIFT3))
    out = [p.astype(LOW) for p in out]
    store_ordered(h[0], column, out)
    store_blocks(h_blocks[0], scalars.table(), column, out)


def norm_out_kernel(scalars, vec, ffn, g, y, d_ffn, d_blocks, result, sums):
    column = scalars[0]
    held = plus(load_ordered(ffn, column, len(g)), vector_of(vec, BIAS_DOWN))
    scaled, inverse = normalize(held)
    gains = vector_of(vec, GAIN4)
    out = y[0][...] + scaled[0] * gains[0] + vector_of(vec, SHIFT4)[0]
    result[0][...] = out.astype(LOW)
    grads = load_pieces(g)
    back = [p.astype(LOW) for p in normalize_back(grads, scaled, inverse, gains)]
    store_ordered(d_ffn[0], column, back)
    store_blocks(d_blocks[0], scalars.table(), column, back)
    column_sums(sums[0], [grads[0] * scaled[0], grads[0], back[0].astype(F32)])


def norm_back_kernel(scalars, vec, d_h2, g, x, branch, d_branch, d_blocks, d_middle, sums):
    column = scalars[0]
    scaled2, inverse2, middle = middle_of(column, vec, branch, x)
    scaled3, inverse3 = normalize(middle)
    grads3 = load_ordered(d_h2, column, len(x))
    back3 = normalize_back(grads3, scaled3, inverse3, vector_of(vec, GAIN3))
    grads2 = [a + b for a, b in zip(load_pieces(g), back3)]
    d_middle[0][...] = grads2[0]
    back2 = normalize_back(grads2, scaled2, inverse2, vector_of(vec, GAIN2))
    back2 = [p.astype(LOW) for p in back2]
    store_ordered(d_branch[0], column, back2)
    store_blocks(d_blocks[0], scalars.table(), column, back2)
    column_sums(
        sums[0],
        [
            grads3[0] * scaled3[0],
            grads3[0],
            grads2[0] * scaled2[0],
            grads2[0],
            back2[0].astype(F32),
        ],
    )


def norm_last_kernel(scalars, vec, d_h1, x, d_middle, out, sums):
    column = scalars[0]
    scaled, inverse = normalize(load_pieces(x))
    grads = load_ordered(d_h1, column, len(x))
    back = normalize_back(grads, scaled, inverse, vector_of(vec, GAIN1))
    out[0][...] = (d_middle[0][...] + back[0]).astype(LOW)
    column_sums(sums[0], [grads[0] * scaled[0], grads[0]])


class Scalars:
    def __init__(self, ref):
        self.ref = ref

    def __getitem__(self, index):
        return self.ref[index]

    def table(self):
        return Table(self.ref)


class Table:
    def __init__(self, ref):
        self.ref = ref

    def __getitem__(self, index):
        return self.ref[index + 1]


def row_call(kernel, scalars, vectors, ins, outs, passes):
    rows = ins[0][0].shape[0]
    step = min(128, rows)
    counts = [len(vectors)] + [len(group) for group in ins] + [1] * len(outs)

    def whole(scalar_ref, *refs):
        groups = []
        for count in counts:
            groups.append(refs[:count])
            refs = refs[count:]
        kernel(Scalars(scalar_ref), *groups)

    def block(width):
        return pl.BlockSpec((step, width), lambda i, c: (i, 0))

    flat = [a for group in ins for a in group]
    shapes = []
    specs = []
    for out in outs:
        if isinstance(out, tuple):
            shapes.append(jax.ShapeDtypeStruct((rows, out[0]), out[1]))
            specs.append(block(out[0]))
        else:
            shapes.append(jax.ShapeDtypeStruct((8, out), F32))
            specs.append(pl.BlockSpec((8, out), lambda i, c: (0, 0)))
    return pl.pallas_call(
        whole,
        grid_spec=pltpu.PrefetchScalarGridSpec(
            num_scalar_prefetch=1,
            grid=(rows // step,),
            in_specs=[pl.BlockSpec(v.shape, lambda i, c: (0, 0)) for v in vectors]
            + [block(a.shape[1]) for a in flat],
            out_specs=specs,
        ),
        out_shape=shapes,
        cost_estimate=pl.CostEstimate(
            flops=passes * rows * D,
            bytes_accessed=sum(a.size * a.dtype.itemsize for a in flat),
            transcendentals=rows,
        ),
    )(scalars, *vectors, *flat)


def route_tables(lengths, dealing, groups, half_rows, shard_count, row_count):
    seq_count = lengths.shape[0]
    per_group = seq_count // groups
    seq_ids = lax.iota(jnp.int32, seq_count)
    units = lengths // shard_count
    starts = jnp.sum(jnp.where(seq_ids[None, :] < seq_ids[:, None], units[None, :], 0), axis=1)
    chosen = dealing[:, None] == seq_ids[None, :]
    slot_len = jnp.sum(jnp.where(chosen, units[None, :], 0), axis=1)
    slot_in = jnp.sum(jnp.where(chosen, starts[None, :], 0), axis=1)
    earlier = (seq_ids[None, :] < seq_ids[:, None]) & (
        seq_ids[None, :] // per_group == seq_ids[:, None] // per_group
    )
    slot_ofs = jnp.sum(jnp.where(earlier, slot_len[None, :], 0), axis=1)
    grid_ofs = slot_ofs.reshape(groups, per_group)
    grid_anchor = (slot_in - slot_ofs).reshape(groups, per_group)
    places = half_rows // shard_count
    unit = (
        lax.broadcasted_iota(jnp.int32, (places, groups, row_count), 2) * places
        + lax.broadcasted_iota(jnp.int32, (places, groups, row_count), 0)
    )
    anchor = jnp.broadcast_to(grid_anchor[None, :, :1], unit.shape)
    for k in range(1, per_group):
        anchor = jnp.where(
            unit >= grid_ofs[None, :, k : k + 1], grid_anchor[None, :, k : k + 1], anchor
        )
    return (anchor + unit).reshape(half_rows), grid_ofs * shard_count


def head_lanes(shape, dim, head):
    lane = lax.broadcasted_iota(jnp.int32, shape, dim)
    return (lane >= head * DH) & (lane < (head + 1) * DH)


def masked_head(values, dim, head):
    return jnp.where(head_lanes(values.shape, dim, head), values, jnp.zeros_like(values))


def fill_bias(bias_ref, begin_ref, base):
    keys, queries = bias_ref.shape
    key_pos = lax.broadcasted_iota(jnp.int32, (keys, queries), 0) + base
    query_pos = lax.broadcasted_iota(jnp.int32, (keys, queries), 1)
    allowed = (key_pos <= query_pos) & (key_pos >= begin_ref[...])
    bias_ref[...] = jnp.where(allowed, 0.0, MASKED)


def query_blocks(rows, own):
    step = min(256, rows)
    return [(at, step, at + step if own else rows) for at in range(0, rows, step)]


def forward_own_kernel(begin_ref, q_ref, k_ref, v_ref, top_ref, sum_ref, acc_ref, bias_ref):
    @pl.when(pl.program_id(0) == 0)
    def _():
        fill_bias(bias_ref, begin_ref, 0)

    values = v_ref[...].T
    for at, size, keys in query_blocks(q_ref.shape[0], True):
        here = slice(at, at + size)
        for head in range(2):
            query = masked_head(q_ref[here, :], 1, head)
            scores = dot_back(k_ref[:keys, :], query) + bias_ref[:keys, here]
            top = jnp.max(scores, axis=0, keepdims=True)
            weights = jnp.exp(scores - top)
            top_ref[0, head : head + 1, here] = top
            sum_ref[0, head : head + 1, here] = jnp.sum(weights, axis=0, keepdims=True)
            part = dot(values[head * DH : (head + 1) * DH, :keys], weights.astype(LOW))
            acc_ref[head * DH : (head + 1) * DH, here] = part


def forward_low_kernel(
    begin_ref, q_ref, k_ref, v_ref, top_ref, sum_ref, acc_ref, out_ref, out_t_ref, log_ref, bias_ref
):
    rows = k_ref.shape[0]

    @pl.when(pl.program_id(0) == 0)
    def _():
        fill_bias(bias_ref, begin_ref, -rows)

    values = v_ref[...].T
    for at, size, keys in query_blocks(q_ref.shape[0], False):
        here = slice(at, at + size)
        for head in range(2):
            query = masked_head(q_ref[here, :], 1, head)
            scores = dot_back(k_ref[...], query) + bias_ref[:, here]
            old_top = top_ref[0, head : head + 1, here]
            top = jnp.maximum(old_top, jnp.max(scores, axis=0, keepdims=True))
            weights = jnp.exp(scores - top)
            scale = jnp.exp(old_top - top)
            norm = sum_ref[0, head : head + 1, here] * scale
            norm = norm + jnp.sum(weights, axis=0, keepdims=True)
            part = dot(values[head * DH : (head + 1) * DH, :], weights.astype(LOW))
            lanes = slice(head * DH, (head + 1) * DH)
            out_t_ref[lanes, here] = (acc_ref[lanes, here] * scale + part) / norm
            log_ref[0, head : head + 1, here] = top + jnp.log(norm)
    out_ref[...] = out_t_ref[...].T.astype(LOW)


def backward_kernel(
    own, begin_ref, q_ref, k_ref, v_ref, g_ref, out_t_ref, log_ref, *rest
):
    if own:
        dq_low_ref, dq_ref, dk_ref, dv_ref, bias_ref = rest
    else:
        dq_ref, dk_ref, dv_ref, bias_ref = rest
    rows = k_ref.shape[0]

    @pl.when(pl.program_id(0) == 0)
    def _():
        fill_bias(bias_ref, begin_ref, 0 if own else -rows)

    dots = g_ref[...].T.astype(F32) * out_t_ref[...]
    keys_t = k_ref[...].T
    dk = []
    dv = []
    for at, size, keys in query_blocks(q_ref.shape[0], own):
        here = slice(at, at + size)
        dq = []
        dk.append(None)
        dv.append(None)
        for head in range(2):
            lanes = slice(head * DH, (head + 1) * DH)
            query = masked_head(q_ref[here, :], 1, head)
            grad = masked_head(g_ref[here, :], 1, head)
            scores = dot_back(k_ref[:keys, :], query) + bias_ref[:keys, here]
            prob = jnp.exp(scores - log_ref[0, head : head + 1, here])
            grad_prob = dot_back(v_ref[:keys, :], grad)
            row_dot = jnp.sum(dots[lanes, here], axis=0, keepdims=True)
            grad_score = (prob * (grad_prob - row_dot)).astype(LOW)
            dq.append(dot(keys_t[lanes, :keys], grad_score))
            new_dk = dot(grad_score, query)
            new_dv = dot(prob.astype(LOW), grad)
            dk[-1] = new_dk if head == 0 else dk[-1] + new_dk
            dv[-1] = new_dv if head == 0 else dv[-1] + new_dv
        if own:
            dq = jnp.concatenate(dq, axis=0) + dq_low_ref[:, here]
            dq_ref[here, :] = (dq * (1.0 / math.sqrt(DH))).T.astype(LOW)
        else:
            dq_ref[:DH, here] = dq[0]
            dq_ref[DH:, here] = dq[1]
    for ref, parts in ((dk_ref, dk), (dv_ref, dv)):
        ends = sorted({p.shape[0] for p in parts})
        for begin, end in zip([0] + ends[:-1], ends):
            pieces = [p[begin:end] for p in parts if p.shape[0] >= end]
            ref[begin:end, :] = total(pieces).astype(LOW)


def pair_spec(rows):
    return pl.BlockSpec((rows, PAIR), lambda i: (0, i))


def pair_t_spec(rows):
    return pl.BlockSpec((PAIR, rows), lambda i: (i, 0))


def stat_spec(rows):
    return pl.BlockSpec((1, 2, rows), lambda i: (i, 0, 0))


def attention_cost(rows, width, dots, other):
    return pl.CostEstimate(
        flops=2 * rows * rows * width * dots,
        bytes_accessed=rows * width * other,
        transcendentals=rows * rows * width // DH,
    )


def attend_call(kernel, rows, width, ins, outs, cost):
    pairs = width // PAIR
    shapes = {
        "rows": (pair_spec(rows), (rows, width)),
        "cols": (pair_t_spec(rows), (width, rows)),
        "stat": (stat_spec(rows), (pairs, 2, rows)),
        "line": (pl.BlockSpec((1, rows), lambda i: (0, 0)), (1, rows)),
    }
    return pl.pallas_call(
        kernel,
        grid=(pairs,),
        in_specs=[shapes[kind][0] for kind in ins],
        out_specs=[shapes[kind][0] for kind, _ in outs],
        out_shape=[jax.ShapeDtypeStruct(shapes[kind][1], dtype) for kind, dtype in outs],
        scratch_shapes=[pltpu.VMEM((rows, rows), F32)],
        cost_estimate=cost,
    )


def pick(values, index):
    size = values.shape[0] // 2
    return lax.dynamic_slice_in_dim(values, index * size, size, 0, allow_negative_indices=False)


def place_table(orders):
    def places(order):
        head = order[:3]
        spare = [phase for phase in head if phase != ROW]
        block = lax.iota(jnp.int32, BLOCKS)
        natural = {ROW: (block >> 2) & 1, spare[0]: (block >> 1) & 1, spare[1]: block & 1}
        place = jnp.zeros((BLOCKS,), jnp.int32)
        for phase in head:
            place = place * 2 + (natural[phase] ^ bit_at(phase))
        return place

    return per_core(places(orders[0]), places(orders[1]))


class GradSum:
    def __init__(self, terms, orders, outs):
        self.terms, self.outs = terms, outs
        self.phases = list(zip(*orders))
        dp_phases = [[p for p in order if p != ROW] for order in orders]
        self.first, self.second = [tuple(order[i] for order in dp_phases) for i in range(2)]
        self.back = list(zip(*[list(reversed(order[:-1])) for order in dp_phases]))
        self.at = 0
        self.results = None

    def product(self, index):
        cut = [dot_tokens(part(left, index, 1), right).astype(LOW) for left, right in self.terms]
        return cut[0] if len(cut) == 1 else jnp.concatenate(cut, axis=1)

    def begin(self):
        sent = self.product(1)
        self.got = swap_phase(sent, self.phases[0])
        return sent

    def keep(self):
        self.kept = self.product(0)
        return self.kept

    def advance(self, *earlier):
        got = after(self.got, *earlier) if earlier else self.got
        self.at += 1
        spot = self.at - len(self.phases)
        if spot < 0:
            held = self.kept.astype(F32) + got.astype(F32)
            phases = self.phases[self.at]
            if spot == -1:
                sent = self.kept = held.astype(LOW)
            elif self.at < 3:
                sent = part(held, 1, 0).astype(LOW)
                self.kept = part(held, 0, 0).astype(LOW)
            else:
                mine = per_core(bit_at(phases[0]), bit_at(phases[1]))
                sent = pick(held, 1 - mine).astype(LOW)
                self.kept = pick(held, mine).astype(LOW)
        else:
            if spot == 0:
                low = (self.kept.astype(F32) + got.astype(F32)).astype(LOW)
            elif spot <= len(self.back) - 2:
                phases = self.back[spot - 1]
                flip = per_core(bit_at(phases[0]), bit_at(phases[1])) == 1
                low = jnp.concatenate(
                    [jnp.where(flip, got, self.kept), jnp.where(flip, self.kept, got)], axis=0
                )
            elif spot == len(self.back) - 1:
                low = jnp.concatenate([self.kept, got], axis=0)
            else:
                self.results = self.spread(self.kept, got)
                return self.results[0]
            phases = self.back[spot]
            sent = self.kept = low
        self.got = swap_phase(sent, phases)
        return sent

    def spread(self, near, far):
        bits = per_core(*[bit_at(self.first[i]) * 2 + bit_at(self.second[i]) for i in range(2)])
        places = lax.iota(jnp.int32, 4) ^ bits
        size = near.shape[0] // 2
        rows = 4 * size

        def kernel(place_ref, near_ref, far_ref, *out_refs):
            def write(values):
                values = values.astype(F32)
                for ref, (begin, end, turned) in zip(out_refs, self.outs):
                    ref[...] = values[:, begin:end].T if turned else values[:, begin:end]

            @pl.when(pl.program_id(0) < 2)
            def _():
                write(near_ref[...])

            @pl.when(pl.program_id(0) >= 2)
            def _():
                write(far_ref[...])

        shapes = []
        specs = []
        for begin, end, turned in self.outs:
            if turned:
                shapes.append(jax.ShapeDtypeStruct((end - begin, rows), F32))
                specs.append(pl.BlockSpec((end - begin, size), lambda i, t: (0, t[i])))
            else:
                shapes.append(jax.ShapeDtypeStruct((rows, end - begin), F32))
                specs.append(pl.BlockSpec((size, end - begin), lambda i, t: (t[i], 0)))
        width = near.shape[1]
        return pl.pallas_call(
            kernel,
            grid_spec=pltpu.PrefetchScalarGridSpec(
                num_scalar_prefetch=1,
                grid=(4,),
                in_specs=[
                    pl.BlockSpec((size, width), lambda i, t: (jnp.minimum(i, 1), 0)),
                    pl.BlockSpec((size, width), lambda i, t: (jnp.maximum(i - 2, 0), 0)),
                ],
                out_specs=specs,
            ),
            out_shape=shapes,
            cost_estimate=pl.CostEstimate(
                flops=1, bytes_accessed=8 * rows * width, transcendentals=0
            ),
        )(places, near, far)


def reduce_small(packed):
    for axis in ("row", "dp"):
        for bit in bits_of(axis):
            packed = packed + swap(packed, axis, bit)
    return packed


ORDERS_DOWN = [[ROW, 0, 1], [0, ROW, 1]]
ORDERS_UP = [[1, 0, ROW], [0, 1, ROW]]
ORDERS_ATTENTION = [[ROW, 0, 1], [1, ROW, 0]]
TAIL = "UWQKaWUQKWUQKoWUQKUQKQK"


def body(
    layer_input,
    cotangent,
    lengths,
    dealing,
    w_query,
    w_key,
    w_value,
    bias_query,
    bias_value,
    w_out,
    bias_out,
    w_up,
    bias_up,
    w_down,
    bias_down,
    gain_attention_in,
    shift_attention_in,
    gain_attention_out,
    shift_attention_out,
    gain_ffn_in,
    shift_ffn_in,
    gain_ffn_out,
    shift_ffn_out,
):
    row_count = lax.axis_size("row")
    groups = lax.axis_size("dp")
    shard_count = groups * row_count
    row_index = lax.axis_index("row")
    group_index = lax.axis_index("dp")
    rows = layer_input.shape[0]
    local_width = layer_input.shape[2]
    places = rows // shard_count
    group_rows = rows * row_count

    routes, grid_ofs = route_tables(lengths, dealing, groups, rows, shard_count, row_count)
    place = (routes[:, None] == lax.iota(jnp.int32, rows)[None, :]).astype(LOW)

    def deal(values):
        sent = dot(place, values.reshape(rows, local_width)).astype(LOW)
        sent = sent.reshape(places, shard_count, local_width)
        got = lax.all_to_all(sent, ("dp", "row"), split_axis=1, concat_axis=1, tiled=True)
        return got.reshape(rows, local_width)

    def undo_deal(values):
        sent = values.astype(LOW).reshape(places, shard_count, local_width)
        got = lax.all_to_all(sent, ("dp", "row"), split_axis=1, concat_axis=1, tiled=True)
        got = got.reshape(rows, local_width)
        return dot_tokens(place, got).astype(LOW).reshape(rows, 1, local_width)

    own_ofs = jnp.sum(
        jnp.where((lax.iota(jnp.int32, groups) == group_index)[:, None], grid_ofs, 0), axis=0
    )
    positions = row_index * rows + lax.iota(jnp.int32, rows)
    begin = jnp.max(
        jnp.where(positions[:, None] >= own_ofs[None, :], own_ofs[None, :], 0), axis=1
    )
    begin = (begin - row_index * rows).reshape(1, rows)

    packed = jnp.stack(
        [
            gain_attention_in,
            shift_attention_in,
            gain_attention_out,
            shift_attention_out,
            gain_ffn_in,
            shift_ffn_in,
            gain_ffn_out,
            shift_ffn_out,
            bias_out,
            bias_down,
        ]
    )
    vectors = col_pieces(packed)
    rest = list(bits_of("dp"))[2:]
    orders_up = [head + rest for head in ORDERS_UP]
    orders_down = [head + rest for head in ORDERS_DOWN]
    orders_attention = [head + rest for head in ORDERS_ATTENTION]
    column = lax.axis_index("col").reshape(1)

    def scalars_for(orders):
        return jnp.concatenate([column, place_table(orders)])

    x_own = deal(layer_input)
    x_low_own = lax.ppermute(x_own, "row", [(0, 1)])
    g_own = deal(cotangent)
    x = col_pieces(x_own)
    scalars_attention = scalars_for(orders_attention)
    h1, h1_blocks = row_call(
        norm_in_kernel, scalars_attention, vectors, [x], [(D, LOW), (D, LOW)], 8
    )
    queries = ((dot(h1, w_query) + bias_query) * (1.0 / math.sqrt(DH))).astype(LOW)
    keys = dot(h1, w_key).astype(LOW)
    values = (dot(h1, w_value) + bias_value).astype(LOW)

    width = queries.shape[1]
    top, norm, acc = attend_call(
        forward_own_kernel,
        rows,
        width,
        ["line", "rows", "rows", "rows"],
        [("stat", F32), ("stat", F32), ("cols", F32)],
        attention_cost(rows, width, 3, 10),
    )(begin, queries, keys, values)

    x_low = col_pieces(after(x_low_own, queries))
    (h_low,) = row_call(norm_in_kernel, column, vectors, [x_low], [(D, LOW)], 8)
    keys_low = dot(h_low, w_key).astype(LOW)
    values_low = (dot(h_low, w_value) + bias_value).astype(LOW)
    attended, attended_t, log_total = attend_call(
        forward_low_kernel,
        rows,
        width,
        ["line", "rows", "rows", "rows", "stat", "stat", "cols"],
        [("rows", LOW), ("cols", F32), ("stat", F32)],
        attention_cost(rows, width, 4, 16),
    )(begin, queries, keys_low, values_low, top, norm, acc)

    branch = col_parts(dot(attended, w_out).astype(LOW))
    h2, h2_blocks, y_own = row_call(
        norm_mid_kernel,
        scalars_for(orders_up),
        vectors,
        [branch, x],
        [(D, LOW), (D, LOW), (local_width, F32)],
        24,
    )
    pre = dot(h2, w_up) + bias_up
    cube = math.sqrt(2.0 / math.pi)
    bend = jnp.tanh(cube * (pre + 0.044715 * pre * pre * pre))
    hidden = (0.5 * pre * (1.0 + bend)).astype(LOW)
    slope = 0.5 * (1.0 + bend) + 0.5 * pre * (1.0 - bend * bend) * cube * (
        1.0 + 3.0 * 0.044715 * pre * pre
    )
    slope = slope.astype(LOW)
    ffn = col_parts(dot(hidden, w_down).astype(LOW))
    g = col_pieces(g_own)
    d_ffn, d_ffn_blocks, result, sums4 = row_call(
        norm_out_kernel,
        scalars_for(orders_down),
        vectors,
        [ffn, g, [y_own]],
        [(D, LOW), (D, LOW), (local_width, LOW), local_width],
        30,
    )

    ff = hidden.shape[1]
    down = GradSum([(d_ffn_blocks, hidden)], orders_down, [(0, ff, True)])
    tip = down.begin()
    d_pre = dot_back(after(d_ffn, tip), w_down) * slope.astype(F32)
    d_pre = d_pre.astype(LOW)
    up = GradSum([(h2_blocks, d_pre)], orders_up, [(0, ff, False)])
    tip = up.begin()
    d_h2 = col_parts(dot_back(after(d_pre, tip), w_up).astype(LOW))
    kept_down = down.keep()
    kept_up = up.keep()
    d_branch, d_branch_blocks, d_middle, sums3 = row_call(
        norm_back_kernel,
        scalars_attention,
        vectors,
        [d_h2, g, x, branch],
        [(D, LOW), (D, LOW), (local_width, F32), local_width],
        60,
    )
    d_attended = dot_back(d_branch, w_out).astype(LOW)
    d_attended = after(d_attended, kept_down, kept_up)
    back_ins = ["line", "rows", "rows", "rows", "rows", "cols", "stat"]
    dq_low, dk_low, dv_low = attend_call(
        functools.partial(backward_kernel, False),
        rows,
        width,
        back_ins,
        [("cols", F32), ("rows", LOW), ("rows", LOW)],
        attention_cost(rows, width, 10, 24),
    )(begin, queries, keys_low, values_low, d_attended, attended_t, log_total)
    tip = down.advance(dq_low)
    dk_back = lax.ppermute(dk_low, "row", [(1, 0)])
    dv_back = lax.ppermute(dv_low, "row", [(1, 0)])
    d_query, dk_own, dv_own = attend_call(
        functools.partial(backward_kernel, True),
        rows,
        width,
        back_ins + ["cols"],
        [("rows", LOW), ("rows", LOW), ("rows", LOW)],
        attention_cost(rows, width, 8, 24),
    )(begin, queries, keys, values, after(d_attended, tip), attended_t, log_total, dq_low)

    query_out = GradSum(
        [(h1_blocks, d_query), (d_branch_blocks, attended)],
        orders_attention,
        [(0, width, False), (width, 2 * width, True)],
    )
    tip = query_out.begin()
    tip = up.advance(tip)
    tip = down.advance(tip)
    kept = query_out.keep()
    dk_back, dv_back = after(dk_back, tip, kept), after(dv_back, tip, kept)
    d_key = (dk_own.astype(F32) + dk_back.astype(F32)).astype(LOW)
    d_value = (dv_own.astype(F32) + dv_back.astype(F32)).astype(LOW)
    key_value = GradSum(
        [(h1_blocks, d_key), (h1_blocks, d_value)],
        orders_attention,
        [(0, width, False), (width, 2 * width, False)],
    )
    tip = key_value.begin()
    d_h1 = dot_back(after(d_query, tip), w_query) + dot_back(d_key, w_key)
    d_h1 = col_parts((d_h1 + dot_back(d_value, w_value)).astype(LOW))
    kept = key_value.keep()
    in_grad, sums1 = row_call(
        norm_last_kernel,
        column,
        vectors,
        [d_h1, x, [d_middle]],
        [(local_width, LOW), local_width],
        20,
    )
    tip = after(in_grad, kept)
    chains = {"W": down, "U": up, "Q": query_out, "K": key_value}
    for name in TAIL:
        if name == "a":
            input_grad = undo_deal(after(in_grad, tip))
        elif name == "o":
            output = undo_deal(after(result, tip))
        else:
            tip = chains[name].advance(tip)
    for chain in chains.values():
        while chain.results is None:
            tip = chain.advance(tip)

    def summed(values):
        return jnp.sum(values.astype(F32), axis=0).reshape(-1, local_width)

    up_rows = d_pre.shape[1] // local_width
    smalls = reduce_small(
        jnp.concatenate(
            [sums1, sums3, sums4, summed(d_query), summed(d_value), summed(d_pre)], axis=0
        )
    )
    grad_query, grad_out = query_out.results
    grad_key, grad_value = key_value.results
    (grad_up,) = up.results
    (grad_down,) = down.results
    return (
        output,
        input_grad,
        grad_query,
        grad_key,
        grad_value,
        smalls[24],
        smalls[25],
        grad_out,
        smalls[12],
        grad_up,
        smalls[26 : 26 + up_rows].reshape(-1),
        grad_down,
        smalls[18],
        smalls[0],
        smalls[1],
        smalls[10],
        smalls[11],
        smalls[8],
        smalls[9],
        smalls[16],
        smalls[17],
    )


def solution(mesh):
    shards = P(None, ("dp", "row"), "col")
    by_col = P("col")
    vectors = (by_col,) * 8
    return jax.shard_map(
        body,
        mesh=mesh,
        in_specs=(
            shards,
            shards,
            P(),
            P(),
            P(None, "col"),
            P(None, "col"),
            P(None, "col"),
            by_col,
            by_col,
            P("col", None),
            by_col,
            P(None, "col"),
            by_col,
            P("col", None),
            by_col,
            *vectors,
        ),
        out_specs=(
            shards,
            shards,
            P("row", "col"),
            P("row", "col"),
            P("row", "col"),
            by_col,
            by_col,
            P("col", "row"),
            by_col,
            P("row", "col"),
            by_col,
            P("col", "row"),
            by_col,
            *vectors,
        ),
        check_vma=False,
    )
```

```python
import functools
import math

import jax
import jax.numpy as jnp
from jax import lax
from jax.experimental import pallas as pl
from jax.experimental.pallas import tpu as pltpu
from jax.sharding import PartitionSpec as P

D = 1024
DH = 64
PAIR = 2 * DH
EPSILON = 1e-05
MASKED = -1e30
LOW = jnp.bfloat16
F32 = jnp.float32
BRIEF = pl.CostEstimate(flops=1, bytes_accessed=1, transcendentals=0)


def swap(values, axis, bit):
    size = lax.axis_size(axis)
    return lax.ppermute(values, axis, [(i, i ^ (1 << bit)) for i in range(size)])


def bits_of(axis):
    return range(lax.axis_size(axis).bit_length() - 1)


def bit_at(phase):
    if phase == ROW:
        return lax.axis_index("row")
    return (lax.axis_index("dp") >> phase) & 1


ROW = "row"


def swap_phase(values, phases):
    sizes = [lax.axis_size(axis) for axis in ("dp", "row", "col")]
    pairs = []
    for dp in range(sizes[0]):
        for row in range(sizes[1]):
            for col in range(sizes[2]):
                phase = phases[col % 2]
                there = (dp, row ^ 1) if phase == ROW else (dp ^ (1 << phase), row)
                pairs.append(
                    (
                        (dp * sizes[1] + row) * sizes[2] + col,
                        (there[0] * sizes[1] + there[1]) * sizes[2] + col,
                    )
                )
    return lax.ppermute(values, ("dp", "row", "col"), pairs)


def per_core(even, odd):
    return jnp.where(lax.axis_index("col") % 2 == 0, even, odd)


def col_pieces(own):
    pieces = [own]
    for bit in bits_of("col"):
        pieces = pieces + [swap(piece, "col", bit) for piece in pieces]
    return pieces


def col_parts(partial):
    bits = list(bits_of("col"))
    for bit in bits[:-1]:
        partial = (partial.astype(F32) + swap(partial, "col", bit).astype(F32)).astype(LOW)
    return [partial, swap(partial, "col", bits[-1])]


def after(values, *earlier):
    return lax.optimization_barrier((values, *earlier))[0]


def part(values, index, dim):
    size = values.shape[dim] // 2
    return lax.slice_in_dim(values, index * size, (index + 1) * size, axis=dim)


def dot(left, right):
    return jnp.dot(left, right, preferred_element_type=F32)


def dot_back(left, right):
    return lax.dot_general(left, right, (((1,), (1,)), ((), ())), preferred_element_type=F32)


def dot_tokens(left, right):
    return lax.dot_general(left, right, (((0,), (0,)), ((), ())), preferred_element_type=F32)


BLOCKS = 8
GAIN1, SHIFT1, GAIN2, SHIFT2, GAIN3, SHIFT3, GAIN4, SHIFT4, BIAS_OUT, BIAS_DOWN = range(10)


def total(parts):
    return functools.reduce(lambda a, b: a + b, parts)


def row_mean(pieces):
    return total([jnp.sum(p, axis=1, keepdims=True) for p in pieces]) * (1.0 / D)


def normalize(pieces):
    average = row_mean(pieces)
    inverse = lax.rsqrt(row_mean([p * p for p in pieces]) - average * average + EPSILON)
    return [(p - average) * inverse for p in pieces], inverse


def normalize_back(grads, scaled, inverse, gains):
    pushed = [e * g for e, g in zip(grads, gains)]
    mean_push = row_mean(pushed)
    mean_dot = row_mean([f * n for f, n in zip(pushed, scaled)])
    return [inverse * (f - mean_push - n * mean_dot) for f, n in zip(pushed, scaled)]


def span(column, k, width):
    return pl.ds(pl.multiple_of((column ^ k) * width, 128), width)


def load_pieces(refs):
    return [ref[...].astype(F32) for ref in refs]


def load_ordered(refs, column, count):
    width = refs[0].shape[1] // count
    return [
        total([ref[:, span(column, k, width)].astype(F32) for ref in refs]) for k in range(count)
    ]


def store_ordered(ref, column, pieces):
    width = ref.shape[1] // len(pieces)
    for k, piece in enumerate(pieces):
        ref[:, span(column, k, width)] = piece


def store_blocks(ref, table, column, pieces):
    size = ref.shape[1] // BLOCKS
    width = ref.shape[1] // len(pieces)
    for k, piece in enumerate(pieces):
        first = (column ^ k) * (width // size)
        for j in range(width // size):
            place = pl.multiple_of(table[first + j] * size, 128)
            ref[:, pl.ds(place, size)] = piece[:, j * size : (j + 1) * size]


def column_sums(ref, rows):
    @pl.when(pl.program_id(0) == 0)
    def _():
        ref[...] = jnp.zeros(ref.shape, F32)

    for at, values in enumerate(rows):
        ref[at : at + 1, :] += jnp.sum(values, axis=0, keepdims=True)


def vector_of(vector_refs, index):
    return [ref[index : index + 1, :] for ref in vector_refs]


def plus(pieces, vectors):
    return [p + v for p, v in zip(pieces, vectors)]


def affine(scaled, gains, shifts):
    return [s * g + b for s, g, b in zip(scaled, gains, shifts)]


def norm_in_kernel(scalars, vec, x, h, h_blocks=None):
    scaled, _ = normalize(load_pieces(x))
    out = affine(scaled, vector_of(vec, GAIN1), vector_of(vec, SHIFT1))
    out = [p.astype(LOW) for p in out]
    store_ordered(h[0], scalars[0], out)
    if h_blocks is not None:
        store_blocks(h_blocks[0], scalars.table(), scalars[0], out)


def middle_of(column, vec, branch, x):
    held = plus(load_ordered(branch, column, len(x)), vector_of(vec, BIAS_OUT))
    scaled, inverse = normalize(held)
    out = affine(scaled, vector_of(vec, GAIN2), vector_of(vec, SHIFT2))
    return scaled, inverse, [a + b for a, b in zip(load_pieces(x), out)]


def norm_mid_kernel(scalars, vec, branch, x, h, h_blocks, y):
    column = scalars[0]
    _, _, middle = middle_of(column, vec, branch, x)
    y[0][...] = middle[0]
    scaled, _ = normalize(middle)
    out = affine(scaled, vector_of(vec, GAIN3), vector_of(vec, SHIFT3))
    out = [p.astype(LOW) for p in out]
    store_ordered(h[0], column, out)
    store_blocks(h_blocks[0], scalars.table(), column, out)


def norm_out_kernel(scalars, vec, ffn, g, y, d_ffn, d_blocks, result, sums):
    column = scalars[0]
    held = plus(load_ordered(ffn, column, len(g)), vector_of(vec, BIAS_DOWN))
    scaled, inverse = normalize(held)
    gains = vector_of(vec, GAIN4)
    out = y[0][...] + scaled[0] * gains[0] + vector_of(vec, SHIFT4)[0]
    result[0][...] = out.astype(LOW)
    grads = load_pieces(g)
    back = [p.astype(LOW) for p in normalize_back(grads, scaled, inverse, gains)]
    store_ordered(d_ffn[0], column, back)
    store_blocks(d_blocks[0], scalars.table(), column, back)
    column_sums(sums[0], [grads[0] * scaled[0], grads[0], back[0].astype(F32)])


def norm_back_kernel(scalars, vec, d_h2, g, x, branch, d_branch, d_blocks, d_middle, sums):
    column = scalars[0]
    scaled2, inverse2, middle = middle_of(column, vec, branch, x)
    scaled3, inverse3 = normalize(middle)
    grads3 = load_ordered(d_h2, column, len(x))
    back3 = normalize_back(grads3, scaled3, inverse3, vector_of(vec, GAIN3))
    grads2 = [a + b for a, b in zip(load_pieces(g), back3)]
    d_middle[0][...] = grads2[0]
    back2 = normalize_back(grads2, scaled2, inverse2, vector_of(vec, GAIN2))
    back2 = [p.astype(LOW) for p in back2]
    store_ordered(d_branch[0], column, back2)
    store_blocks(d_blocks[0], scalars.table(), column, back2)
    column_sums(
        sums[0],
        [
            grads3[0] * scaled3[0],
            grads3[0],
            grads2[0] * scaled2[0],
            grads2[0],
            back2[0].astype(F32),
        ],
    )


def norm_last_kernel(scalars, vec, d_h1, x, d_middle, out, sums):
    column = scalars[0]
    scaled, inverse = normalize(load_pieces(x))
    grads = load_ordered(d_h1, column, len(x))
    back = normalize_back(grads, scaled, inverse, vector_of(vec, GAIN1))
    out[0][...] = (d_middle[0][...] + back[0]).astype(LOW)
    column_sums(sums[0], [grads[0] * scaled[0], grads[0]])


class Scalars:
    def __init__(self, ref):
        self.ref = ref

    def __getitem__(self, index):
        return self.ref[index]

    def table(self):
        return Table(self.ref)


class Table:
    def __init__(self, ref):
        self.ref = ref

    def __getitem__(self, index):
        return self.ref[index + 1]


def row_call(kernel, scalars, vectors, ins, outs):
    rows = ins[0][0].shape[0]
    step = min(256, rows)
    counts = [len(vectors)] + [len(group) for group in ins] + [1] * len(outs)

    def whole(scalar_ref, *refs):
        groups = []
        for count in counts:
            groups.append(refs[:count])
            refs = refs[count:]
        kernel(Scalars(scalar_ref), *groups)

    def block(width):
        return pl.BlockSpec((step, width), lambda i, c: (i, 0))

    flat = [a for group in ins for a in group]
    shapes = []
    specs = []
    for out in outs:
        if isinstance(out, tuple):
            shapes.append(jax.ShapeDtypeStruct((rows, out[0]), out[1]))
            specs.append(block(out[0]))
        else:
            shapes.append(jax.ShapeDtypeStruct((8, out), F32))
            specs.append(pl.BlockSpec((8, out), lambda i, c: (0, 0)))
    return pl.pallas_call(
        whole,
        grid_spec=pltpu.PrefetchScalarGridSpec(
            num_scalar_prefetch=1,
            grid=(rows // step,),
            in_specs=[pl.BlockSpec(v.shape, lambda i, c: (0, 0)) for v in vectors]
            + [block(a.shape[1]) for a in flat],
            out_specs=specs,
        ),
        out_shape=shapes,
        cost_estimate=BRIEF,
    )(scalars, *vectors, *flat)


def route_tables(lengths, dealing, groups, half_rows, shard_count, row_count):
    seq_count = lengths.shape[0]
    per_group = seq_count // groups
    seq_ids = lax.iota(jnp.int32, seq_count)
    units = lengths // shard_count
    starts = jnp.sum(jnp.where(seq_ids[None, :] < seq_ids[:, None], units[None, :], 0), axis=1)
    chosen = dealing[:, None] == seq_ids[None, :]
    slot_len = jnp.sum(jnp.where(chosen, units[None, :], 0), axis=1)
    slot_in = jnp.sum(jnp.where(chosen, starts[None, :], 0), axis=1)
    earlier = (seq_ids[None, :] < seq_ids[:, None]) & (
        seq_ids[None, :] // per_group == seq_ids[:, None] // per_group
    )
    slot_ofs = jnp.sum(jnp.where(earlier, slot_len[None, :], 0), axis=1)
    grid_ofs = slot_ofs.reshape(groups, per_group)
    grid_anchor = (slot_in - slot_ofs).reshape(groups, per_group)
    places = half_rows // shard_count
    unit = (
        lax.broadcasted_iota(jnp.int32, (places, groups, row_count), 2) * places
        + lax.broadcasted_iota(jnp.int32, (places, groups, row_count), 0)
    )
    anchor = jnp.broadcast_to(grid_anchor[None, :, :1], unit.shape)
    for k in range(1, per_group):
        anchor = jnp.where(
            unit >= grid_ofs[None, :, k : k + 1], grid_anchor[None, :, k : k + 1], anchor
        )
    return (anchor + unit).reshape(half_rows), grid_ofs * shard_count


def head_lanes(shape, dim, head):
    lane = lax.broadcasted_iota(jnp.int32, shape, dim)
    return (lane >= head * DH) & (lane < (head + 1) * DH)


def masked_head(values, dim, head):
    return jnp.where(head_lanes(values.shape, dim, head), values, jnp.zeros_like(values))


def forward_kernel(
    begin_ref, q_ref, k_low_ref, v_low_ref, k_ref, v_ref, out_ref, log_ref, bias_ref
):
    rows = q_ref.shape[0]

    @pl.when(pl.program_id(0) == 0)
    def _():
        key_pos = lax.broadcasted_iota(jnp.int32, (rows, 2 * rows), 1) - rows
        query_pos = lax.broadcasted_iota(jnp.int32, (rows, 2 * rows), 0)
        allowed = (key_pos <= query_pos) & (key_pos >= begin_ref[...])
        bias_ref[...] = jnp.where(allowed, 0.0, MASKED)

    step = min(256, rows)
    first = head_lanes((step, PAIR), 1, 0)
    for at in range(0, rows, step):
        here = slice(at, at + step)
        keys = at + step
        parts = []
        logs = []
        for head in range(2):
            query = masked_head(q_ref[here, :], 1, head)
            scores = jnp.concatenate(
                [dot_back(query, k_low_ref[...]), dot_back(query, k_ref[:keys, :])], axis=1
            )
            scores = scores + bias_ref[here, : rows + keys]
            top = jnp.max(scores, axis=1, keepdims=True)
            weights = jnp.exp(scores - top)
            norm = jnp.sum(weights, axis=1, keepdims=True)
            weights = weights.astype(LOW)
            part_low = dot(weights[:, :rows], v_low_ref[...])
            parts.append((part_low + dot(weights[:, rows:], v_ref[:keys, :])) / norm)
            logs.append(top + jnp.log(norm))
        out_ref[here, :] = jnp.where(first, parts[0], parts[1]).astype(LOW)
        turned = jnp.where(first, logs[0], logs[1]).T
        log_ref[0, 0:1, here] = turned[:1]
        log_ref[0, 1:2, here] = turned[DH : DH + 1]


def backward_kernel(own, begin_ref, q_ref, k_ref, v_ref, g_ref, out_ref, log_ref, *rest):
    if own:
        dq_low_ref, dq_ref, dkv_ref, bias_ref = rest
    else:
        dq_ref, dkv_ref, bias_ref = rest
    rows = k_ref.shape[0]

    @pl.when(pl.program_id(0) == 0)
    def _():
        key_pos = lax.broadcasted_iota(jnp.int32, (rows, rows), 0) + (0 if own else -rows)
        query_pos = lax.broadcasted_iota(jnp.int32, (rows, rows), 1)
        allowed = (key_pos <= query_pos) & (key_pos >= begin_ref[...])
        bias_ref[...] = jnp.where(allowed, 0.0, MASKED)

    dots = (g_ref[...].astype(F32) * out_ref[...].astype(F32)).T
    keys_t = k_ref[...].T
    dk = []
    dv = []
    step = min(256, rows) if own else rows
    for at in range(0, rows, step):
        here = slice(at, at + step)
        keys = at + step if own else rows
        dq = []
        new_dk = []
        new_dv = []
        for head in range(2):
            lanes = slice(head * DH, (head + 1) * DH)
            query = masked_head(q_ref[here, :], 1, head)
            grad = masked_head(g_ref[here, :], 1, head)
            scores = dot_back(k_ref[:keys, :], query) + bias_ref[:keys, here]
            prob = jnp.exp(scores - log_ref[0, head : head + 1, here])
            grad_prob = dot_back(v_ref[:keys, :], grad)
            row_dot = jnp.sum(dots[lanes, here], axis=0, keepdims=True)
            grad_score = (prob * (grad_prob - row_dot)).astype(LOW)
            dq.append(dot(keys_t[lanes, :keys], grad_score))
            new_dk.append(dot(grad_score, query))
            new_dv.append(dot(prob.astype(LOW), grad))
        dk.append(total(new_dk))
        dv.append(total(new_dv))
        if own:
            dq = jnp.concatenate(dq, axis=0) + dq_low_ref[:, here]
            dq_ref[here, :] = (dq * (1.0 / math.sqrt(DH))).T.astype(LOW)
        else:
            dq_ref[:DH, here] = dq[0]
            dq_ref[DH:, here] = dq[1]
    for at, parts in enumerate((dk, dv)):
        ends = sorted({p.shape[0] for p in parts})
        for begin, end in zip([0] + ends[:-1], ends):
            pieces = [p[begin:end] for p in parts if p.shape[0] >= end]
            dkv_ref[at, begin:end, :] = total(pieces).astype(LOW)


def pair_spec(rows):
    return pl.BlockSpec((rows, PAIR), lambda i: (0, i))


def pair_t_spec(rows):
    return pl.BlockSpec((PAIR, rows), lambda i: (i, 0))


def stat_spec(rows):
    return pl.BlockSpec((1, 2, rows), lambda i: (i, 0, 0))


def attend_call(kernel, rows, width, ins, outs, keys):
    pairs = width // PAIR
    shapes = {
        "rows": (pair_spec(rows), (rows, width)),
        "cols": (pair_t_spec(rows), (width, rows)),
        "stat": (stat_spec(rows), (pairs, 2, rows)),
        "two": (pl.BlockSpec((2, rows, PAIR), lambda i: (0, 0, i)), (2, rows, width)),
        "line": (pl.BlockSpec((1, rows), lambda i: (0, 0)), (1, rows)),
        "post": (pl.BlockSpec((rows, 1), lambda i: (0, 0)), (rows, 1)),
    }
    return pl.pallas_call(
        kernel,
        grid=(pairs,),
        in_specs=[shapes[kind][0] for kind in ins],
        out_specs=[shapes[kind][0] for kind, _ in outs],
        out_shape=[jax.ShapeDtypeStruct(shapes[kind][1], dtype) for kind, dtype in outs],
        scratch_shapes=[pltpu.VMEM((rows, keys), F32)],
        cost_estimate=BRIEF,
    )


def pick(values, index):
    size = values.shape[0] // 2
    return lax.dynamic_slice_in_dim(values, index * size, size, 0, allow_negative_indices=False)


def place_table(orders):
    def places(order):
        head = order[:3]
        spare = [phase for phase in head if phase != ROW]
        block = lax.iota(jnp.int32, BLOCKS)
        natural = {ROW: (block >> 2) & 1, spare[0]: (block >> 1) & 1, spare[1]: block & 1}
        place = jnp.zeros((BLOCKS,), jnp.int32)
        for phase in head:
            place = place * 2 + (natural[phase] ^ bit_at(phase))
        return place

    return per_core(places(orders[0]), places(orders[1]))


class GradSum:
    def __init__(self, name, terms, orders, outs):
        self.name, self.terms, self.outs = name, terms, outs
        self.phases = list(zip(*orders))
        dp_phases = [[p for p in order if p != ROW] for order in orders]
        self.first, self.second = [tuple(order[i] for order in dp_phases) for i in range(2)]
        self.back = list(zip(*[list(reversed(order[:-1])) for order in dp_phases]))
        self.at = 0
        self.results = None

    def product(self, index):
        cut = [dot_tokens(part(left, index, 1), right).astype(LOW) for left, right in self.terms]
        return cut[0] if len(cut) == 1 else jnp.concatenate(cut, axis=1)

    def begin(self):
        with jax.named_scope(self.name + "_phase0"):
            sent = self.product(1)
            self.got = swap_phase(sent, self.phases[0])
        return sent

    def keep(self, *earlier):
        if earlier:
            self.terms = [(left, after(right, *earlier)) for left, right in self.terms]
        self.kept = self.product(0)
        return self.kept

    def advance(self, *earlier):
        self.at += 1
        with jax.named_scope(f"{self.name}_phase{self.at}"):
            return self.step(after(self.got, *earlier))

    def step(self, got):
        spot = self.at - len(self.phases)
        if spot < 0:
            held = self.kept.astype(F32) + got.astype(F32)
            phases = self.phases[self.at]
            if spot == -1:
                sent = self.kept = held.astype(LOW)
            elif self.at < 3:
                sent = part(held, 1, 0).astype(LOW)
                self.kept = part(held, 0, 0).astype(LOW)
            else:
                mine = per_core(bit_at(phases[0]), bit_at(phases[1]))
                sent = pick(held, 1 - mine).astype(LOW)
                self.kept = pick(held, mine).astype(LOW)
        else:
            if spot == 0:
                low = (self.kept.astype(F32) + got.astype(F32)).astype(LOW)
            elif spot <= len(self.back) - 2:
                phases = self.back[spot - 1]
                flip = per_core(bit_at(phases[0]), bit_at(phases[1])) == 1
                low = jnp.concatenate(
                    [jnp.where(flip, got, self.kept), jnp.where(flip, self.kept, got)], axis=0
                )
            elif spot == len(self.back) - 1:
                low = jnp.concatenate([self.kept, got], axis=0)
            else:
                self.results = self.spread(self.kept, got)
                return self.results[0]
            phases = self.back[spot]
            sent = self.kept = low
        self.got = swap_phase(sent, phases)
        return sent

    def spread(self, near, far):
        bits = per_core(*[bit_at(self.first[i]) * 2 + bit_at(self.second[i]) for i in range(2)])
        places = lax.iota(jnp.int32, 4) ^ bits
        size = near.shape[0] // 2
        rows = 4 * size

        def kernel(place_ref, near_ref, far_ref, *out_refs):
            def write(values):
                values = values.astype(F32)
                for ref, (begin, end, turned) in zip(out_refs, self.outs):
                    ref[...] = values[:, begin:end].T if turned else values[:, begin:end]

            @pl.when(pl.program_id(0) < 2)
            def _():
                write(near_ref[...])

            @pl.when(pl.program_id(0) >= 2)
            def _():
                write(far_ref[...])

        shapes = []
        specs = []
        for begin, end, turned in self.outs:
            if turned:
                shapes.append(jax.ShapeDtypeStruct((end - begin, rows), F32))
                specs.append(pl.BlockSpec((end - begin, size), lambda i, t: (0, t[i])))
            else:
                shapes.append(jax.ShapeDtypeStruct((rows, end - begin), F32))
                specs.append(pl.BlockSpec((size, end - begin), lambda i, t: (t[i], 0)))
        width = near.shape[1]
        return pl.pallas_call(
            kernel,
            grid_spec=pltpu.PrefetchScalarGridSpec(
                num_scalar_prefetch=1,
                grid=(4,),
                in_specs=[
                    pl.BlockSpec((size, width), lambda i, t: (jnp.minimum(i, 1), 0)),
                    pl.BlockSpec((size, width), lambda i, t: (jnp.maximum(i - 2, 0), 0)),
                ],
                out_specs=specs,
            ),
            out_shape=shapes,
            cost_estimate=BRIEF,
        )(places, near, far)


class SmallSum:
    def __init__(self, packed):
        self.left = [("row", bit) for bit in bits_of("row")] + [("dp", bit) for bit in bits_of("dp")]
        self.held = packed
        self.got = swap(packed, *self.left.pop(0))
        self.results = None

    def advance(self, *earlier):
        self.held = self.held + after(self.got, *earlier)
        if self.left:
            self.got = swap(self.held, *self.left.pop(0))
        else:
            self.results = self.held
        return self.held


ORDERS_DOWN = [[ROW, 0, 1], [0, ROW, 1]]
ORDERS_UP = [[1, 0, ROW], [0, 1, ROW]]
ORDERS_ATTENTION = [[ROW, 0, 1], [1, ROW, 0]]
TAIL = "AaUWAsUWAsUWAsUsWAoUA"


def body(
    layer_input,
    cotangent,
    lengths,
    dealing,
    w_query,
    w_key,
    w_value,
    bias_query,
    bias_value,
    w_out,
    bias_out,
    w_up,
    bias_up,
    w_down,
    bias_down,
    gain_attention_in,
    shift_attention_in,
    gain_attention_out,
    shift_attention_out,
    gain_ffn_in,
    shift_ffn_in,
    gain_ffn_out,
    shift_ffn_out,
):
    row_count = lax.axis_size("row")
    groups = lax.axis_size("dp")
    shard_count = groups * row_count
    row_index = lax.axis_index("row")
    group_index = lax.axis_index("dp")
    rows = layer_input.shape[0]
    local_width = layer_input.shape[2]
    places = rows // shard_count
    group_rows = rows * row_count

    routes, grid_ofs = route_tables(lengths, dealing, groups, rows, shard_count, row_count)
    place = (routes[:, None] == lax.iota(jnp.int32, rows)[None, :]).astype(LOW)

    def deal(values):
        sent = dot(place, values.reshape(rows, local_width)).astype(LOW)
        sent = sent.reshape(places, shard_count, local_width)
        got = lax.all_to_all(sent, ("dp", "row"), split_axis=1, concat_axis=1, tiled=True)
        return got.reshape(rows, local_width)

    def undo_deal(values):
        sent = values.astype(LOW).reshape(places, shard_count, local_width)
        got = lax.all_to_all(sent, ("dp", "row"), split_axis=1, concat_axis=1, tiled=True)
        got = got.reshape(rows, local_width)
        return dot_tokens(place, got).astype(LOW).reshape(rows, 1, local_width)

    own_ofs = jnp.sum(
        jnp.where((lax.iota(jnp.int32, groups) == group_index)[:, None], grid_ofs, 0), axis=0
    )
    positions = row_index * rows + lax.iota(jnp.int32, rows)
    begin = jnp.max(
        jnp.where(positions[:, None] >= own_ofs[None, :], own_ofs[None, :], 0), axis=1
    )
    begin = (begin - row_index * rows).reshape(1, rows)

    packed = jnp.stack(
        [
            gain_attention_in,
            shift_attention_in,
            gain_attention_out,
            shift_attention_out,
            gain_ffn_in,
            shift_ffn_in,
            gain_ffn_out,
            shift_ffn_out,
            bias_out,
            bias_down,
        ]
    )
    vectors = col_pieces(packed)
    rest = list(bits_of("dp"))[2:]
    orders_up = [head + rest for head in ORDERS_UP]
    orders_down = [head + rest for head in ORDERS_DOWN]
    orders_attention = [head + rest for head in ORDERS_ATTENTION]
    column = lax.axis_index("col").reshape(1)

    def scalars_for(orders):
        return jnp.concatenate([column, place_table(orders)])

    x_own = deal(layer_input)
    x_low_own = lax.ppermute(x_own, "row", [(0, 1)])
    g_own = deal(cotangent)
    x = col_pieces(x_own)
    scalars_attention = scalars_for(orders_attention)
    h1, h1_blocks = row_call(
        norm_in_kernel, scalars_attention, vectors, [x], [(D, LOW), (D, LOW)]
    )
    queries = ((dot(h1, w_query) + bias_query) * (1.0 / math.sqrt(DH))).astype(LOW)
    keys = dot(h1, w_key).astype(LOW)
    values = (dot(h1, w_value) + bias_value).astype(LOW)

    width = queries.shape[1]
    x_low = col_pieces(after(x_low_own, queries))
    (h_low,) = row_call(norm_in_kernel, column, vectors, [x_low], [(D, LOW)])
    keys_low = dot(h_low, w_key).astype(LOW)
    values_low = (dot(h_low, w_value) + bias_value).astype(LOW)
    attended, log_total = attend_call(
        forward_kernel,
        rows,
        width,
        ["post"] + ["rows"] * 5,
        [("rows", LOW), ("stat", F32)],
        2 * rows,
    )(begin.reshape(rows, 1), queries, keys_low, values_low, keys, values)

    branch = col_parts(dot(attended, w_out).astype(LOW))
    h2, h2_blocks, y_own = row_call(
        norm_mid_kernel,
        scalars_for(orders_up),
        vectors,
        [branch, x],
        [(D, LOW), (D, LOW), (local_width, F32)],
    )
    pre = dot(h2, w_up) + bias_up
    cube = math.sqrt(2.0 / math.pi)
    bend = jnp.tanh(cube * (pre + 0.044715 * pre * pre * pre))
    hidden = (0.5 * pre * (1.0 + bend)).astype(LOW)
    slope = 0.5 * (1.0 + bend) + 0.5 * pre * (1.0 - bend * bend) * cube * (
        1.0 + 3.0 * 0.044715 * pre * pre
    )
    slope = slope.astype(LOW)
    ffn = col_parts(dot(hidden, w_down).astype(LOW))
    g = col_pieces(g_own)
    d_ffn, d_ffn_blocks, result, sums4 = row_call(
        norm_out_kernel,
        scalars_for(orders_down),
        vectors,
        [ffn, g, [y_own]],
        [(D, LOW), (D, LOW), (local_width, LOW), local_width],
    )

    ff = hidden.shape[1]
    down = GradSum("down", [(d_ffn_blocks, hidden)], orders_down, [(0, ff, True)])
    tip = down.begin()
    d_pre = dot_back(after(d_ffn, tip), w_down) * slope.astype(F32)
    d_pre = d_pre.astype(LOW)
    up = GradSum("up", [(h2_blocks, d_pre)], orders_up, [(0, ff, False)])
    tip = up.begin()
    d_h2 = col_parts(dot_back(after(d_pre, tip), w_up).astype(LOW))
    kept_down = down.keep(d_h2[0])
    d_branch, d_branch_blocks, d_middle, sums3 = row_call(
        norm_back_kernel,
        scalars_attention,
        vectors,
        [d_h2, g, x, branch],
        [(D, LOW), (D, LOW), (local_width, F32), local_width],
    )
    tip = down.advance(d_branch, kept_down)
    d_attended = dot_back(after(d_branch, tip), w_out).astype(LOW)
    back_ins = ["line"] + ["rows"] * 5 + ["stat"]
    dq_low, dkv_low = attend_call(
        functools.partial(backward_kernel, False),
        rows,
        width,
        back_ins,
        [("cols", F32), ("two", LOW)],
        rows,
    )(begin, queries, keys_low, values_low, d_attended, attended, log_total)
    dkv_back = lax.ppermute(dkv_low, "row", [(1, 0)])
    tip = up.keep(dq_low)
    tip = up.advance(tip)
    tip = down.advance(tip)
    d_query, dkv_own = attend_call(
        functools.partial(backward_kernel, True),
        rows,
        width,
        back_ins + ["cols"],
        [("rows", LOW), ("two", LOW)],
        rows,
    )(begin, queries, keys, values, after(d_attended, tip), attended, log_total, dq_low)

    tip = up.advance(d_query)
    tip = down.advance(tip)
    dkv = dkv_own.astype(F32) + after(dkv_back, tip).astype(F32)
    d_key, d_value = dkv[0].astype(LOW), dkv[1].astype(LOW)
    attention = GradSum(
        "attention",
        [
            (h1_blocks, d_query),
            (h1_blocks, d_key),
            (h1_blocks, d_value),
            (d_branch_blocks, attended),
        ],
        orders_attention,
        [(k * width, (k + 1) * width, k == 3) for k in range(4)],
    )
    tip = attention.begin()
    d_h1 = dot_back(after(d_query, tip), w_query) + dot_back(d_key, w_key)
    d_h1 = col_parts((d_h1 + dot_back(d_value, w_value)).astype(LOW))
    kept = attention.keep(d_h1[0])
    in_grad, sums1 = row_call(
        norm_last_kernel,
        column,
        vectors,
        [d_h1, x, [d_middle]],
        [(local_width, LOW), local_width],
    )
    tip = after(in_grad, kept)

    def summed(values):
        return jnp.sum(values.astype(F32), axis=0).reshape(-1, local_width)

    up_rows = d_pre.shape[1] // local_width
    packed_sums = jnp.concatenate(
        [sums1, sums3, sums4, summed(d_query), summed(d_value), summed(d_pre)], axis=0
    )
    small = SmallSum(after(packed_sums, tip))
    chains = {"W": down, "U": up, "A": attention, "s": small}
    for name in TAIL:
        if name == "a":
            input_grad = undo_deal(after(in_grad, tip))
        elif name == "o":
            output = undo_deal(after(result, tip))
        else:
            tip = chains[name].advance(tip)
    for chain in chains.values():
        while chain.results is None:
            tip = chain.advance(tip)

    smalls = small.results
    grad_query, grad_key, grad_value, grad_out = attention.results
    (grad_up,) = up.results
    (grad_down,) = down.results
    return (
        output,
        input_grad,
        grad_query,
        grad_key,
        grad_value,
        smalls[24],
        smalls[25],
        grad_out,
        smalls[12],
        grad_up,
        smalls[26 : 26 + up_rows].reshape(-1),
        grad_down,
        smalls[18],
        smalls[0],
        smalls[1],
        smalls[10],
        smalls[11],
        smalls[8],
        smalls[9],
        smalls[16],
        smalls[17],
    )


def solution(mesh):
    shards = P(None, ("dp", "row"), "col")
    by_col = P("col")
    vectors = (by_col,) * 8
    return jax.shard_map(
        body,
        mesh=mesh,
        in_specs=(
            shards,
            shards,
            P(),
            P(),
            P(None, "col"),
            P(None, "col"),
            P(None, "col"),
            by_col,
            by_col,
            P("col", None),
            by_col,
            P(None, "col"),
            by_col,
            P("col", None),
            by_col,
            *vectors,
        ),
        out_specs=(
            shards,
            shards,
            P("row", "col"),
            P("row", "col"),
            P("row", "col"),
            by_col,
            by_col,
            P("col", "row"),
            by_col,
            P("row", "col"),
            by_col,
            P("col", "row"),
            by_col,
            *vectors,
        ),
        check_vma=False,
    )
```

```python
import functools
import math

import jax
import jax.numpy as jnp
from jax import lax
from jax.experimental import pallas as pl
from jax.experimental.pallas import tpu as pltpu
from jax.sharding import PartitionSpec as P

D = 1024
DH = 64
PAIR = 2 * DH
EPSILON = 1e-05
MASKED = -1e30
LOW = jnp.bfloat16
F32 = jnp.float32
BRIEF = pl.CostEstimate(flops=1, bytes_accessed=1, transcendentals=0)


def swap(values, axis, bit):
    size = lax.axis_size(axis)
    return lax.ppermute(values, axis, [(i, i ^ (1 << bit)) for i in range(size)])


def bits_of(axis):
    return range(lax.axis_size(axis).bit_length() - 1)


def bit_at(phase):
    if phase == ROW:
        return lax.axis_index("row")
    return (lax.axis_index("dp") >> phase) & 1


ROW = "row"


def swap_phase(values, phases):
    sizes = [lax.axis_size(axis) for axis in ("dp", "row", "col")]
    pairs = []
    for dp in range(sizes[0]):
        for row in range(sizes[1]):
            for col in range(sizes[2]):
                phase = phases[col % 2]
                there = (dp, row ^ 1) if phase == ROW else (dp ^ (1 << phase), row)
                pairs.append(
                    (
                        (dp * sizes[1] + row) * sizes[2] + col,
                        (there[0] * sizes[1] + there[1]) * sizes[2] + col,
                    )
                )
    return lax.ppermute(values, ("dp", "row", "col"), pairs)


def per_core(even, odd):
    return jnp.where(lax.axis_index("col") % 2 == 0, even, odd)


def col_pieces(own):
    pieces = [own]
    for bit in bits_of("col"):
        pieces = pieces + [swap(piece, "col", bit) for piece in pieces]
    return pieces


def col_parts(partial):
    bits = list(bits_of("col"))
    for bit in bits[:-1]:
        partial = (partial.astype(F32) + swap(partial, "col", bit).astype(F32)).astype(LOW)
    return [partial, swap(partial, "col", bits[-1])]


def after(values, *earlier):
    return lax.optimization_barrier((values, *earlier))[0]


def dot(left, right):
    return jnp.dot(left, right, preferred_element_type=F32)


def dot_back(left, right):
    return lax.dot_general(left, right, (((1,), (1,)), ((), ())), preferred_element_type=F32)


def dot_tokens(left, right):
    return lax.dot_general(left, right, (((0,), (0,)), ((), ())), preferred_element_type=F32)


BLOCKS = 8
GAIN1, SHIFT1, GAIN2, SHIFT2, GAIN3, SHIFT3, GAIN4, SHIFT4, BIAS_OUT, BIAS_DOWN = range(10)


def total(parts):
    return functools.reduce(lambda a, b: a + b, parts)


def row_mean(pieces):
    return total([jnp.sum(p, axis=1, keepdims=True) for p in pieces]) * (1.0 / D)


def normalize(pieces):
    average = row_mean(pieces)
    inverse = lax.rsqrt(row_mean([p * p for p in pieces]) - average * average + EPSILON)
    return [(p - average) * inverse for p in pieces], inverse


def normalize_back(grads, scaled, inverse, gains):
    pushed = [e * g for e, g in zip(grads, gains)]
    mean_push = row_mean(pushed)
    mean_dot = row_mean([f * n for f, n in zip(pushed, scaled)])
    return [inverse * (f - mean_push - n * mean_dot) for f, n in zip(pushed, scaled)]


def span(column, k, width):
    return pl.ds(pl.multiple_of((column ^ k) * width, 128), width)


def load_pieces(refs):
    return [ref[...].astype(F32) for ref in refs]


def load_ordered(refs, column, count):
    width = refs[0].shape[1] // count
    return [
        total([ref[:, span(column, k, width)].astype(F32) for ref in refs]) for k in range(count)
    ]


def store_ordered(ref, column, pieces):
    width = ref.shape[1] // len(pieces)
    for k, piece in enumerate(pieces):
        ref[:, span(column, k, width)] = piece


def store_blocks(ref, table, column, pieces):
    size = ref.shape[1] // BLOCKS
    width = ref.shape[1] // len(pieces)
    for k, piece in enumerate(pieces):
        first = (column ^ k) * (width // size)
        for j in range(width // size):
            place = pl.multiple_of(table[first + j] * size, 128)
            ref[:, pl.ds(place, size)] = piece[:, j * size : (j + 1) * size]


def column_sums(ref, rows):
    for at, values in enumerate(rows):
        ref[at : at + 1, :] += jnp.sum(values, axis=0, keepdims=True)


def vector_of(vector_refs, index):
    return [ref[index : index + 1, :] for ref in vector_refs]


def plus(pieces, vectors):
    return [p + v for p, v in zip(pieces, vectors)]


def affine(scaled, gains, shifts):
    return [s * g + b for s, g, b in zip(scaled, gains, shifts)]


def norm_in_kernel(scalars, vec, x, h, h_blocks=None):
    scaled, _ = normalize(load_pieces(x))
    out = affine(scaled, vector_of(vec, GAIN1), vector_of(vec, SHIFT1))
    out = [p.astype(LOW) for p in out]
    store_ordered(h[0], scalars[0], out)
    if h_blocks is not None:
        store_blocks(h_blocks[0], scalars.table(), scalars[0], out)


def middle_of(column, vec, branch, x):
    held = plus(load_ordered(branch, column, len(x)), vector_of(vec, BIAS_OUT))
    scaled, inverse = normalize(held)
    out = affine(scaled, vector_of(vec, GAIN2), vector_of(vec, SHIFT2))
    return scaled, inverse, [a + b for a, b in zip(load_pieces(x), out)]


def norm_mid_kernel(scalars, vec, branch, x, h, h_blocks, y):
    column = scalars[0]
    _, _, middle = middle_of(column, vec, branch, x)
    y[0][...] = middle[0]
    scaled, _ = normalize(middle)
    out = affine(scaled, vector_of(vec, GAIN3), vector_of(vec, SHIFT3))
    out = [p.astype(LOW) for p in out]
    store_ordered(h[0], column, out)
    store_blocks(h_blocks[0], scalars.table(), column, out)


def norm_out_kernel(scalars, vec, ffn, g, y, d_ffn, d_blocks, result, sums):
    column = scalars[0]
    held = plus(load_ordered(ffn, column, len(g)), vector_of(vec, BIAS_DOWN))
    scaled, inverse = normalize(held)
    gains = vector_of(vec, GAIN4)
    out = y[0][...] + scaled[0] * gains[0] + vector_of(vec, SHIFT4)[0]
    result[0][...] = out.astype(LOW)
    grads = load_pieces(g)
    back = [p.astype(LOW) for p in normalize_back(grads, scaled, inverse, gains)]
    store_ordered(d_ffn[0], column, back)
    store_blocks(d_blocks[0], scalars.table(), column, back)
    column_sums(sums[0], [grads[0] * scaled[0], grads[0], back[0].astype(F32)])


def norm_back_kernel(scalars, vec, d_h2, g, x, branch, d_branch, d_blocks, d_middle, sums):
    column = scalars[0]
    scaled2, inverse2, middle = middle_of(column, vec, branch, x)
    scaled3, inverse3 = normalize(middle)
    grads3 = load_ordered(d_h2, column, len(x))
    back3 = normalize_back(grads3, scaled3, inverse3, vector_of(vec, GAIN3))
    grads2 = [a + b for a, b in zip(load_pieces(g), back3)]
    d_middle[0][...] = grads2[0]
    back2 = normalize_back(grads2, scaled2, inverse2, vector_of(vec, GAIN2))
    back2 = [p.astype(LOW) for p in back2]
    store_ordered(d_branch[0], column, back2)
    store_blocks(d_blocks[0], scalars.table(), column, back2)
    column_sums(
        sums[0],
        [
            grads3[0] * scaled3[0],
            grads3[0],
            grads2[0] * scaled2[0],
            grads2[0],
            back2[0].astype(F32),
        ],
    )


def norm_last_kernel(scalars, vec, d_h1, x, d_middle, out, sums):
    column = scalars[0]
    scaled, inverse = normalize(load_pieces(x))
    grads = load_ordered(d_h1, column, len(x))
    back = normalize_back(grads, scaled, inverse, vector_of(vec, GAIN1))
    out[0][...] = (d_middle[0][...] + back[0]).astype(LOW)
    column_sums(sums[0], [grads[0] * scaled[0], grads[0]])


class Scalars:
    def __init__(self, ref):
        self.ref = ref

    def __getitem__(self, index):
        return self.ref[index]

    def table(self):
        return Table(self.ref)


class Table:
    def __init__(self, ref):
        self.ref = ref

    def __getitem__(self, index):
        return self.ref[index + 1]


def row_call(kernel, scalars, vectors, ins, outs):
    rows = ins[0][0].shape[0]
    step = min(256, rows)
    counts = [len(vectors)] + [len(group) for group in ins] + [1] * len(outs)

    chunk = min(128, step)

    def whole(scalar_ref, *refs):
        @pl.when(pl.program_id(0) == 0)
        def _():
            for ref, out in zip(refs[len(refs) - len(outs) :], outs):
                if not isinstance(out, tuple):
                    ref[...] = jnp.zeros(ref.shape, F32)

        def part(at, carry):
            groups = []
            used = 0
            here = pl.ds(pl.multiple_of(at * chunk, chunk), chunk)
            for count in counts:
                group = refs[used : used + count]
                used += count
                groups.append([r.at[here, :] if r.shape[0] == step else r for r in group])
            kernel(Scalars(scalar_ref), *groups)
            return carry

        lax.fori_loop(0, step // chunk, part, 0)

    def block(width):
        return pl.BlockSpec((step, width), lambda i, c: (i, 0))

    flat = [a for group in ins for a in group]
    shapes = []
    specs = []
    for out in outs:
        if isinstance(out, tuple):
            shapes.append(jax.ShapeDtypeStruct((rows, out[0]), out[1]))
            specs.append(block(out[0]))
        else:
            shapes.append(jax.ShapeDtypeStruct((8, out), F32))
            specs.append(pl.BlockSpec((8, out), lambda i, c: (0, 0)))
    return pl.pallas_call(
        whole,
        grid_spec=pltpu.PrefetchScalarGridSpec(
            num_scalar_prefetch=1,
            grid=(rows // step,),
            in_specs=[pl.BlockSpec(v.shape, lambda i, c: (0, 0)) for v in vectors]
            + [block(a.shape[1]) for a in flat],
            out_specs=specs,
        ),
        out_shape=shapes,
        cost_estimate=BRIEF,
    )(scalars, *vectors, *flat)


def route_tables(lengths, dealing, groups, half_rows, shard_count, row_count):
    seq_count = lengths.shape[0]
    per_group = seq_count // groups
    seq_ids = lax.iota(jnp.int32, seq_count)
    units = lengths // shard_count
    starts = jnp.sum(jnp.where(seq_ids[None, :] < seq_ids[:, None], units[None, :], 0), axis=1)
    chosen = dealing[:, None] == seq_ids[None, :]
    slot_len = jnp.sum(jnp.where(chosen, units[None, :], 0), axis=1)
    slot_in = jnp.sum(jnp.where(chosen, starts[None, :], 0), axis=1)
    earlier = (seq_ids[None, :] < seq_ids[:, None]) & (
        seq_ids[None, :] // per_group == seq_ids[:, None] // per_group
    )
    slot_ofs = jnp.sum(jnp.where(earlier, slot_len[None, :], 0), axis=1)
    grid_ofs = slot_ofs.reshape(groups, per_group)
    grid_anchor = (slot_in - slot_ofs).reshape(groups, per_group)
    places = half_rows // shard_count
    unit = (
        lax.broadcasted_iota(jnp.int32, (places, groups, row_count), 2) * places
        + lax.broadcasted_iota(jnp.int32, (places, groups, row_count), 0)
    )
    anchor = jnp.broadcast_to(grid_anchor[None, :, :1], unit.shape)
    for k in range(1, per_group):
        anchor = jnp.where(
            unit >= grid_ofs[None, :, k : k + 1], grid_anchor[None, :, k : k + 1], anchor
        )
    return (anchor + unit).reshape(half_rows), grid_ofs * shard_count


def head_lanes(shape, dim, head):
    lane = lax.broadcasted_iota(jnp.int32, shape, dim)
    return (lane >= head * DH) & (lane < (head + 1) * DH)


def masked_head(values, dim, head):
    return jnp.where(head_lanes(values.shape, dim, head), values, jnp.zeros_like(values))


def forward_kernel(
    begin_ref, q_ref, k_low_ref, v_low_ref, k_ref, v_ref, out_ref, log_ref, bias_ref
):
    rows = q_ref.shape[0]

    @pl.when(pl.program_id(0) == 0)
    def _():
        key_pos = lax.broadcasted_iota(jnp.int32, (rows, 2 * rows), 1) - rows
        query_pos = lax.broadcasted_iota(jnp.int32, (rows, 2 * rows), 0)
        allowed = (key_pos <= query_pos) & (key_pos >= begin_ref[...])
        bias_ref[...] = jnp.where(allowed, 0.0, MASKED)

    step = min(256, rows)
    first = head_lanes((step, PAIR), 1, 0)
    for at in range(0, rows, step):
        here = slice(at, at + step)
        keys = at + step
        parts = []
        logs = []
        for head in range(2):
            query = masked_head(q_ref[here, :], 1, head)
            scores = jnp.concatenate(
                [dot_back(query, k_low_ref[...]), dot_back(query, k_ref[:keys, :])], axis=1
            )
            scores = scores + bias_ref[here, : rows + keys]
            top = jnp.max(scores, axis=1, keepdims=True)
            weights = jnp.exp(scores - top)
            norm = jnp.sum(weights, axis=1, keepdims=True)
            weights = weights.astype(LOW)
            part_low = dot(weights[:, :rows], v_low_ref[...])
            parts.append((part_low + dot(weights[:, rows:], v_ref[:keys, :])) / norm)
            logs.append(top + jnp.log(norm))
        out_ref[here, :] = jnp.where(first, parts[0], parts[1]).astype(LOW)
        turned = jnp.where(first, logs[0], logs[1]).T
        log_ref[0, 0:1, here] = turned[:1]
        log_ref[0, 1:2, here] = turned[DH : DH + 1]


def backward_kernel(own, begin_ref, q_ref, k_ref, v_ref, g_ref, out_ref, log_ref, *rest):
    if own:
        dq_low_ref, dq_ref, dkv_ref, bias_ref = rest
    else:
        dq_ref, dkv_ref, bias_ref = rest
    rows = k_ref.shape[0]

    @pl.when(pl.program_id(0) == 0)
    def _():
        key_pos = lax.broadcasted_iota(jnp.int32, (rows, rows), 0) + (0 if own else -rows)
        query_pos = lax.broadcasted_iota(jnp.int32, (rows, rows), 1)
        allowed = (key_pos <= query_pos) & (key_pos >= begin_ref[...])
        bias_ref[...] = jnp.where(allowed, 0.0, MASKED)

    dots = (g_ref[...].astype(F32) * out_ref[...].astype(F32)).T
    keys_t = k_ref[...].T
    dk = []
    dv = []
    step = min(256, rows) if own else rows
    for at in range(0, rows, step):
        here = slice(at, at + step)
        keys = at + step if own else rows
        dq = []
        new_dk = []
        new_dv = []
        for head in range(2):
            lanes = slice(head * DH, (head + 1) * DH)
            query = masked_head(q_ref[here, :], 1, head)
            grad = masked_head(g_ref[here, :], 1, head)
            scores = dot_back(k_ref[:keys, :], query) + bias_ref[:keys, here]
            prob = jnp.exp(scores - log_ref[0, head : head + 1, here])
            grad_prob = dot_back(v_ref[:keys, :], grad)
            row_dot = jnp.sum(dots[lanes, here], axis=0, keepdims=True)
            grad_score = (prob * (grad_prob - row_dot)).astype(LOW)
            dq.append(dot(keys_t[lanes, :keys], grad_score))
            new_dk.append(dot(grad_score, query))
            new_dv.append(dot(prob.astype(LOW), grad))
        dk.append(total(new_dk))
        dv.append(total(new_dv))
        if own:
            dq = jnp.concatenate(dq, axis=0) + dq_low_ref[:, here]
            dq_ref[here, :] = (dq * (1.0 / math.sqrt(DH))).T.astype(LOW)
        else:
            dq_ref[:DH, here] = dq[0]
            dq_ref[DH:, here] = dq[1]
    for at, parts in enumerate((dk, dv)):
        ends = sorted({p.shape[0] for p in parts})
        for begin, end in zip([0] + ends[:-1], ends):
            pieces = [p[begin:end] for p in parts if p.shape[0] >= end]
            dkv_ref[at, begin:end, :] = total(pieces).astype(LOW)


def pair_spec(rows):
    return pl.BlockSpec((rows, PAIR), lambda i: (0, i))


def pair_t_spec(rows):
    return pl.BlockSpec((PAIR, rows), lambda i: (i, 0))


def stat_spec(rows):
    return pl.BlockSpec((1, 2, rows), lambda i: (i, 0, 0))


def attend_call(kernel, rows, width, ins, outs, keys):
    pairs = width // PAIR
    shapes = {
        "rows": (pair_spec(rows), (rows, width)),
        "cols": (pair_t_spec(rows), (width, rows)),
        "stat": (stat_spec(rows), (pairs, 2, rows)),
        "two": (pl.BlockSpec((2, rows, PAIR), lambda i: (0, 0, i)), (2, rows, width)),
        "line": (pl.BlockSpec((1, rows), lambda i: (0, 0)), (1, rows)),
        "post": (pl.BlockSpec((rows, 1), lambda i: (0, 0)), (rows, 1)),
    }
    return pl.pallas_call(
        kernel,
        grid=(pairs,),
        in_specs=[shapes[kind][0] for kind in ins],
        out_specs=[shapes[kind][0] for kind, _ in outs],
        out_shape=[jax.ShapeDtypeStruct(shapes[kind][1], dtype) for kind, dtype in outs],
        scratch_shapes=[pltpu.VMEM((rows, keys), F32)],
        cost_estimate=BRIEF,
    )


def pick(values, index):
    size = values.shape[0] // 2
    return lax.dynamic_slice_in_dim(values, index * size, size, 0, allow_negative_indices=False)


def place_table(orders):
    def places(order):
        head = order[:3]
        spare = [phase for phase in head if phase != ROW]
        block = lax.iota(jnp.int32, BLOCKS)
        natural = {ROW: (block >> 2) & 1, spare[0]: (block >> 1) & 1, spare[1]: block & 1}
        place = jnp.zeros((BLOCKS,), jnp.int32)
        for phase in head:
            place = place * 2 + (natural[phase] ^ bit_at(phase))
        return place

    return per_core(places(orders[0]), places(orders[1]))


class GradSum:
    def __init__(self, name, terms, orders, outs):
        self.name, self.terms, self.outs = name, terms, outs
        self.phases = list(zip(*orders))
        dp_phases = [[p for p in order if p != ROW] for order in orders]
        self.first, self.second = [tuple(order[i] for order in dp_phases) for i in range(2)]
        self.back = list(zip(*[list(reversed(order[:-1])) for order in dp_phases]))
        self.at = 0
        self.results = None

    def product(self, index):
        cut = []
        for left, right in self.terms:
            size = left.shape[1] // 2
            half = lax.slice_in_dim(left, index * size, (index + 1) * size, axis=1)
            cut.append(dot_tokens(half, right).astype(LOW))
        return cut[0] if len(cut) == 1 else jnp.concatenate(cut, axis=1)

    def begin(self):
        with jax.named_scope(self.name + "_phase0"):
            sent = self.product(1)
            self.got = swap_phase(sent, self.phases[0])
        return sent

    def keep(self, *earlier):
        if earlier:
            self.terms = [(left, after(right, *earlier)) for left, right in self.terms]
        self.held = [self.product(0)]
        return self.held[0]

    def advance(self, *earlier):
        self.at += 1
        with jax.named_scope(f"{self.name}_phase{self.at}"):
            return self.step(after(self.got, *earlier))

    def rows_sum(self, begin, end):
        return total([a[begin:end].astype(F32) for a in self.held]).astype(LOW)

    def step(self, got):
        spot = self.at - len(self.phases)
        rows = got.shape[0]
        if spot < 0:
            self.held.append(got)
            phases = self.phases[self.at]
            if spot == -1:
                sent = self.rows_sum(0, rows)
                self.held = [sent]
            elif self.at < 3:
                sent = self.rows_sum(rows // 2, rows)
            else:
                mine = per_core(bit_at(phases[0]), bit_at(phases[1]))
                held = self.rows_sum(0, rows)
                sent = pick(held, 1 - mine)
                self.held = [pick(held, mine)]
        else:
            kept = self.held[0]
            if spot == 0:
                low = (kept.astype(F32) + got.astype(F32)).astype(LOW)
            elif spot <= len(self.back) - 2:
                phases = self.back[spot - 1]
                flip = per_core(bit_at(phases[0]), bit_at(phases[1])) == 1
                low = jnp.concatenate(
                    [jnp.where(flip, got, kept), jnp.where(flip, kept, got)], axis=0
                )
            elif spot == len(self.back) - 1:
                low = jnp.concatenate([kept, got], axis=0)
            else:
                self.results = self.spread(kept, got)
                return self.results[0]
            phases = self.back[spot]
            sent = low
            self.held = [low]
        self.got = swap_phase(sent, phases)
        return sent

    def spread(self, near, far):
        bits = per_core(*[bit_at(self.first[i]) * 2 + bit_at(self.second[i]) for i in range(2)])
        places = lax.iota(jnp.int32, 4) ^ bits
        size = near.shape[0] // 2
        rows = 4 * size

        def kernel(place_ref, near_ref, far_ref, *out_refs):
            def write(values):
                values = values.astype(F32)
                for ref, (begin, end, turned) in zip(out_refs, self.outs):
                    ref[...] = values[:, begin:end].T if turned else values[:, begin:end]

            @pl.when(pl.program_id(0) < 2)
            def _():
                write(near_ref[...])

            @pl.when(pl.program_id(0) >= 2)
            def _():
                write(far_ref[...])

        shapes = []
        specs = []
        for begin, end, turned in self.outs:
            if turned:
                shapes.append(jax.ShapeDtypeStruct((end - begin, rows), F32))
                specs.append(pl.BlockSpec((end - begin, size), lambda i, t: (0, t[i])))
            else:
                shapes.append(jax.ShapeDtypeStruct((rows, end - begin), F32))
                specs.append(pl.BlockSpec((size, end - begin), lambda i, t: (t[i], 0)))
        width = near.shape[1]
        return pl.pallas_call(
            kernel,
            grid_spec=pltpu.PrefetchScalarGridSpec(
                num_scalar_prefetch=1,
                grid=(4,),
                in_specs=[
                    pl.BlockSpec((size, width), lambda i, t: (jnp.minimum(i, 1), 0)),
                    pl.BlockSpec((size, width), lambda i, t: (jnp.maximum(i - 2, 0), 0)),
                ],
                out_specs=specs,
            ),
            out_shape=shapes,
            cost_estimate=BRIEF,
        )(places, near, far)


ORDERS_DOWN = [[ROW, 0, 1], [0, ROW, 1]]
ORDERS_UP = [[1, 0, ROW], [0, 1, ROW]]
ORDERS_ATTENTION = [[ROW, 0, 1], [1, ROW, 0]]
TAIL = "UWAxAUWAUWUAAUA"


def body(
    layer_input,
    cotangent,
    lengths,
    dealing,
    w_query,
    w_key,
    w_value,
    bias_query,
    bias_value,
    w_out,
    bias_out,
    w_up,
    bias_up,
    w_down,
    bias_down,
    gain_attention_in,
    shift_attention_in,
    gain_attention_out,
    shift_attention_out,
    gain_ffn_in,
    shift_ffn_in,
    gain_ffn_out,
    shift_ffn_out,
):
    row_count = lax.axis_size("row")
    groups = lax.axis_size("dp")
    shard_count = groups * row_count
    row_index = lax.axis_index("row")
    group_index = lax.axis_index("dp")
    rows = layer_input.shape[0]
    local_width = layer_input.shape[2]
    places = rows // shard_count
    group_rows = rows * row_count

    routes, grid_ofs = route_tables(lengths, dealing, groups, rows, shard_count, row_count)
    place = (routes[:, None] == lax.iota(jnp.int32, rows)[None, :]).astype(LOW)

    def deal(values):
        sent = dot(place, values.reshape(rows, local_width)).astype(LOW)
        sent = sent.reshape(places, shard_count, local_width)
        got = lax.all_to_all(sent, ("dp", "row"), split_axis=1, concat_axis=1, tiled=True)
        return got.reshape(rows, local_width)

    def undo_deal(values, sums=None):
        sent = values.reshape(places, shard_count, local_width)
        if sums is not None:
            copies = (sums.shape[0],) + sent.shape[1:]
            spread = jnp.broadcast_to(sums.astype(LOW)[:, None, :], copies)
            sent = jnp.concatenate([sent, spread], axis=0)
        got = lax.all_to_all(sent, ("dp", "row"), split_axis=1, concat_axis=1, tiled=True)
        back = dot_tokens(place, got[:places].reshape(rows, local_width)).astype(LOW)
        back = back.reshape(rows, 1, local_width)
        if sums is None:
            return back
        return back, jnp.sum(got[places:].astype(F32), axis=1)

    own_ofs = jnp.sum(
        jnp.where((lax.iota(jnp.int32, groups) == group_index)[:, None], grid_ofs, 0), axis=0
    )
    positions = row_index * rows + lax.iota(jnp.int32, rows)
    begin = jnp.max(
        jnp.where(positions[:, None] >= own_ofs[None, :], own_ofs[None, :], 0), axis=1
    )
    begin = (begin - row_index * rows).reshape(1, rows)

    packed = jnp.stack(
        [
            gain_attention_in,
            shift_attention_in,
            gain_attention_out,
            shift_attention_out,
            gain_ffn_in,
            shift_ffn_in,
            gain_ffn_out,
            shift_ffn_out,
            bias_out,
            bias_down,
        ]
    )
    vectors = col_pieces(packed)
    rest = list(bits_of("dp"))[2:]
    orders_up = [head + rest for head in ORDERS_UP]
    orders_down = [head + rest for head in ORDERS_DOWN]
    orders_attention = [head + rest for head in ORDERS_ATTENTION]
    column = lax.axis_index("col").reshape(1)

    def scalars_for(orders):
        return jnp.concatenate([column, place_table(orders)])

    x_own = deal(layer_input)
    x_low_own = lax.ppermute(x_own, "row", [(0, 1)])
    g_own = deal(cotangent)
    x = col_pieces(x_own)
    scalars_attention = scalars_for(orders_attention)
    h1, h1_blocks = row_call(
        norm_in_kernel, scalars_attention, vectors, [x], [(D, LOW), (D, LOW)]
    )
    queries = ((dot(h1, w_query) + bias_query) * (1.0 / math.sqrt(DH))).astype(LOW)
    keys = dot(h1, w_key).astype(LOW)
    values = (dot(h1, w_value) + bias_value).astype(LOW)

    width = queries.shape[1]
    x_low = col_pieces(after(x_low_own, queries))
    (h_low,) = row_call(norm_in_kernel, column, vectors, [x_low], [(D, LOW)])
    keys_low = dot(h_low, w_key).astype(LOW)
    values_low = (dot(h_low, w_value) + bias_value).astype(LOW)
    attended, log_total = attend_call(
        forward_kernel,
        rows,
        width,
        ["post"] + ["rows"] * 5,
        [("rows", LOW), ("stat", F32)],
        2 * rows,
    )(begin.reshape(rows, 1), queries, keys_low, values_low, keys, values)

    branch = col_parts(dot(attended, w_out).astype(LOW))
    h2, h2_blocks, y_own = row_call(
        norm_mid_kernel,
        scalars_for(orders_up),
        vectors,
        [branch, x],
        [(D, LOW), (D, LOW), (local_width, F32)],
    )
    pre = dot(h2, w_up) + bias_up
    cube = math.sqrt(2.0 / math.pi)
    bend = jnp.tanh(cube * (pre + 0.044715 * pre * pre * pre))
    hidden = (0.5 * pre * (1.0 + bend)).astype(LOW)
    slope = 0.5 * (1.0 + bend) + 0.5 * pre * (1.0 - bend * bend) * cube * (
        1.0 + 3.0 * 0.044715 * pre * pre
    )
    slope = slope.astype(LOW)
    ffn = col_parts(dot(hidden, w_down).astype(LOW))
    g = col_pieces(g_own)
    d_ffn, d_ffn_blocks, result, sums4 = row_call(
        norm_out_kernel,
        scalars_for(orders_down),
        vectors,
        [ffn, g, [y_own]],
        [(D, LOW), (D, LOW), (local_width, LOW), local_width],
    )

    ff = hidden.shape[1]
    down = GradSum("down", [(d_ffn_blocks, hidden)], orders_down, [(0, ff, True)])
    tip = down.begin()
    d_pre = dot_back(after(d_ffn, tip), w_down) * slope.astype(F32)
    d_pre = d_pre.astype(LOW)
    up = GradSum("up", [(h2_blocks, d_pre)], orders_up, [(0, ff, False)])
    tip = up.begin()
    d_h2 = col_parts(dot_back(after(d_pre, tip), w_up).astype(LOW))
    kept_down = down.keep(d_h2[0])
    d_branch, d_branch_blocks, d_middle, sums3 = row_call(
        norm_back_kernel,
        scalars_attention,
        vectors,
        [d_h2, g, x, branch],
        [(D, LOW), (D, LOW), (local_width, F32), local_width],
    )
    tip = down.advance(d_branch, kept_down)
    d_attended = dot_back(after(d_branch, tip), w_out).astype(LOW)
    back_ins = ["line"] + ["rows"] * 5 + ["stat"]
    dq_low, dkv_low = attend_call(
        functools.partial(backward_kernel, False),
        rows,
        width,
        back_ins,
        [("cols", F32), ("two", LOW)],
        rows,
    )(begin, queries, keys_low, values_low, d_attended, attended, log_total)
    dkv_back = lax.ppermute(dkv_low, "row", [(1, 0)])
    tip = up.keep(dq_low)
    tip = down.advance(tip)
    d_query, dkv_own = attend_call(
        functools.partial(backward_kernel, True),
        rows,
        width,
        back_ins + ["cols"],
        [("rows", LOW), ("two", LOW)],
        rows,
    )(begin, queries, keys, values, after(d_attended, tip), attended, log_total, dq_low)

    tip = up.advance(d_query)
    tip = down.advance(tip)
    dkv = dkv_own.astype(F32) + after(dkv_back, tip).astype(F32)
    d_key, d_value = dkv[0].astype(LOW), dkv[1].astype(LOW)
    attention = GradSum(
        "attention",
        [
            (h1_blocks, d_query),
            (h1_blocks, d_key),
            (h1_blocks, d_value),
            (d_branch_blocks, attended),
        ],
        orders_attention,
        [(k * width, (k + 1) * width, k == 3) for k in range(4)],
    )
    tip = attention.begin()
    output = undo_deal(after(result, tip))
    d_h1 = dot_back(after(d_query, tip), w_query) + dot_back(d_key, w_key)
    d_h1 = col_parts((d_h1 + dot_back(d_value, w_value)).astype(LOW))
    kept = attention.keep(d_h1[0])
    in_grad, sums1 = row_call(
        norm_last_kernel,
        column,
        vectors,
        [d_h1, x, [d_middle]],
        [(local_width, LOW), local_width],
    )
    tip = in_grad
    ready = [in_grad, kept]

    def summed(values):
        return jnp.sum(values.astype(F32), axis=0).reshape(-1, local_width)

    small_rows = [sums1[:2], sums3[:5], sums4[:3]]
    small_rows = small_rows + [summed(d_query), summed(d_value), summed(d_pre)]
    packed_sums = jnp.concatenate(small_rows, axis=0)
    chains = {"W": down, "U": up, "A": attention}
    for name in TAIL:
        if name == "x":
            input_grad, smalls = undo_deal(after(in_grad, tip), packed_sums)
        else:
            tip = chains[name].advance(tip, *ready)
            ready = []
    for chain in chains.values():
        while chain.results is None:
            tip = chain.advance(tip)

    grad_query, grad_key, grad_value, grad_out = attention.results
    (grad_up,) = up.results
    (grad_down,) = down.results
    return (
        output,
        input_grad,
        grad_query,
        grad_key,
        grad_value,
        smalls[10],
        smalls[11],
        grad_out,
        smalls[6],
        grad_up,
        smalls[12:].reshape(-1),
        grad_down,
        smalls[9],
        smalls[0],
        smalls[1],
        smalls[4],
        smalls[5],
        smalls[2],
        smalls[3],
        smalls[7],
        smalls[8],
    )


def solution(mesh):
    shards = P(None, ("dp", "row"), "col")
    by_col = P("col")
    vectors = (by_col,) * 8
    return jax.shard_map(
        body,
        mesh=mesh,
        in_specs=(
            shards,
            shards,
            P(),
            P(),
            P(None, "col"),
            P(None, "col"),
            P(None, "col"),
            by_col,
            by_col,
            P("col", None),
            by_col,
            P(None, "col"),
            by_col,
            P("col", None),
            by_col,
            *vectors,
        ),
        out_specs=(
            shards,
            shards,
            P("row", "col"),
            P("row", "col"),
            P("row", "col"),
            by_col,
            by_col,
            P("col", "row"),
            by_col,
            P("row", "col"),
            by_col,
            P("col", "row"),
            by_col,
            *vectors,
        ),
        check_vma=False,
    )
```

```python
import functools
import math

import jax
import jax.numpy as jnp
from jax import lax
from jax.experimental import pallas as pl
from jax.experimental.pallas import tpu as pltpu
from jax.sharding import PartitionSpec as P

D = 1024
DH = 64
PAIR = 2 * DH
EPSILON = 1e-05
MASKED = -1e30
LOW = jnp.bfloat16
F32 = jnp.float32
BRIEF = pl.CostEstimate(flops=1, bytes_accessed=1, transcendentals=0)


def swap(values, axis, bit):
    size = lax.axis_size(axis)
    return lax.ppermute(values, axis, [(i, i ^ (1 << bit)) for i in range(size)])


def bits_of(axis):
    return range(lax.axis_size(axis).bit_length() - 1)


def bit_at(phase):
    if phase == ROW:
        return lax.axis_index("row")
    return (lax.axis_index("dp") >> phase) & 1


ROW = "row"


def swap_phase(values, phases):
    sizes = [lax.axis_size(axis) for axis in ("dp", "row", "col")]
    pairs = []
    for dp in range(sizes[0]):
        for row in range(sizes[1]):
            for col in range(sizes[2]):
                phase = phases[col % 2]
                there = (dp, row ^ 1) if phase == ROW else (dp ^ (1 << phase), row)
                pairs.append(
                    (
                        (dp * sizes[1] + row) * sizes[2] + col,
                        (there[0] * sizes[1] + there[1]) * sizes[2] + col,
                    )
                )
    return lax.ppermute(values, ("dp", "row", "col"), pairs)


def per_core(even, odd):
    return jnp.where(lax.axis_index("col") % 2 == 0, even, odd)


def col_pieces(own):
    pieces = [own]
    for bit in bits_of("col"):
        pieces = pieces + [swap(piece, "col", bit) for piece in pieces]
    return pieces


def col_parts(partial):
    bits = list(bits_of("col"))
    for bit in bits[:-1]:
        partial = (partial.astype(F32) + swap(partial, "col", bit).astype(F32)).astype(LOW)
    return [partial, swap(partial, "col", bits[-1])]


def after(values, *earlier):
    return lax.optimization_barrier((values, *earlier))[0]


def dot(left, right):
    return jnp.dot(left, right, preferred_element_type=F32)


def dot_back(left, right):
    return lax.dot_general(left, right, (((1,), (1,)), ((), ())), preferred_element_type=F32)


def dot_tokens(left, right):
    return lax.dot_general(left, right, (((0,), (0,)), ((), ())), preferred_element_type=F32)


BLOCKS = 8
GAIN1, SHIFT1, GAIN2, SHIFT2, GAIN3, SHIFT3, GAIN4, SHIFT4, BIAS_OUT, BIAS_DOWN = range(10)


def total(parts):
    return functools.reduce(lambda a, b: a + b, parts)


def row_mean(pieces):
    return total([jnp.sum(p, axis=1, keepdims=True) for p in pieces]) * (1.0 / D)


def normalize(pieces):
    average = row_mean(pieces)
    inverse = lax.rsqrt(row_mean([p * p for p in pieces]) - average * average + EPSILON)
    return [(p - average) * inverse for p in pieces], inverse


def normalize_back(grads, scaled, inverse, gains):
    pushed = [e * g for e, g in zip(grads, gains)]
    mean_push = row_mean(pushed)
    mean_dot = row_mean([f * n for f, n in zip(pushed, scaled)])
    return [inverse * (f - mean_push - n * mean_dot) for f, n in zip(pushed, scaled)]


def span(column, k, width):
    return pl.ds(pl.multiple_of((column ^ k) * width, 128), width)


def load_pieces(refs):
    return [ref[...].astype(F32) for ref in refs]


def load_ordered(refs, column, count):
    width = refs[0].shape[1] // count
    return [
        total([ref[:, span(column, k, width)].astype(F32) for ref in refs]) for k in range(count)
    ]


def store_ordered(ref, column, pieces):
    width = ref.shape[1] // len(pieces)
    for k, piece in enumerate(pieces):
        ref[:, span(column, k, width)] = piece


def store_blocks(ref, table, column, pieces):
    size = ref.shape[1] // BLOCKS
    width = ref.shape[1] // len(pieces)
    for k, piece in enumerate(pieces):
        first = (column ^ k) * (width // size)
        for j in range(width // size):
            place = pl.multiple_of(table[first + j] * size, 128)
            ref[:, pl.ds(place, size)] = piece[:, j * size : (j + 1) * size]


def column_sums(ref, rows):
    for at, values in enumerate(rows):
        ref[at : at + 1, :] += jnp.sum(values, axis=0, keepdims=True)


def vector_of(vector_refs, index):
    return [ref[index : index + 1, :] for ref in vector_refs]


def plus(pieces, vectors):
    return [p + v for p, v in zip(pieces, vectors)]


def affine(scaled, gains, shifts):
    return [s * g + b for s, g, b in zip(scaled, gains, shifts)]


def norm_in_kernel(scalars, vec, x, h, h_blocks=None):
    scaled, _ = normalize(load_pieces(x))
    out = affine(scaled, vector_of(vec, GAIN1), vector_of(vec, SHIFT1))
    out = [p.astype(LOW) for p in out]
    store_ordered(h[0], scalars[0], out)
    if h_blocks is not None:
        store_blocks(h_blocks[0], scalars.table(), scalars[0], out)


def middle_of(column, vec, branch, x):
    held = plus(load_ordered(branch, column, len(x)), vector_of(vec, BIAS_OUT))
    scaled, inverse = normalize(held)
    out = affine(scaled, vector_of(vec, GAIN2), vector_of(vec, SHIFT2))
    return scaled, inverse, [a + b for a, b in zip(load_pieces(x), out)]


def norm_mid_kernel(scalars, vec, branch, x, h, h_blocks, y):
    column = scalars[0]
    _, _, middle = middle_of(column, vec, branch, x)
    y[0][...] = middle[0]
    scaled, _ = normalize(middle)
    out = affine(scaled, vector_of(vec, GAIN3), vector_of(vec, SHIFT3))
    out = [p.astype(LOW) for p in out]
    store_ordered(h[0], column, out)
    store_blocks(h_blocks[0], scalars.table(), column, out)


def norm_out_kernel(scalars, vec, ffn, g, y, d_ffn, d_blocks, result, sums):
    column = scalars[0]
    held = plus(load_ordered(ffn, column, len(g)), vector_of(vec, BIAS_DOWN))
    scaled, inverse = normalize(held)
    gains = vector_of(vec, GAIN4)
    out = y[0][...] + scaled[0] * gains[0] + vector_of(vec, SHIFT4)[0]
    result[0][...] = out.astype(LOW)
    grads = load_pieces(g)
    back = [p.astype(LOW) for p in normalize_back(grads, scaled, inverse, gains)]
    store_ordered(d_ffn[0], column, back)
    store_blocks(d_blocks[0], scalars.table(), column, back)
    column_sums(sums[0], [grads[0] * scaled[0], grads[0], back[0].astype(F32)])


def norm_back_kernel(scalars, vec, d_h2, g, x, branch, d_branch, d_blocks, d_middle, sums):
    column = scalars[0]
    scaled2, inverse2, middle = middle_of(column, vec, branch, x)
    scaled3, inverse3 = normalize(middle)
    grads3 = load_ordered(d_h2, column, len(x))
    back3 = normalize_back(grads3, scaled3, inverse3, vector_of(vec, GAIN3))
    grads2 = [a + b for a, b in zip(load_pieces(g), back3)]
    d_middle[0][...] = grads2[0]
    back2 = normalize_back(grads2, scaled2, inverse2, vector_of(vec, GAIN2))
    back2 = [p.astype(LOW) for p in back2]
    store_ordered(d_branch[0], column, back2)
    store_blocks(d_blocks[0], scalars.table(), column, back2)
    column_sums(
        sums[0],
        [
            grads3[0] * scaled3[0],
            grads3[0],
            grads2[0] * scaled2[0],
            grads2[0],
            back2[0].astype(F32),
        ],
    )


def norm_last_kernel(scalars, vec, d_h1, x, d_middle, out, sums):
    column = scalars[0]
    scaled, inverse = normalize(load_pieces(x))
    grads = load_ordered(d_h1, column, len(x))
    back = normalize_back(grads, scaled, inverse, vector_of(vec, GAIN1))
    out[0][...] = (d_middle[0][...] + back[0]).astype(LOW)
    column_sums(sums[0], [grads[0] * scaled[0], grads[0]])


class Scalars:
    def __init__(self, ref, which):
        self.ref, self.which = ref, which

    def __getitem__(self, index):
        return self.ref[index]

    def table(self):
        return Table(self.ref, 1 + BLOCKS * self.which)


class Table:
    def __init__(self, ref, start):
        self.ref, self.start = ref, start

    def __getitem__(self, index):
        return self.ref[index + self.start]


def row_call(kernel, scalars, vectors, ins, outs, which=0):
    rows = ins[0][0].shape[0]
    step = min(256, rows)
    counts = [len(vectors)] + [len(group) for group in ins] + [1] * len(outs)

    chunk = min(128, step)

    def whole(scalar_ref, *refs):
        @pl.when(pl.program_id(0) == 0)
        def _():
            for ref, out in zip(refs[len(refs) - len(outs) :], outs):
                if not isinstance(out, tuple):
                    ref[...] = jnp.zeros(ref.shape, F32)

        def part(at, carry):
            groups = []
            used = 0
            here = pl.ds(pl.multiple_of(at * chunk, chunk), chunk)
            for count in counts:
                group = refs[used : used + count]
                used += count
                groups.append([r.at[here, :] if r.shape[0] == step else r for r in group])
            kernel(Scalars(scalar_ref, which), *groups)
            return carry

        lax.fori_loop(0, step // chunk, part, 0)

    def block(width):
        return pl.BlockSpec((step, width), lambda i, c: (i, 0))

    flat = [a for group in ins for a in group]
    shapes = []
    specs = []
    for out in outs:
        if isinstance(out, tuple):
            shapes.append(jax.ShapeDtypeStruct((rows, out[0]), out[1]))
            specs.append(block(out[0]))
        else:
            shapes.append(jax.ShapeDtypeStruct((8, out), F32))
            specs.append(pl.BlockSpec((8, out), lambda i, c: (0, 0)))
    return pl.pallas_call(
        whole,
        grid_spec=pltpu.PrefetchScalarGridSpec(
            num_scalar_prefetch=1,
            grid=(rows // step,),
            in_specs=[pl.BlockSpec(v.shape, lambda i, c: (0, 0)) for v in vectors]
            + [block(a.shape[1]) for a in flat],
            out_specs=specs,
        ),
        out_shape=shapes,
        cost_estimate=BRIEF,
    )(scalars, *vectors, *flat)


def route_tables(lengths, dealing, groups, half_rows, shard_count, row_count):
    seq_count = lengths.shape[0]
    per_group = seq_count // groups
    seq_ids = lax.iota(jnp.int32, seq_count)
    units = lengths // shard_count
    starts = jnp.sum(jnp.where(seq_ids[None, :] < seq_ids[:, None], units[None, :], 0), axis=1)
    chosen = dealing[:, None] == seq_ids[None, :]
    slot_len = jnp.sum(jnp.where(chosen, units[None, :], 0), axis=1)
    slot_in = jnp.sum(jnp.where(chosen, starts[None, :], 0), axis=1)
    earlier = (seq_ids[None, :] < seq_ids[:, None]) & (
        seq_ids[None, :] // per_group == seq_ids[:, None] // per_group
    )
    slot_ofs = jnp.sum(jnp.where(earlier, slot_len[None, :], 0), axis=1)
    grid_ofs = slot_ofs.reshape(groups, per_group)
    grid_anchor = (slot_in - slot_ofs).reshape(groups, per_group)
    places = half_rows // shard_count
    unit = (
        lax.broadcasted_iota(jnp.int32, (places, groups, row_count), 2) * places
        + lax.broadcasted_iota(jnp.int32, (places, groups, row_count), 0)
    )
    anchor = jnp.broadcast_to(grid_anchor[None, :, :1], unit.shape)
    for k in range(1, per_group):
        anchor = jnp.where(
            unit >= grid_ofs[None, :, k : k + 1], grid_anchor[None, :, k : k + 1], anchor
        )
    return (anchor + unit).reshape(half_rows), grid_ofs * shard_count


def head_lanes(shape, dim, head):
    lane = lax.broadcasted_iota(jnp.int32, shape, dim)
    return (lane >= head * DH) & (lane < (head + 1) * DH)


def masked_head(values, dim, head):
    return jnp.where(head_lanes(values.shape, dim, head), values, jnp.zeros_like(values))


def forward_kernel(
    begin_ref, q_ref, k_low_ref, v_low_ref, k_ref, v_ref, out_ref, log_ref, bias_ref
):
    rows = q_ref.shape[0]

    @pl.when(pl.program_id(0) == 0)
    def _():
        key_pos = lax.broadcasted_iota(jnp.int32, (rows, 2 * rows), 1) - rows
        query_pos = lax.broadcasted_iota(jnp.int32, (rows, 2 * rows), 0)
        allowed = (key_pos <= query_pos) & (key_pos >= begin_ref[...])
        bias_ref[...] = jnp.where(allowed, 0.0, MASKED)

    step = min(256, rows)
    first = head_lanes((step, PAIR), 1, 0)
    for at in range(0, rows, step):
        here = slice(at, at + step)
        keys = at + step
        parts = []
        logs = []
        for head in range(2):
            query = masked_head(q_ref[here, :], 1, head)
            scores = jnp.concatenate(
                [dot_back(query, k_low_ref[...]), dot_back(query, k_ref[:keys, :])], axis=1
            )
            scores = scores + bias_ref[here, : rows + keys]
            top = jnp.max(scores, axis=1, keepdims=True)
            weights = jnp.exp(scores - top)
            norm = jnp.sum(weights, axis=1, keepdims=True)
            weights = weights.astype(LOW)
            part_low = dot(weights[:, :rows], v_low_ref[...])
            parts.append((part_low + dot(weights[:, rows:], v_ref[:keys, :])) / norm)
            logs.append(top + jnp.log(norm))
        out_ref[here, :] = jnp.where(first, parts[0], parts[1]).astype(LOW)
        turned = jnp.where(first, logs[0], logs[1]).T
        log_ref[0, 0:1, here] = turned[:1]
        log_ref[0, 1:2, here] = turned[DH : DH + 1]


def backward_kernel(own, begin_ref, q_ref, k_ref, v_ref, g_ref, out_ref, log_ref, *rest):
    if own:
        dq_low_ref, dq_ref, dkv_ref, bias_ref = rest
    else:
        dq_ref, dkv_ref, bias_ref = rest
    rows = k_ref.shape[0]

    @pl.when(pl.program_id(0) == 0)
    def _():
        key_pos = lax.broadcasted_iota(jnp.int32, (rows, rows), 0) + (0 if own else -rows)
        query_pos = lax.broadcasted_iota(jnp.int32, (rows, rows), 1)
        allowed = (key_pos <= query_pos) & (key_pos >= begin_ref[...])
        bias_ref[...] = jnp.where(allowed, 0.0, MASKED)

    dots = (g_ref[...].astype(F32) * out_ref[...].astype(F32)).T
    keys_t = k_ref[...].T
    dk = []
    dv = []
    step = min(256, rows) if own else rows
    for at in range(0, rows, step):
        here = slice(at, at + step)
        keys = at + step if own else rows
        dq = []
        new_dk = []
        new_dv = []
        for head in range(2):
            lanes = slice(head * DH, (head + 1) * DH)
            query = masked_head(q_ref[here, :], 1, head)
            grad = masked_head(g_ref[here, :], 1, head)
            scores = dot_back(k_ref[:keys, :], query) + bias_ref[:keys, here]
            prob = jnp.exp(scores - log_ref[0, head : head + 1, here])
            grad_prob = dot_back(v_ref[:keys, :], grad)
            row_dot = jnp.sum(dots[lanes, here], axis=0, keepdims=True)
            grad_score = (prob * (grad_prob - row_dot)).astype(LOW)
            dq.append(dot(keys_t[lanes, :keys], grad_score))
            new_dk.append(dot(grad_score, query))
            new_dv.append(dot(prob.astype(LOW), grad))
        dk.append(total(new_dk))
        dv.append(total(new_dv))
        if own:
            dq = jnp.concatenate(dq, axis=0) + dq_low_ref[:, here]
            dq_ref[here, :] = (dq * (1.0 / math.sqrt(DH))).T.astype(LOW)
        else:
            dq_ref[:DH, here] = dq[0]
            dq_ref[DH:, here] = dq[1]
    for at, parts in enumerate((dk, dv)):
        ends = sorted({p.shape[0] for p in parts})
        for begin, end in zip([0] + ends[:-1], ends):
            pieces = [p[begin:end] for p in parts if p.shape[0] >= end]
            dkv_ref[at, begin:end, :] = total(pieces).astype(LOW)


def pair_spec(rows):
    return pl.BlockSpec((rows, PAIR), lambda i: (0, i))


def pair_t_spec(rows):
    return pl.BlockSpec((PAIR, rows), lambda i: (i, 0))


def stat_spec(rows):
    return pl.BlockSpec((1, 2, rows), lambda i: (i, 0, 0))


def attend_call(kernel, rows, width, ins, outs, keys):
    pairs = width // PAIR
    shapes = {
        "rows": (pair_spec(rows), (rows, width)),
        "cols": (pair_t_spec(rows), (width, rows)),
        "stat": (stat_spec(rows), (pairs, 2, rows)),
        "two": (pl.BlockSpec((2, rows, PAIR), lambda i: (0, 0, i)), (2, rows, width)),
        "line": (pl.BlockSpec((1, rows), lambda i: (0, 0)), (1, rows)),
        "post": (pl.BlockSpec((rows, 1), lambda i: (0, 0)), (rows, 1)),
    }
    return pl.pallas_call(
        kernel,
        grid=(pairs,),
        in_specs=[shapes[kind][0] for kind in ins],
        out_specs=[shapes[kind][0] for kind, _ in outs],
        out_shape=[jax.ShapeDtypeStruct(shapes[kind][1], dtype) for kind, dtype in outs],
        scratch_shapes=[pltpu.VMEM((rows, keys), F32)],
        cost_estimate=BRIEF,
    )


def pick(values, index):
    size = values.shape[0] // 2
    return lax.dynamic_slice_in_dim(values, index * size, size, 0, allow_negative_indices=False)


def place_table(orders):
    def places(order):
        head = order[:3]
        spare = [phase for phase in head if phase != ROW]
        block = lax.iota(jnp.int32, BLOCKS)
        natural = {ROW: (block >> 2) & 1, spare[0]: (block >> 1) & 1, spare[1]: block & 1}
        place = jnp.zeros((BLOCKS,), jnp.int32)
        for phase in head:
            place = place * 2 + (natural[phase] ^ bit_at(phase))
        return place

    return per_core(places(orders[0]), places(orders[1]))


class GradSum:
    def __init__(self, name, terms, orders, outs):
        self.name, self.terms, self.outs = name, terms, outs
        self.phases = list(zip(*orders))
        dp_phases = [[p for p in order if p != ROW] for order in orders]
        self.first, self.second = [tuple(order[i] for order in dp_phases) for i in range(2)]
        self.back = list(zip(*[list(reversed(order[:-1])) for order in dp_phases]))
        self.at = 0
        self.results = None

    def product(self, index):
        cut = []
        for left, right in self.terms:
            size = left.shape[1] // 2
            half = lax.slice_in_dim(left, index * size, (index + 1) * size, axis=1)
            cut.append(dot_tokens(half, right).astype(LOW))
        return cut[0] if len(cut) == 1 else jnp.concatenate(cut, axis=1)

    def begin(self):
        with jax.named_scope(self.name + "_phase0"):
            sent = self.product(1)
            self.got = swap_phase(sent, self.phases[0])
        return sent

    def keep(self, *earlier):
        if earlier:
            self.terms = [(left, after(right, *earlier)) for left, right in self.terms]
        self.held = [self.product(0)]
        return self.held[0]

    def advance(self, *earlier):
        self.at += 1
        with jax.named_scope(f"{self.name}_phase{self.at}"):
            return self.step(after(self.got, *earlier))

    def rows_sum(self, begin, end):
        return total([a[begin:end].astype(F32) for a in self.held]).astype(LOW)

    def step(self, got):
        spot = self.at - len(self.phases)
        rows = got.shape[0]
        if spot < 0:
            self.held.append(got)
            phases = self.phases[self.at]
            if spot == -1:
                sent = self.rows_sum(0, rows)
                self.held = [sent]
            elif self.at < 3:
                sent = self.rows_sum(rows // 2, rows)
            else:
                mine = per_core(bit_at(phases[0]), bit_at(phases[1]))
                held = self.rows_sum(0, rows)
                sent = pick(held, 1 - mine)
                self.held = [pick(held, mine)]
        else:
            kept = self.held[0]
            if spot == 0:
                low = (kept.astype(F32) + got.astype(F32)).astype(LOW)
            elif spot <= len(self.back) - 2:
                phases = self.back[spot - 1]
                flip = per_core(bit_at(phases[0]), bit_at(phases[1])) == 1
                low = jnp.concatenate(
                    [jnp.where(flip, got, kept), jnp.where(flip, kept, got)], axis=0
                )
            elif spot == len(self.back) - 1:
                low = jnp.concatenate([kept, got], axis=0)
                self.partial = self.spread(low, 0)
            else:
                self.results = self.spread(got, 1, self.partial)
                return self.results[0]
            phases = self.back[spot]
            sent = low
            self.held = [low]
        self.got = swap_phase(sent, phases)
        return sent

    def spread(self, half, index, held=None):
        bits = per_core(*[bit_at(self.first[i]) * 2 + bit_at(self.second[i]) for i in range(2)])
        places = (2 * index + lax.iota(jnp.int32, 2)) ^ bits
        size = half.shape[0] // 2
        rows = 4 * size
        width = half.shape[1]
        held = list(held or [])

        def kernel(place_ref, half_ref, *refs):
            values = half_ref[...].astype(F32)
            for ref, (begin, end, turned) in zip(refs[len(held) :], self.outs):
                ref[...] = values[:, begin:end].T if turned else values[:, begin:end]

        shapes = []
        specs = []
        for begin, end, turned in self.outs:
            if turned:
                shapes.append(jax.ShapeDtypeStruct((end - begin, rows), F32))
                specs.append(pl.BlockSpec((end - begin, size), lambda i, t: (0, t[i])))
            else:
                shapes.append(jax.ShapeDtypeStruct((rows, end - begin), F32))
                specs.append(pl.BlockSpec((size, end - begin), lambda i, t: (t[i], 0)))
        return pl.pallas_call(
            kernel,
            grid_spec=pltpu.PrefetchScalarGridSpec(
                num_scalar_prefetch=1,
                grid=(2,),
                in_specs=[pl.BlockSpec((size, width), lambda i, t: (i, 0))]
                + [pl.BlockSpec(memory_space=pl.ANY)] * len(held),
                out_specs=specs,
            ),
            out_shape=shapes,
            input_output_aliases={2 + k: k for k in range(len(held))},
            cost_estimate=BRIEF,
        )(places, half, *held)


ORDERS_DOWN = [[ROW, 1, 0], [0, ROW, 1]]
ORDERS_UP = [[1, 0, ROW], [0, 1, ROW]]
ORDERS_ATTENTION = [[ROW, 0, 1], [1, ROW, 0]]
TAIL = "UWAxAUWAUWUAAUA"


def body(
    layer_input,
    cotangent,
    lengths,
    dealing,
    w_query,
    w_key,
    w_value,
    bias_query,
    bias_value,
    w_out,
    bias_out,
    w_up,
    bias_up,
    w_down,
    bias_down,
    gain_attention_in,
    shift_attention_in,
    gain_attention_out,
    shift_attention_out,
    gain_ffn_in,
    shift_ffn_in,
    gain_ffn_out,
    shift_ffn_out,
):
    row_count = lax.axis_size("row")
    groups = lax.axis_size("dp")
    shard_count = groups * row_count
    row_index = lax.axis_index("row")
    group_index = lax.axis_index("dp")
    rows = layer_input.shape[0]
    local_width = layer_input.shape[2]
    places = rows // shard_count
    group_rows = rows * row_count

    routes, grid_ofs = route_tables(lengths, dealing, groups, rows, shard_count, row_count)
    place = (routes[:, None] == lax.iota(jnp.int32, rows)[None, :]).astype(LOW)

    def deal(values):
        sent = dot(place, values.reshape(rows, local_width)).astype(LOW)
        sent = sent.reshape(places, shard_count, local_width)
        got = lax.all_to_all(sent, ("dp", "row"), split_axis=1, concat_axis=1, tiled=True)
        return got.reshape(rows, local_width)

    def undo_deal(values, sums=None):
        sent = values.reshape(places, shard_count, local_width)
        if sums is not None:
            copies = (sums.shape[0],) + sent.shape[1:]
            spread = jnp.broadcast_to(sums.astype(LOW)[:, None, :], copies)
            sent = jnp.concatenate([sent, spread], axis=0)
        got = lax.all_to_all(sent, ("dp", "row"), split_axis=1, concat_axis=1, tiled=True)
        back = dot_tokens(place, got[:places].reshape(rows, local_width)).astype(LOW)
        back = back.reshape(rows, 1, local_width)
        if sums is None:
            return back
        return back, jnp.sum(got[places:].astype(F32), axis=1)

    own_ofs = jnp.sum(
        jnp.where((lax.iota(jnp.int32, groups) == group_index)[:, None], grid_ofs, 0), axis=0
    )
    positions = row_index * rows + lax.iota(jnp.int32, rows)
    begin = jnp.max(
        jnp.where(positions[:, None] >= own_ofs[None, :], own_ofs[None, :], 0), axis=1
    )
    begin = (begin - row_index * rows).reshape(1, rows)

    packed = jnp.stack(
        [
            gain_attention_in,
            shift_attention_in,
            gain_attention_out,
            shift_attention_out,
            gain_ffn_in,
            shift_ffn_in,
            gain_ffn_out,
            shift_ffn_out,
            bias_out,
            bias_down,
        ]
    )
    vectors = col_pieces(packed)
    rest = list(bits_of("dp"))[2:]
    orders_up = [head + rest for head in ORDERS_UP]
    orders_down = [head + rest for head in ORDERS_DOWN]
    orders_attention = [head + rest for head in ORDERS_ATTENTION]
    column = lax.axis_index("col").reshape(1)

    tables = [place_table(o) for o in (orders_attention, orders_up, orders_down)]
    scalars = jnp.concatenate([column] + tables)

    x_own = deal(layer_input)
    x_low_own = lax.ppermute(x_own, "row", [(0, 1)])
    g_own = deal(cotangent)
    x = col_pieces(x_own)
    h1, h1_blocks = row_call(
        norm_in_kernel, scalars, vectors, [x], [(D, LOW), (D, LOW)]
    )
    queries = ((dot(h1, w_query) + bias_query) * (1.0 / math.sqrt(DH))).astype(LOW)
    keys = dot(h1, w_key).astype(LOW)
    values = (dot(h1, w_value) + bias_value).astype(LOW)

    width = queries.shape[1]
    x_low = col_pieces(after(x_low_own, queries))
    (h_low,) = row_call(norm_in_kernel, scalars, vectors, [x_low], [(D, LOW)])
    keys_low = dot(h_low, w_key).astype(LOW)
    values_low = (dot(h_low, w_value) + bias_value).astype(LOW)
    attended, log_total = attend_call(
        forward_kernel,
        rows,
        width,
        ["post"] + ["rows"] * 5,
        [("rows", LOW), ("stat", F32)],
        2 * rows,
    )(begin.reshape(rows, 1), queries, keys_low, values_low, keys, values)

    branch = col_parts(dot(attended, w_out).astype(LOW))
    h2, h2_blocks, y_own = row_call(
        norm_mid_kernel,
        scalars,
        vectors,
        [branch, x],
        [(D, LOW), (D, LOW), (local_width, F32)],
        1,
    )
    pre = dot(h2, w_up) + bias_up
    cube = math.sqrt(2.0 / math.pi)
    bend = jnp.tanh(cube * (pre + 0.044715 * pre * pre * pre))
    hidden = (0.5 * pre * (1.0 + bend)).astype(LOW)
    slope = 0.5 * (1.0 + bend) + 0.5 * pre * (1.0 - bend * bend) * cube * (
        1.0 + 3.0 * 0.044715 * pre * pre
    )
    slope = slope.astype(LOW)
    ffn = col_parts(dot(hidden, w_down).astype(LOW))
    g = col_pieces(g_own)
    d_ffn, d_ffn_blocks, result, sums4 = row_call(
        norm_out_kernel,
        scalars,
        vectors,
        [ffn, g, [y_own]],
        [(D, LOW), (D, LOW), (local_width, LOW), local_width],
        2,
    )

    ff = hidden.shape[1]
    down = GradSum("down", [(d_ffn_blocks, hidden)], orders_down, [(0, ff, True)])
    tip = down.begin()
    d_pre = dot_back(after(d_ffn, tip), w_down) * slope.astype(F32)
    d_pre = d_pre.astype(LOW)
    up = GradSum("up", [(h2_blocks, d_pre)], orders_up, [(0, ff, False)])
    tip = up.begin()
    d_h2 = col_parts(dot_back(after(d_pre, tip), w_up).astype(LOW))
    kept_down = down.keep(d_h2[0])
    d_branch, d_branch_blocks, d_middle, sums3 = row_call(
        norm_back_kernel,
        scalars,
        vectors,
        [d_h2, g, x, branch],
        [(D, LOW), (D, LOW), (local_width, F32), local_width],
    )
    tip = down.advance(d_branch, kept_down)
    d_attended = dot_back(after(d_branch, tip), w_out).astype(LOW)
    back_ins = ["line"] + ["rows"] * 5 + ["stat"]
    dq_low, dkv_low = attend_call(
        functools.partial(backward_kernel, False),
        rows,
        width,
        back_ins,
        [("cols", F32), ("two", LOW)],
        rows,
    )(begin, queries, keys_low, values_low, d_attended, attended, log_total)
    dkv_back = lax.ppermute(dkv_low, "row", [(1, 0)])
    tip = up.keep(dq_low)
    tip = down.advance(tip)
    d_query, dkv_own = attend_call(
        functools.partial(backward_kernel, True),
        rows,
        width,
        back_ins + ["cols"],
        [("rows", LOW), ("two", LOW)],
        rows,
    )(begin, queries, keys, values, after(d_attended, tip), attended, log_total, dq_low)

    tip = up.advance(d_query)
    tip = down.advance(tip)
    dkv = dkv_own.astype(F32) + after(dkv_back, tip).astype(F32)
    d_key, d_value = dkv[0].astype(LOW), dkv[1].astype(LOW)
    attention = GradSum(
        "attention",
        [
            (h1_blocks, d_query),
            (h1_blocks, d_key),
            (h1_blocks, d_value),
            (d_branch_blocks, attended),
        ],
        orders_attention,
        [(k * width, (k + 1) * width, k == 3) for k in range(4)],
    )
    tip = attention.begin()
    output = undo_deal(after(result, tip))
    d_h1 = dot_back(after(d_query, tip), w_query) + dot_back(d_key, w_key)
    d_h1 = col_parts((d_h1 + dot_back(d_value, w_value)).astype(LOW))
    kept = attention.keep(d_h1[0])
    in_grad, sums1 = row_call(
        norm_last_kernel,
        scalars,
        vectors,
        [d_h1, x, [d_middle]],
        [(local_width, LOW), local_width],
    )
    tip = in_grad
    ready = [in_grad, kept]

    def summed(values):
        return jnp.sum(values.astype(F32), axis=0).reshape(-1, local_width)

    small_rows = [sums1[:2], sums3[:5], sums4[:3]]
    small_rows = small_rows + [summed(d_query), summed(d_value), summed(d_pre)]
    packed_sums = jnp.concatenate(small_rows, axis=0)
    chains = {"W": down, "U": up, "A": attention}
    for name in TAIL:
        if name == "x":
            input_grad, smalls = undo_deal(after(in_grad, tip), packed_sums)
        else:
            tip = chains[name].advance(tip, *ready)
            ready = []
    for chain in chains.values():
        while chain.results is None:
            tip = chain.advance(tip)

    grad_query, grad_key, grad_value, grad_out = attention.results
    (grad_up,) = up.results
    (grad_down,) = down.results
    return (
        output,
        input_grad,
        grad_query,
        grad_key,
        grad_value,
        smalls[10],
        smalls[11],
        grad_out,
        smalls[6],
        grad_up,
        smalls[12:].reshape(-1),
        grad_down,
        smalls[9],
        smalls[0],
        smalls[1],
        smalls[4],
        smalls[5],
        smalls[2],
        smalls[3],
        smalls[7],
        smalls[8],
    )


def solution(mesh):
    shards = P(None, ("dp", "row"), "col")
    by_col = P("col")
    vectors = (by_col,) * 8
    return jax.shard_map(
        body,
        mesh=mesh,
        in_specs=(
            shards,
            shards,
            P(),
            P(),
            P(None, "col"),
            P(None, "col"),
            P(None, "col"),
            by_col,
            by_col,
            P("col", None),
            by_col,
            P(None, "col"),
            by_col,
            P("col", None),
            by_col,
            *vectors,
        ),
        out_specs=(
            shards,
            shards,
            P("row", "col"),
            P("row", "col"),
            P("row", "col"),
            by_col,
            by_col,
            P("col", "row"),
            by_col,
            P("row", "col"),
            by_col,
            P("col", "row"),
            by_col,
            *vectors,
        ),
        check_vma=False,
    )
```

```python
import functools
import math

import jax
import jax.numpy as jnp
from jax import lax
from jax.experimental import pallas as pl
from jax.experimental.pallas import tpu as pltpu
from jax.sharding import PartitionSpec as P

D = 1024
DH = 64
PAIR = 2 * DH
EPSILON = 1e-05
MASKED = -1e30
LOW = jnp.bfloat16
F32 = jnp.float32
BRIEF = pl.CostEstimate(flops=1, bytes_accessed=1, transcendentals=0)


def swap(values, axis, bit):
    size = lax.axis_size(axis)
    return lax.ppermute(values, axis, [(i, i ^ (1 << bit)) for i in range(size)])


def bits_of(axis):
    return range(lax.axis_size(axis).bit_length() - 1)


def bit_at(phase):
    if phase == ROW:
        return lax.axis_index("row")
    return (lax.axis_index("dp") >> phase) & 1


ROW = "row"


def swap_phase(values, phases):
    sizes = [lax.axis_size(axis) for axis in ("dp", "row", "col")]
    pairs = []
    for dp in range(sizes[0]):
        for row in range(sizes[1]):
            for col in range(sizes[2]):
                phase = phases[col % 2]
                there = (dp, row ^ 1) if phase == ROW else (dp ^ (1 << phase), row)
                pairs.append(
                    (
                        (dp * sizes[1] + row) * sizes[2] + col,
                        (there[0] * sizes[1] + there[1]) * sizes[2] + col,
                    )
                )
    return lax.ppermute(values, ("dp", "row", "col"), pairs)


def per_core(even, odd):
    return jnp.where(lax.axis_index("col") % 2 == 0, even, odd)


def col_pieces(own):
    pieces = [own]
    for bit in bits_of("col"):
        pieces = pieces + [swap(piece, "col", bit) for piece in pieces]
    return pieces


def col_parts(partial):
    bits = list(bits_of("col"))
    for bit in bits[:-1]:
        partial = (partial.astype(F32) + swap(partial, "col", bit).astype(F32)).astype(LOW)
    return [partial, swap(partial, "col", bits[-1])]


def after(values, *earlier):
    return lax.optimization_barrier((values, *earlier))[0]


def dot(left, right):
    return jnp.dot(left, right, preferred_element_type=F32)


def dot_back(left, right):
    return lax.dot_general(left, right, (((1,), (1,)), ((), ())), preferred_element_type=F32)


def dot_tokens(left, right):
    return lax.dot_general(left, right, (((0,), (0,)), ((), ())), preferred_element_type=F32)


BLOCKS = 8
GAIN1, SHIFT1, GAIN2, SHIFT2, GAIN3, SHIFT3, GAIN4, SHIFT4, BIAS_OUT, BIAS_DOWN = range(10)


def total(parts):
    return functools.reduce(lambda a, b: a + b, parts)


def row_mean(pieces):
    return total([jnp.sum(p, axis=1, keepdims=True) for p in pieces]) * (1.0 / D)


def normalize(pieces):
    average = row_mean(pieces)
    inverse = lax.rsqrt(row_mean([p * p for p in pieces]) - average * average + EPSILON)
    return [(p - average) * inverse for p in pieces], inverse


def normalize_back(grads, scaled, inverse, gains):
    pushed = [e * g for e, g in zip(grads, gains)]
    mean_push = row_mean(pushed)
    mean_dot = row_mean([f * n for f, n in zip(pushed, scaled)])
    return [inverse * (f - mean_push - n * mean_dot) for f, n in zip(pushed, scaled)]


def span(column, k, width):
    return pl.ds(pl.multiple_of((column ^ k) * width, 128), width)


def load_pieces(refs):
    return [ref[...].astype(F32) for ref in refs]


def load_ordered(refs, column, count):
    width = refs[0].shape[1] // count
    return [
        total([ref[:, span(column, k, width)].astype(F32) for ref in refs]) for k in range(count)
    ]


def store_ordered(ref, column, pieces):
    width = ref.shape[1] // len(pieces)
    for k, piece in enumerate(pieces):
        ref[:, span(column, k, width)] = piece


def store_blocks(ref, table, column, pieces):
    size = ref.shape[1] // BLOCKS
    width = ref.shape[1] // len(pieces)
    for k, piece in enumerate(pieces):
        first = (column ^ k) * (width // size)
        for j in range(width // size):
            place = pl.multiple_of(table[first + j] * size, 128)
            ref[:, pl.ds(place, size)] = piece[:, j * size : (j + 1) * size]


def column_sums(ref, rows):
    for at, values in enumerate(rows):
        ref[at : at + 1, :] += jnp.sum(values, axis=0, keepdims=True)


def vector_of(vector_refs, index):
    return [ref[index : index + 1, :] for ref in vector_refs]


def plus(pieces, vectors):
    return [p + v for p, v in zip(pieces, vectors)]


def affine(scaled, gains, shifts):
    return [s * g + b for s, g, b in zip(scaled, gains, shifts)]


def norm_in_kernel(scalars, vec, x, h, h_blocks=None):
    scaled, _ = normalize(load_pieces(x))
    out = affine(scaled, vector_of(vec, GAIN1), vector_of(vec, SHIFT1))
    out = [p.astype(LOW) for p in out]
    store_ordered(h[0], scalars[0], out)
    if h_blocks is not None:
        store_blocks(h_blocks[0], scalars.table(), scalars[0], out)


def middle_of(column, vec, branch, x):
    held = plus(load_ordered(branch, column, len(x)), vector_of(vec, BIAS_OUT))
    scaled, inverse = normalize(held)
    out = affine(scaled, vector_of(vec, GAIN2), vector_of(vec, SHIFT2))
    return scaled, inverse, [a + b for a, b in zip(load_pieces(x), out)]


def norm_mid_kernel(scalars, vec, branch, x, h, h_blocks, y):
    column = scalars[0]
    _, _, middle = middle_of(column, vec, branch, x)
    y[0][...] = middle[0]
    scaled, _ = normalize(middle)
    out = affine(scaled, vector_of(vec, GAIN3), vector_of(vec, SHIFT3))
    out = [p.astype(LOW) for p in out]
    store_ordered(h[0], column, out)
    store_blocks(h_blocks[0], scalars.table(), column, out)


def norm_out_kernel(scalars, vec, ffn, g, y, d_ffn, d_blocks, result, sums):
    column = scalars[0]
    held = plus(load_ordered(ffn, column, len(g)), vector_of(vec, BIAS_DOWN))
    scaled, inverse = normalize(held)
    gains = vector_of(vec, GAIN4)
    out = y[0][...] + scaled[0] * gains[0] + vector_of(vec, SHIFT4)[0]
    result[0][...] = out.astype(LOW)
    grads = load_pieces(g)
    back = [p.astype(LOW) for p in normalize_back(grads, scaled, inverse, gains)]
    store_ordered(d_ffn[0], column, back)
    store_blocks(d_blocks[0], scalars.table(), column, back)
    column_sums(sums[0], [grads[0] * scaled[0], grads[0], back[0].astype(F32)])


def norm_back_kernel(scalars, vec, d_h2, g, x, branch, d_branch, d_blocks, d_middle, sums):
    column = scalars[0]
    scaled2, inverse2, middle = middle_of(column, vec, branch, x)
    scaled3, inverse3 = normalize(middle)
    grads3 = load_ordered(d_h2, column, len(x))
    back3 = normalize_back(grads3, scaled3, inverse3, vector_of(vec, GAIN3))
    grads2 = [a + b for a, b in zip(load_pieces(g), back3)]
    d_middle[0][...] = grads2[0]
    back2 = normalize_back(grads2, scaled2, inverse2, vector_of(vec, GAIN2))
    back2 = [p.astype(LOW) for p in back2]
    store_ordered(d_branch[0], column, back2)
    store_blocks(d_blocks[0], scalars.table(), column, back2)
    column_sums(
        sums[0],
        [
            grads3[0] * scaled3[0],
            grads3[0],
            grads2[0] * scaled2[0],
            grads2[0],
            back2[0].astype(F32),
        ],
    )


def norm_last_kernel(scalars, vec, d_h1, x, d_middle, out, sums):
    column = scalars[0]
    scaled, inverse = normalize(load_pieces(x))
    grads = load_ordered(d_h1, column, len(x))
    back = normalize_back(grads, scaled, inverse, vector_of(vec, GAIN1))
    out[0][...] = (d_middle[0][...] + back[0]).astype(LOW)
    column_sums(sums[0], [grads[0] * scaled[0], grads[0]])


class Scalars:
    def __init__(self, ref, which):
        self.ref, self.which = ref, which

    def __getitem__(self, index):
        return self.ref[index]

    def table(self):
        return Table(self.ref, 1 + BLOCKS * self.which)


class Table:
    def __init__(self, ref, start):
        self.ref, self.start = ref, start

    def __getitem__(self, index):
        return self.ref[index + self.start]


def row_call(kernel, scalars, vectors, ins, outs, which=0):
    rows = ins[0][0].shape[0]
    step = min(256, rows)
    counts = [len(vectors)] + [len(group) for group in ins] + [1] * len(outs)

    chunk = min(128, step)

    def whole(scalar_ref, *refs):
        @pl.when(pl.program_id(0) == 0)
        def _():
            for ref, out in zip(refs[len(refs) - len(outs) :], outs):
                if not isinstance(out, tuple):
                    ref[...] = jnp.zeros(ref.shape, F32)

        def part(at, carry):
            groups = []
            used = 0
            here = pl.ds(pl.multiple_of(at * chunk, chunk), chunk)
            for count in counts:
                group = refs[used : used + count]
                used += count
                groups.append([r.at[here, :] if r.shape[0] == step else r for r in group])
            kernel(Scalars(scalar_ref, which), *groups)
            return carry

        lax.fori_loop(0, step // chunk, part, 0)

    def block(width):
        return pl.BlockSpec((step, width), lambda i, c: (i, 0))

    flat = [a for group in ins for a in group]
    shapes = []
    specs = []
    for out in outs:
        if isinstance(out, tuple):
            shapes.append(jax.ShapeDtypeStruct((rows, out[0]), out[1]))
            specs.append(block(out[0]))
        else:
            shapes.append(jax.ShapeDtypeStruct((8, out), F32))
            specs.append(pl.BlockSpec((8, out), lambda i, c: (0, 0)))
    return pl.pallas_call(
        whole,
        grid_spec=pltpu.PrefetchScalarGridSpec(
            num_scalar_prefetch=1,
            grid=(rows // step,),
            in_specs=[pl.BlockSpec(v.shape, lambda i, c: (0, 0)) for v in vectors]
            + [block(a.shape[1]) for a in flat],
            out_specs=specs,
        ),
        out_shape=shapes,
        cost_estimate=BRIEF,
    )(scalars, *vectors, *flat)


def route_tables(lengths, dealing, groups, half_rows, shard_count, row_count):
    seq_count = lengths.shape[0]
    per_group = seq_count // groups
    seq_ids = lax.iota(jnp.int32, seq_count)
    units = lengths // shard_count
    starts = jnp.sum(jnp.where(seq_ids[None, :] < seq_ids[:, None], units[None, :], 0), axis=1)
    chosen = dealing[:, None] == seq_ids[None, :]
    slot_len = jnp.sum(jnp.where(chosen, units[None, :], 0), axis=1)
    slot_in = jnp.sum(jnp.where(chosen, starts[None, :], 0), axis=1)
    earlier = (seq_ids[None, :] < seq_ids[:, None]) & (
        seq_ids[None, :] // per_group == seq_ids[:, None] // per_group
    )
    slot_ofs = jnp.sum(jnp.where(earlier, slot_len[None, :], 0), axis=1)
    grid_ofs = slot_ofs.reshape(groups, per_group)
    grid_anchor = (slot_in - slot_ofs).reshape(groups, per_group)
    places = half_rows // shard_count
    unit = (
        lax.broadcasted_iota(jnp.int32, (places, groups, row_count), 2) * places
        + lax.broadcasted_iota(jnp.int32, (places, groups, row_count), 0)
    )
    anchor = jnp.broadcast_to(grid_anchor[None, :, :1], unit.shape)
    for k in range(1, per_group):
        anchor = jnp.where(
            unit >= grid_ofs[None, :, k : k + 1], grid_anchor[None, :, k : k + 1], anchor
        )
    return (anchor + unit).reshape(half_rows), grid_ofs * shard_count


def head_lanes(shape, dim, head):
    lane = lax.broadcasted_iota(jnp.int32, shape, dim)
    return (lane >= head * DH) & (lane < (head + 1) * DH)


def masked_head(values, dim, head):
    return jnp.where(head_lanes(values.shape, dim, head), values, jnp.zeros_like(values))


def forward_kernel(
    begin_ref, q_ref, k_low_ref, v_low_ref, k_ref, v_ref, out_ref, log_ref, bias_ref
):
    rows = q_ref.shape[0]

    @pl.when(pl.program_id(0) == 0)
    def _():
        key_pos = lax.broadcasted_iota(jnp.int32, (rows, 2 * rows), 1) - rows
        query_pos = lax.broadcasted_iota(jnp.int32, (rows, 2 * rows), 0)
        allowed = (key_pos <= query_pos) & (key_pos >= begin_ref[...])
        bias_ref[...] = jnp.where(allowed, 0.0, MASKED)

    step = min(256, rows)
    first = head_lanes((step, PAIR), 1, 0)
    for at in range(0, rows, step):
        here = slice(at, at + step)
        keys = at + step
        parts = []
        logs = []
        for head in range(2):
            query = masked_head(q_ref[here, :], 1, head)
            scores = jnp.concatenate(
                [dot_back(query, k_low_ref[...]), dot_back(query, k_ref[:keys, :])], axis=1
            )
            scores = scores + bias_ref[here, : rows + keys]
            top = jnp.max(scores, axis=1, keepdims=True)
            weights = jnp.exp(scores - top)
            norm = jnp.sum(weights, axis=1, keepdims=True)
            weights = weights.astype(LOW)
            part_low = dot(weights[:, :rows], v_low_ref[...])
            parts.append((part_low + dot(weights[:, rows:], v_ref[:keys, :])) / norm)
            logs.append(top + jnp.log(norm))
        out_ref[here, :] = jnp.where(first, parts[0], parts[1]).astype(LOW)
        turned = jnp.where(first, logs[0], logs[1]).T
        log_ref[0, 0:1, here] = turned[:1]
        log_ref[0, 1:2, here] = turned[DH : DH + 1]


def backward_kernel(own, begin_ref, q_ref, k_ref, v_ref, g_ref, out_ref, log_ref, *rest):
    if own:
        dq_low_ref, dq_ref, dkv_ref, bias_ref = rest
    else:
        dq_ref, dkv_ref, bias_ref = rest
    rows = k_ref.shape[0]

    @pl.when(pl.program_id(0) == 0)
    def _():
        key_pos = lax.broadcasted_iota(jnp.int32, (rows, rows), 0) + (0 if own else -rows)
        query_pos = lax.broadcasted_iota(jnp.int32, (rows, rows), 1)
        allowed = (key_pos <= query_pos) & (key_pos >= begin_ref[...])
        bias_ref[...] = jnp.where(allowed, 0.0, MASKED)

    dots = (g_ref[...].astype(F32) * out_ref[...].astype(F32)).T
    keys_t = k_ref[...].T
    dk = []
    dv = []
    step = min(256, rows) if own else rows
    for at in range(0, rows, step):
        here = slice(at, at + step)
        keys = at + step if own else rows
        dq = []
        new_dk = []
        new_dv = []
        for head in range(2):
            lanes = slice(head * DH, (head + 1) * DH)
            query = masked_head(q_ref[here, :], 1, head)
            grad = masked_head(g_ref[here, :], 1, head)
            scores = dot_back(k_ref[:keys, :], query) + bias_ref[:keys, here]
            prob = jnp.exp(scores - log_ref[0, head : head + 1, here])
            grad_prob = dot_back(v_ref[:keys, :], grad)
            row_dot = jnp.sum(dots[lanes, here], axis=0, keepdims=True)
            grad_score = (prob * (grad_prob - row_dot)).astype(LOW)
            dq.append(dot(keys_t[lanes, :keys], grad_score))
            new_dk.append(dot(grad_score, query))
            new_dv.append(dot(prob.astype(LOW), grad))
        dk.append(total(new_dk))
        dv.append(total(new_dv))
        if own:
            dq = jnp.concatenate(dq, axis=0) + dq_low_ref[:, here]
            dq_ref[here, :] = (dq * (1.0 / math.sqrt(DH))).T.astype(LOW)
        else:
            dq_ref[:DH, here] = dq[0]
            dq_ref[DH:, here] = dq[1]
    for at, parts in enumerate((dk, dv)):
        ends = sorted({p.shape[0] for p in parts})
        for begin, end in zip([0] + ends[:-1], ends):
            pieces = [p[begin:end] for p in parts if p.shape[0] >= end]
            dkv_ref[at, begin:end, :] = total(pieces).astype(LOW)


def pair_spec(rows):
    return pl.BlockSpec((rows, PAIR), lambda i: (0, i))


def pair_t_spec(rows):
    return pl.BlockSpec((PAIR, rows), lambda i: (i, 0))


def stat_spec(rows):
    return pl.BlockSpec((1, 2, rows), lambda i: (i, 0, 0))


def attend_call(kernel, rows, width, ins, outs, keys):
    pairs = width // PAIR
    shapes = {
        "rows": (pair_spec(rows), (rows, width)),
        "cols": (pair_t_spec(rows), (width, rows)),
        "stat": (stat_spec(rows), (pairs, 2, rows)),
        "two": (pl.BlockSpec((2, rows, PAIR), lambda i: (0, 0, i)), (2, rows, width)),
        "line": (pl.BlockSpec((1, rows), lambda i: (0, 0)), (1, rows)),
        "post": (pl.BlockSpec((rows, 1), lambda i: (0, 0)), (rows, 1)),
    }
    return pl.pallas_call(
        kernel,
        grid=(pairs,),
        in_specs=[shapes[kind][0] for kind in ins],
        out_specs=[shapes[kind][0] for kind, _ in outs],
        out_shape=[jax.ShapeDtypeStruct(shapes[kind][1], dtype) for kind, dtype in outs],
        scratch_shapes=[pltpu.VMEM((rows, keys), F32)],
        cost_estimate=BRIEF,
    )


def pick(values, index):
    size = values.shape[0] // 2
    return lax.dynamic_slice_in_dim(values, index * size, size, 0, allow_negative_indices=False)


def place_table(orders):
    def places(order):
        head = order[:3]
        spare = [phase for phase in head if phase != ROW]
        block = lax.iota(jnp.int32, BLOCKS)
        natural = {ROW: (block >> 2) & 1, spare[0]: (block >> 1) & 1, spare[1]: block & 1}
        place = jnp.zeros((BLOCKS,), jnp.int32)
        for phase in head:
            place = place * 2 + (natural[phase] ^ bit_at(phase))
        return place

    return per_core(places(orders[0]), places(orders[1]))


class GradSum:
    def __init__(self, name, terms, orders, outs):
        self.name, self.terms, self.outs = name, terms, outs
        self.phases = list(zip(*orders))
        dp_phases = [[p for p in order if p != ROW] for order in orders]
        self.first, self.second = [tuple(order[i] for order in dp_phases) for i in range(2)]
        self.back = list(zip(*[list(reversed(order[:-1])) for order in dp_phases]))
        self.at = 0
        self.results = None

    def product(self, index):
        cut = []
        for left, right in self.terms:
            size = left.shape[1] // 2
            half = lax.slice_in_dim(left, index * size, (index + 1) * size, axis=1)
            cut.append(dot_tokens(half, right).astype(LOW))
        return cut[0] if len(cut) == 1 else jnp.concatenate(cut, axis=1)

    def begin(self):
        with jax.named_scope(self.name + "_phase0"):
            sent = self.product(1)
            self.got = swap_phase(sent, self.phases[0])
        return sent

    def keep(self, *earlier):
        if earlier:
            self.terms = [(left, after(right, *earlier)) for left, right in self.terms]
        self.held = [self.product(0)]
        return self.held[0]

    def advance(self, *earlier):
        self.at += 1
        with jax.named_scope(f"{self.name}_phase{self.at}"):
            return self.step(after(self.got, *earlier))

    def rows_sum(self, begin, end):
        return total([a[begin:end].astype(F32) for a in self.held]).astype(LOW)

    def step(self, got):
        spot = self.at - len(self.phases)
        rows = got.shape[0]
        if spot < 0:
            self.held.append(got)
            phases = self.phases[self.at]
            if spot == -1:
                sent = self.rows_sum(0, rows)
                self.held = [sent]
            elif self.at < 3:
                sent = self.rows_sum(rows // 2, rows)
            else:
                mine = per_core(bit_at(phases[0]), bit_at(phases[1]))
                held = self.rows_sum(0, rows)
                sent = pick(held, 1 - mine)
                self.held = [pick(held, mine)]
        else:
            kept = self.held[0]
            if spot == 0:
                low = (kept.astype(F32) + got.astype(F32)).astype(LOW)
            elif spot <= len(self.back) - 2:
                phases = self.back[spot - 1]
                flip = per_core(bit_at(phases[0]), bit_at(phases[1])) == 1
                low = jnp.concatenate(
                    [jnp.where(flip, got, kept), jnp.where(flip, kept, got)], axis=0
                )
            elif spot == len(self.back) - 1:
                low = jnp.concatenate([kept, got], axis=0)
                self.partial = self.spread(low, 0)
            else:
                self.results = self.spread(got, 1, self.partial)
                return self.results[0]
            phases = self.back[spot]
            sent = low
            self.held = [low]
        self.got = swap_phase(sent, phases)
        return sent

    def spread(self, half, index, held=None):
        bits = per_core(*[bit_at(self.first[i]) * 2 + bit_at(self.second[i]) for i in range(2)])
        places = (2 * index + lax.iota(jnp.int32, 2)) ^ bits
        size = half.shape[0] // 2
        rows = 4 * size
        width = half.shape[1]
        held = list(held or [])

        def kernel(place_ref, half_ref, *refs):
            values = half_ref[...].astype(F32)
            for ref, (begin, end, turned) in zip(refs[len(held) :], self.outs):
                ref[...] = values[:, begin:end].T if turned else values[:, begin:end]

        shapes = []
        specs = []
        for begin, end, turned in self.outs:
            if turned:
                shapes.append(jax.ShapeDtypeStruct((end - begin, rows), F32))
                specs.append(pl.BlockSpec((end - begin, size), lambda i, t: (0, t[i])))
            else:
                shapes.append(jax.ShapeDtypeStruct((rows, end - begin), F32))
                specs.append(pl.BlockSpec((size, end - begin), lambda i, t: (t[i], 0)))
        return pl.pallas_call(
            kernel,
            grid_spec=pltpu.PrefetchScalarGridSpec(
                num_scalar_prefetch=1,
                grid=(2,),
                in_specs=[pl.BlockSpec((size, width), lambda i, t: (i, 0))]
                + [pl.BlockSpec(memory_space=pl.ANY)] * len(held),
                out_specs=specs,
            ),
            out_shape=shapes,
            input_output_aliases={2 + k: k for k in range(len(held))},
            cost_estimate=BRIEF,
        )(places, half, *held)


ORDERS_DOWN = [[ROW, 1, 0], [0, ROW, 1]]
ORDERS_UP = [[1, 0, ROW], [0, 1, ROW]]
ORDERS_ATTENTION = [[ROW, 0, 1], [1, ROW, 0]]
TAIL = "UWAAxUWAUWUAAAU"


def body(
    layer_input,
    cotangent,
    lengths,
    dealing,
    w_query,
    w_key,
    w_value,
    bias_query,
    bias_value,
    w_out,
    bias_out,
    w_up,
    bias_up,
    w_down,
    bias_down,
    gain_attention_in,
    shift_attention_in,
    gain_attention_out,
    shift_attention_out,
    gain_ffn_in,
    shift_ffn_in,
    gain_ffn_out,
    shift_ffn_out,
):
    row_count = lax.axis_size("row")
    groups = lax.axis_size("dp")
    shard_count = groups * row_count
    row_index = lax.axis_index("row")
    group_index = lax.axis_index("dp")
    rows = layer_input.shape[0]
    local_width = layer_input.shape[2]
    places = rows // shard_count
    group_rows = rows * row_count

    routes, grid_ofs = route_tables(lengths, dealing, groups, rows, shard_count, row_count)
    place = (routes[:, None] == lax.iota(jnp.int32, rows)[None, :]).astype(LOW)

    def deal(values):
        sent = dot(place, values.reshape(rows, local_width)).astype(LOW)
        sent = sent.reshape(places, shard_count, local_width)
        got = lax.all_to_all(sent, ("dp", "row"), split_axis=1, concat_axis=1, tiled=True)
        return got.reshape(rows, local_width)

    def undo_deal(values, sums=None):
        sent = values.reshape(places, shard_count, local_width)
        if sums is not None:
            copies = (sums.shape[0],) + sent.shape[1:]
            spread = jnp.broadcast_to(sums.astype(LOW)[:, None, :], copies)
            sent = jnp.concatenate([sent, spread], axis=0)
        got = lax.all_to_all(sent, ("dp", "row"), split_axis=1, concat_axis=1, tiled=True)
        back = dot_tokens(place, got[:places].reshape(rows, local_width)).astype(LOW)
        back = back.reshape(rows, 1, local_width)
        if sums is None:
            return back
        return back, jnp.sum(got[places:].astype(F32), axis=1)

    own_ofs = jnp.sum(
        jnp.where((lax.iota(jnp.int32, groups) == group_index)[:, None], grid_ofs, 0), axis=0
    )
    positions = row_index * rows + lax.iota(jnp.int32, rows)
    begin = jnp.max(
        jnp.where(positions[:, None] >= own_ofs[None, :], own_ofs[None, :], 0), axis=1
    )
    begin = (begin - row_index * rows).reshape(1, rows)

    packed = jnp.stack(
        [
            gain_attention_in,
            shift_attention_in,
            gain_attention_out,
            shift_attention_out,
            gain_ffn_in,
            shift_ffn_in,
            gain_ffn_out,
            shift_ffn_out,
            bias_out,
            bias_down,
        ]
    )
    vectors = col_pieces(packed)
    rest = list(bits_of("dp"))[2:]
    orders_up = [head + rest for head in ORDERS_UP]
    orders_down = [head + rest for head in ORDERS_DOWN]
    orders_attention = [head + rest for head in ORDERS_ATTENTION]
    column = lax.axis_index("col").reshape(1)

    tables = [place_table(o) for o in (orders_attention, orders_up, orders_down)]
    scalars = jnp.concatenate([column] + tables)

    x_own = deal(layer_input)
    x_low_own = lax.ppermute(x_own, "row", [(0, 1)])
    g_own = deal(cotangent)
    x = col_pieces(x_own)
    h1, h1_blocks = row_call(
        norm_in_kernel, scalars, vectors, [x], [(D, LOW), (D, LOW)]
    )
    queries = ((dot(h1, w_query) + bias_query) * (1.0 / math.sqrt(DH))).astype(LOW)
    keys = dot(h1, w_key).astype(LOW)
    values = (dot(h1, w_value) + bias_value).astype(LOW)

    width = queries.shape[1]
    x_low = col_pieces(after(x_low_own, queries))
    (h_low,) = row_call(norm_in_kernel, scalars, vectors, [x_low], [(D, LOW)])
    keys_low = dot(h_low, w_key).astype(LOW)
    values_low = (dot(h_low, w_value) + bias_value).astype(LOW)
    attended, log_total = attend_call(
        forward_kernel,
        rows,
        width,
        ["post"] + ["rows"] * 5,
        [("rows", LOW), ("stat", F32)],
        2 * rows,
    )(begin.reshape(rows, 1), queries, keys_low, values_low, keys, values)

    branch = col_parts(dot(attended, w_out).astype(LOW))
    h2, h2_blocks, y_own = row_call(
        norm_mid_kernel,
        scalars,
        vectors,
        [branch, x],
        [(D, LOW), (D, LOW), (local_width, F32)],
        1,
    )
    pre = dot(h2, w_up) + bias_up
    cube = math.sqrt(2.0 / math.pi)
    bend = jnp.tanh(cube * (pre + 0.044715 * pre * pre * pre))
    hidden = (0.5 * pre * (1.0 + bend)).astype(LOW)
    slope = 0.5 * (1.0 + bend) + 0.5 * pre * (1.0 - bend * bend) * cube * (
        1.0 + 3.0 * 0.044715 * pre * pre
    )
    slope = slope.astype(LOW)
    ffn = col_parts(dot(hidden, w_down).astype(LOW))
    g = col_pieces(g_own)
    d_ffn, d_ffn_blocks, result, sums4 = row_call(
        norm_out_kernel,
        scalars,
        vectors,
        [ffn, g, [y_own]],
        [(D, LOW), (D, LOW), (local_width, LOW), local_width],
        2,
    )

    ff = hidden.shape[1]
    down = GradSum("down", [(d_ffn_blocks, hidden)], orders_down, [(0, ff, True)])
    tip = down.begin()
    d_pre = dot_back(after(d_ffn, tip), w_down) * slope.astype(F32)
    d_pre = d_pre.astype(LOW)
    up = GradSum("up", [(h2_blocks, d_pre)], orders_up, [(0, ff, False)])
    tip = up.begin()
    d_h2 = col_parts(dot_back(after(d_pre, tip), w_up).astype(LOW))
    kept_down = down.keep(d_h2[0])
    d_branch, d_branch_blocks, d_middle, sums3 = row_call(
        norm_back_kernel,
        scalars,
        vectors,
        [d_h2, g, x, branch],
        [(D, LOW), (D, LOW), (local_width, F32), local_width],
    )
    tip = down.advance(d_branch, kept_down)
    d_attended = dot_back(after(d_branch, tip), w_out).astype(LOW)
    back_ins = ["line"] + ["rows"] * 5 + ["stat"]
    dq_low, dkv_low = attend_call(
        functools.partial(backward_kernel, False),
        rows,
        width,
        back_ins,
        [("cols", F32), ("two", LOW)],
        rows,
    )(begin, queries, keys_low, values_low, d_attended, attended, log_total)
    dkv_back = lax.ppermute(dkv_low, "row", [(1, 0)])
    tip = up.keep(dq_low)
    tip = down.advance(tip)
    d_query, dkv_own = attend_call(
        functools.partial(backward_kernel, True),
        rows,
        width,
        back_ins + ["cols"],
        [("rows", LOW), ("two", LOW)],
        rows,
    )(begin, queries, keys, values, after(d_attended, tip), attended, log_total, dq_low)

    tip = up.advance(d_query)
    tip = down.advance(tip)
    dkv = dkv_own.astype(F32) + after(dkv_back, tip).astype(F32)
    d_key, d_value = dkv[0].astype(LOW), dkv[1].astype(LOW)
    attention = GradSum(
        "attention",
        [
            (h1_blocks, d_query),
            (h1_blocks, d_key),
            (h1_blocks, d_value),
            (d_branch_blocks, attended),
        ],
        orders_attention,
        [(k * width, (k + 1) * width, k == 3) for k in range(4)],
    )
    tip = attention.begin()
    output = undo_deal(after(result, tip))
    d_h1 = dot_back(after(d_query, tip), w_query) + dot_back(d_key, w_key)
    d_h1 = col_parts((d_h1 + dot_back(d_value, w_value)).astype(LOW))
    kept = attention.keep(d_h1[0])
    in_grad, sums1 = row_call(
        norm_last_kernel,
        scalars,
        vectors,
        [d_h1, x, [d_middle]],
        [(local_width, LOW), local_width],
    )
    tip = in_grad
    ready = [in_grad, kept]

    def summed(values):
        return jnp.sum(values.astype(F32), axis=0).reshape(-1, local_width)

    small_rows = [sums1[:2], sums3[:5], sums4[:3]]
    small_rows = small_rows + [summed(d_query), summed(d_value), summed(d_pre)]
    packed_sums = jnp.concatenate(small_rows, axis=0)
    chains = {"W": down, "U": up, "A": attention}
    for name in TAIL:
        if name == "x":
            input_grad, smalls = undo_deal(after(in_grad, tip), packed_sums)
        else:
            tip = chains[name].advance(tip, *ready)
            ready = []
    for chain in chains.values():
        while chain.results is None:
            tip = chain.advance(tip)

    grad_query, grad_key, grad_value, grad_out = attention.results
    (grad_up,) = up.results
    (grad_down,) = down.results
    return (
        output,
        input_grad,
        grad_query,
        grad_key,
        grad_value,
        smalls[10],
        smalls[11],
        grad_out,
        smalls[6],
        grad_up,
        smalls[12:].reshape(-1),
        grad_down,
        smalls[9],
        smalls[0],
        smalls[1],
        smalls[4],
        smalls[5],
        smalls[2],
        smalls[3],
        smalls[7],
        smalls[8],
    )


def solution(mesh):
    shards = P(None, ("dp", "row"), "col")
    by_col = P("col")
    vectors = (by_col,) * 8
    return jax.shard_map(
        body,
        mesh=mesh,
        in_specs=(
            shards,
            shards,
            P(),
            P(),
            P(None, "col"),
            P(None, "col"),
            P(None, "col"),
            by_col,
            by_col,
            P("col", None),
            by_col,
            P(None, "col"),
            by_col,
            P("col", None),
            by_col,
            *vectors,
        ),
        out_specs=(
            shards,
            shards,
            P("row", "col"),
            P("row", "col"),
            P("row", "col"),
            by_col,
            by_col,
            P("col", "row"),
            by_col,
            P("row", "col"),
            by_col,
            P("col", "row"),
            by_col,
            *vectors,
        ),
        check_vma=False,
    )
```

```python
import functools
import math

import jax
import jax.numpy as jnp
from jax import lax
from jax.experimental import pallas as pl
from jax.experimental.pallas import tpu as pltpu
from jax.sharding import PartitionSpec as P

D = 1024
DH = 64
PAIR = 2 * DH
EPSILON = 1e-05
MASKED = -1e30
LOW = jnp.bfloat16
F32 = jnp.float32
BRIEF = pl.CostEstimate(flops=1, bytes_accessed=1, transcendentals=0)


def swap(values, axis, bit):
    size = lax.axis_size(axis)
    return lax.ppermute(values, axis, [(i, i ^ (1 << bit)) for i in range(size)])


def bits_of(axis):
    return range(lax.axis_size(axis).bit_length() - 1)


def bit_at(phase):
    if phase == ROW:
        return lax.axis_index("row")
    return (lax.axis_index("dp") >> phase) & 1


ROW = "row"


def swap_phase(values, phases):
    sizes = [lax.axis_size(axis) for axis in ("dp", "row", "col")]
    pairs = []
    for dp in range(sizes[0]):
        for row in range(sizes[1]):
            for col in range(sizes[2]):
                phase = phases[col % 2]
                there = (dp, row ^ 1) if phase == ROW else (dp ^ (1 << phase), row)
                pairs.append(
                    (
                        (dp * sizes[1] + row) * sizes[2] + col,
                        (there[0] * sizes[1] + there[1]) * sizes[2] + col,
                    )
                )
    return lax.ppermute(values, ("dp", "row", "col"), pairs)


def per_core(even, odd):
    return jnp.where(lax.axis_index("col") % 2 == 0, even, odd)


def col_pieces(own):
    pieces = [own]
    for bit in bits_of("col"):
        pieces = pieces + [swap(piece, "col", bit) for piece in pieces]
    return pieces


def col_parts(partial):
    bits = list(bits_of("col"))
    for bit in bits[:-1]:
        partial = (partial.astype(F32) + swap(partial, "col", bit).astype(F32)).astype(LOW)
    return [partial, swap(partial, "col", bits[-1])]


def after(values, *earlier):
    return lax.optimization_barrier((values, *earlier))[0]


def dot(left, right):
    return jnp.dot(left, right, preferred_element_type=F32)


def dot_back(left, right):
    return lax.dot_general(left, right, (((1,), (1,)), ((), ())), preferred_element_type=F32)


def dot_tokens(left, right):
    return lax.dot_general(left, right, (((0,), (0,)), ((), ())), preferred_element_type=F32)


BLOCKS = 8
GAIN1, SHIFT1, GAIN2, SHIFT2, GAIN3, SHIFT3, GAIN4, SHIFT4, BIAS_OUT, BIAS_DOWN = range(10)


def total(parts):
    return functools.reduce(lambda a, b: a + b, parts)


def row_mean(pieces):
    return total([jnp.sum(p, axis=1, keepdims=True) for p in pieces]) * (1.0 / D)


def normalize(pieces):
    average = row_mean(pieces)
    inverse = lax.rsqrt(row_mean([p * p for p in pieces]) - average * average + EPSILON)
    return [(p - average) * inverse for p in pieces], inverse


def normalize_back(grads, scaled, inverse, gains):
    pushed = [e * g for e, g in zip(grads, gains)]
    mean_push = row_mean(pushed)
    mean_dot = row_mean([f * n for f, n in zip(pushed, scaled)])
    return [inverse * (f - mean_push - n * mean_dot) for f, n in zip(pushed, scaled)]


def span(column, k, width):
    return pl.ds(pl.multiple_of((column ^ k) * width, 128), width)


def load_pieces(refs):
    return [ref[...].astype(F32) for ref in refs]


def load_ordered(refs, column, count):
    width = refs[0].shape[1] // count
    return [
        total([ref[:, span(column, k, width)].astype(F32) for ref in refs]) for k in range(count)
    ]


def store_ordered(ref, column, pieces):
    width = ref.shape[1] // len(pieces)
    for k, piece in enumerate(pieces):
        ref[:, span(column, k, width)] = piece


def store_blocks(ref, table, column, pieces):
    size = ref.shape[1] // BLOCKS
    width = ref.shape[1] // len(pieces)
    for k, piece in enumerate(pieces):
        first = (column ^ k) * (width // size)
        for j in range(width // size):
            place = pl.multiple_of(table[first + j] * size, 128)
            ref[:, pl.ds(place, size)] = piece[:, j * size : (j + 1) * size]


def column_sums(ref, rows):
    for at, values in enumerate(rows):
        ref[at : at + 1, :] += jnp.sum(values, axis=0, keepdims=True)


def vector_of(vector_refs, index):
    return [ref[index : index + 1, :] for ref in vector_refs]


def plus(pieces, vectors):
    return [p + v for p, v in zip(pieces, vectors)]


def affine(scaled, gains, shifts):
    return [s * g + b for s, g, b in zip(scaled, gains, shifts)]


def norm_in_kernel(scalars, vec, x, h, h_blocks=None):
    scaled, _ = normalize(load_pieces(x))
    out = affine(scaled, vector_of(vec, GAIN1), vector_of(vec, SHIFT1))
    out = [p.astype(LOW) for p in out]
    store_ordered(h[0], scalars[0], out)
    if h_blocks is not None:
        store_blocks(h_blocks[0], scalars.table(), scalars[0], out)


def middle_of(column, vec, branch, x):
    held = plus(load_ordered(branch, column, len(x)), vector_of(vec, BIAS_OUT))
    scaled, inverse = normalize(held)
    out = affine(scaled, vector_of(vec, GAIN2), vector_of(vec, SHIFT2))
    return scaled, inverse, [a + b for a, b in zip(load_pieces(x), out)]


def norm_mid_kernel(scalars, vec, branch, x, h, h_blocks, y):
    column = scalars[0]
    _, _, middle = middle_of(column, vec, branch, x)
    y[0][...] = middle[0]
    scaled, _ = normalize(middle)
    out = affine(scaled, vector_of(vec, GAIN3), vector_of(vec, SHIFT3))
    out = [p.astype(LOW) for p in out]
    store_ordered(h[0], column, out)
    store_blocks(h_blocks[0], scalars.table(), column, out)


def norm_out_kernel(scalars, vec, ffn, g, y, d_ffn, d_blocks, result, sums):
    column = scalars[0]
    held = plus(load_ordered(ffn, column, len(g)), vector_of(vec, BIAS_DOWN))
    scaled, inverse = normalize(held)
    gains = vector_of(vec, GAIN4)
    out = y[0][...] + scaled[0] * gains[0] + vector_of(vec, SHIFT4)[0]
    result[0][...] = out.astype(LOW)
    grads = load_pieces(g)
    back = [p.astype(LOW) for p in normalize_back(grads, scaled, inverse, gains)]
    store_ordered(d_ffn[0], column, back)
    store_blocks(d_blocks[0], scalars.table(), column, back)
    column_sums(sums[0], [grads[0] * scaled[0], grads[0], back[0].astype(F32)])


def norm_back_kernel(scalars, vec, d_h2, g, x, branch, d_branch, d_blocks, d_middle, sums):
    column = scalars[0]
    scaled2, inverse2, middle = middle_of(column, vec, branch, x)
    scaled3, inverse3 = normalize(middle)
    grads3 = load_ordered(d_h2, column, len(x))
    back3 = normalize_back(grads3, scaled3, inverse3, vector_of(vec, GAIN3))
    grads2 = [a + b for a, b in zip(load_pieces(g), back3)]
    d_middle[0][...] = grads2[0]
    back2 = normalize_back(grads2, scaled2, inverse2, vector_of(vec, GAIN2))
    back2 = [p.astype(LOW) for p in back2]
    store_ordered(d_branch[0], column, back2)
    store_blocks(d_blocks[0], scalars.table(), column, back2)
    column_sums(
        sums[0],
        [
            grads3[0] * scaled3[0],
            grads3[0],
            grads2[0] * scaled2[0],
            grads2[0],
            back2[0].astype(F32),
        ],
    )


def norm_last_kernel(scalars, vec, d_h1, x, d_middle, out, sums):
    column = scalars[0]
    scaled, inverse = normalize(load_pieces(x))
    grads = load_ordered(d_h1, column, len(x))
    back = normalize_back(grads, scaled, inverse, vector_of(vec, GAIN1))
    out[0][...] = (d_middle[0][...] + back[0]).astype(LOW)
    column_sums(sums[0], [grads[0] * scaled[0], grads[0]])


class Scalars:
    def __init__(self, ref, which):
        self.ref, self.which = ref, which

    def __getitem__(self, index):
        return self.ref[index]

    def table(self):
        return Table(self.ref, 1 + BLOCKS * self.which)


class Table:
    def __init__(self, ref, start):
        self.ref, self.start = ref, start

    def __getitem__(self, index):
        return self.ref[index + self.start]


def row_call(kernel, scalars, vectors, ins, outs, which=0):
    rows = ins[0][0].shape[0]
    step = min(256, rows)
    counts = [len(vectors)] + [len(group) for group in ins] + [1] * len(outs)

    chunk = min(128, step)

    def whole(scalar_ref, *refs):
        @pl.when(pl.program_id(0) == 0)
        def _():
            for ref, out in zip(refs[len(refs) - len(outs) :], outs):
                if not isinstance(out, tuple):
                    ref[...] = jnp.zeros(ref.shape, F32)

        def part(at, carry):
            groups = []
            used = 0
            here = pl.ds(pl.multiple_of(at * chunk, chunk), chunk)
            for count in counts:
                group = refs[used : used + count]
                used += count
                groups.append([r.at[here, :] if r.shape[0] == step else r for r in group])
            kernel(Scalars(scalar_ref, which), *groups)
            return carry

        lax.fori_loop(0, step // chunk, part, 0)

    def block(width):
        return pl.BlockSpec((step, width), lambda i, c: (i, 0))

    flat = [a for group in ins for a in group]
    shapes = []
    specs = []
    for out in outs:
        if isinstance(out, tuple):
            shapes.append(jax.ShapeDtypeStruct((rows, out[0]), out[1]))
            specs.append(block(out[0]))
        else:
            shapes.append(jax.ShapeDtypeStruct((8, out), F32))
            specs.append(pl.BlockSpec((8, out), lambda i, c: (0, 0)))
    return pl.pallas_call(
        whole,
        grid_spec=pltpu.PrefetchScalarGridSpec(
            num_scalar_prefetch=1,
            grid=(rows // step,),
            in_specs=[pl.BlockSpec(v.shape, lambda i, c: (0, 0)) for v in vectors]
            + [block(a.shape[1]) for a in flat],
            out_specs=specs,
        ),
        out_shape=shapes,
        cost_estimate=BRIEF,
    )(scalars, *vectors, *flat)


def route_tables(lengths, dealing, groups, half_rows, shard_count, row_count):
    seq_count = lengths.shape[0]
    per_group = seq_count // groups
    seq_ids = lax.iota(jnp.int32, seq_count)
    units = lengths // shard_count
    starts = jnp.sum(jnp.where(seq_ids[None, :] < seq_ids[:, None], units[None, :], 0), axis=1)
    chosen = dealing[:, None] == seq_ids[None, :]
    slot_len = jnp.sum(jnp.where(chosen, units[None, :], 0), axis=1)
    slot_in = jnp.sum(jnp.where(chosen, starts[None, :], 0), axis=1)
    earlier = (seq_ids[None, :] < seq_ids[:, None]) & (
        seq_ids[None, :] // per_group == seq_ids[:, None] // per_group
    )
    slot_ofs = jnp.sum(jnp.where(earlier, slot_len[None, :], 0), axis=1)
    grid_ofs = slot_ofs.reshape(groups, per_group)
    grid_anchor = (slot_in - slot_ofs).reshape(groups, per_group)
    places = half_rows // shard_count
    unit = (
        lax.broadcasted_iota(jnp.int32, (places, groups, row_count), 2) * places
        + lax.broadcasted_iota(jnp.int32, (places, groups, row_count), 0)
    )
    anchor = jnp.broadcast_to(grid_anchor[None, :, :1], unit.shape)
    for k in range(1, per_group):
        anchor = jnp.where(
            unit >= grid_ofs[None, :, k : k + 1], grid_anchor[None, :, k : k + 1], anchor
        )
    return (anchor + unit).reshape(half_rows), grid_ofs * shard_count


def head_lanes(shape, dim, head):
    lane = lax.broadcasted_iota(jnp.int32, shape, dim)
    return (lane >= head * DH) & (lane < (head + 1) * DH)


def masked_head(values, dim, head):
    return jnp.where(head_lanes(values.shape, dim, head), values, jnp.zeros_like(values))


def forward_kernel(
    begin_ref, q_ref, k_low_ref, v_low_ref, k_ref, v_ref, out_ref, log_ref, bias_ref
):
    rows = q_ref.shape[0]

    @pl.when(pl.program_id(0) == 0)
    def _():
        key_pos = lax.broadcasted_iota(jnp.int32, (rows, 2 * rows), 1) - rows
        query_pos = lax.broadcasted_iota(jnp.int32, (rows, 2 * rows), 0)
        allowed = (key_pos <= query_pos) & (key_pos >= begin_ref[...])
        bias_ref[...] = jnp.where(allowed, 0.0, MASKED)

    step = min(256, rows)
    first = head_lanes((step, PAIR), 1, 0)
    for at in range(0, rows, step):
        here = slice(at, at + step)
        keys = at + step
        parts = []
        logs = []
        for head in range(2):
            query = masked_head(q_ref[here, :], 1, head)
            scores = jnp.concatenate(
                [dot_back(query, k_low_ref[...]), dot_back(query, k_ref[:keys, :])], axis=1
            )
            scores = scores + bias_ref[here, : rows + keys]
            top = jnp.max(scores, axis=1, keepdims=True)
            weights = jnp.exp(scores - top)
            norm = jnp.sum(weights, axis=1, keepdims=True)
            weights = weights.astype(LOW)
            part_low = dot(weights[:, :rows], v_low_ref[...])
            parts.append((part_low + dot(weights[:, rows:], v_ref[:keys, :])) / norm)
            logs.append(top + jnp.log(norm))
        out_ref[here, :] = jnp.where(first, parts[0], parts[1]).astype(LOW)
        turned = jnp.where(first, logs[0], logs[1]).T
        log_ref[0, 0:1, here] = turned[:1]
        log_ref[0, 1:2, here] = turned[DH : DH + 1]


def backward_kernel(own, begin_ref, q_ref, k_ref, v_ref, g_ref, out_ref, log_ref, *rest):
    if own:
        dq_low_ref, dq_ref, dkv_ref, bias_ref = rest
    else:
        dq_ref, dkv_ref, bias_ref = rest
    rows = k_ref.shape[0]

    @pl.when(pl.program_id(0) == 0)
    def _():
        key_pos = lax.broadcasted_iota(jnp.int32, (rows, rows), 0) + (0 if own else -rows)
        query_pos = lax.broadcasted_iota(jnp.int32, (rows, rows), 1)
        allowed = (key_pos <= query_pos) & (key_pos >= begin_ref[...])
        bias_ref[...] = jnp.where(allowed, 0.0, MASKED)

    dots = (g_ref[...].astype(F32) * out_ref[...].astype(F32)).T
    keys_t = k_ref[...].T
    dk = []
    dv = []
    step = min(256, rows) if own else rows
    for at in range(0, rows, step):
        here = slice(at, at + step)
        keys = at + step if own else rows
        dq = []
        new_dk = []
        new_dv = []
        for head in range(2):
            lanes = slice(head * DH, (head + 1) * DH)
            query = masked_head(q_ref[here, :], 1, head)
            grad = masked_head(g_ref[here, :], 1, head)
            scores = dot_back(k_ref[:keys, :], query) + bias_ref[:keys, here]
            prob = jnp.exp(scores - log_ref[0, head : head + 1, here])
            grad_prob = dot_back(v_ref[:keys, :], grad)
            row_dot = jnp.sum(dots[lanes, here], axis=0, keepdims=True)
            grad_score = (prob * (grad_prob - row_dot)).astype(LOW)
            dq.append(dot(keys_t[lanes, :keys], grad_score))
            new_dk.append(dot(grad_score, query))
            new_dv.append(dot(prob.astype(LOW), grad))
        dk.append(total(new_dk))
        dv.append(total(new_dv))
        if own:
            dq = jnp.concatenate(dq, axis=0) + dq_low_ref[:, here]
            dq_ref[here, :] = (dq * (1.0 / math.sqrt(DH))).T.astype(LOW)
        else:
            dq_ref[:DH, here] = dq[0]
            dq_ref[DH:, here] = dq[1]
    for at, parts in enumerate((dk, dv)):
        ends = sorted({p.shape[0] for p in parts})
        for begin, end in zip([0] + ends[:-1], ends):
            pieces = [p[begin:end] for p in parts if p.shape[0] >= end]
            dkv_ref[at, begin:end, :] = total(pieces).astype(LOW)


def pair_spec(rows):
    return pl.BlockSpec((rows, PAIR), lambda i: (0, i))


def pair_t_spec(rows):
    return pl.BlockSpec((PAIR, rows), lambda i: (i, 0))


def stat_spec(rows):
    return pl.BlockSpec((1, 2, rows), lambda i: (i, 0, 0))


def attend_call(kernel, rows, width, ins, outs, keys):
    pairs = width // PAIR
    shapes = {
        "rows": (pair_spec(rows), (rows, width)),
        "cols": (pair_t_spec(rows), (width, rows)),
        "stat": (stat_spec(rows), (pairs, 2, rows)),
        "two": (pl.BlockSpec((2, rows, PAIR), lambda i: (0, 0, i)), (2, rows, width)),
        "line": (pl.BlockSpec((1, rows), lambda i: (0, 0)), (1, rows)),
        "post": (pl.BlockSpec((rows, 1), lambda i: (0, 0)), (rows, 1)),
    }
    return pl.pallas_call(
        kernel,
        grid=(pairs,),
        in_specs=[shapes[kind][0] for kind in ins],
        out_specs=[shapes[kind][0] for kind, _ in outs],
        out_shape=[jax.ShapeDtypeStruct(shapes[kind][1], dtype) for kind, dtype in outs],
        scratch_shapes=[pltpu.VMEM((rows, keys), F32)],
        cost_estimate=BRIEF,
    )


def pick(values, index):
    size = values.shape[0] // 2
    return lax.dynamic_slice_in_dim(values, index * size, size, 0, allow_negative_indices=False)


def place_table(orders):
    def places(order):
        head = order[:3]
        spare = [phase for phase in head if phase != ROW]
        block = lax.iota(jnp.int32, BLOCKS)
        natural = {ROW: (block >> 2) & 1, spare[0]: (block >> 1) & 1, spare[1]: block & 1}
        place = jnp.zeros((BLOCKS,), jnp.int32)
        for phase in head:
            place = place * 2 + (natural[phase] ^ bit_at(phase))
        return place

    return per_core(places(orders[0]), places(orders[1]))


class GradSum:
    def __init__(self, name, terms, orders, outs):
        self.name, self.terms, self.outs = name, terms, outs
        self.phases = list(zip(*orders))
        dp_phases = [[p for p in order if p != ROW] for order in orders]
        self.first, self.second = [tuple(order[i] for order in dp_phases) for i in range(2)]
        self.back = list(zip(*[list(reversed(order[:-1])) for order in dp_phases]))
        self.at = 0
        self.results = None

    def product(self, index):
        cut = []
        for left, right in self.terms:
            size = left.shape[1] // 2
            half = lax.slice_in_dim(left, index * size, (index + 1) * size, axis=1)
            cut.append(dot_tokens(half, right).astype(LOW))
        return cut[0] if len(cut) == 1 else jnp.concatenate(cut, axis=1)

    def begin(self):
        with jax.named_scope(self.name + "_phase0"):
            sent = self.product(1)
            self.got = swap_phase(sent, self.phases[0])
        return sent

    def keep(self, *earlier):
        if earlier:
            self.terms = [(left, after(right, *earlier)) for left, right in self.terms]
        self.held = [self.product(0)]
        return self.held[0]

    def advance(self, *earlier):
        self.at += 1
        with jax.named_scope(f"{self.name}_phase{self.at}"):
            return self.step(after(self.got, *earlier))

    def rows_sum(self, begin, end):
        return total([a[begin:end].astype(F32) for a in self.held]).astype(LOW)

    def step(self, got):
        spot = self.at - len(self.phases)
        rows = got.shape[0]
        if spot < 0:
            self.held.append(got)
            phases = self.phases[self.at]
            if spot == -1:
                sent = self.rows_sum(0, rows)
                self.held = [sent]
            elif self.at < 3:
                sent = self.rows_sum(rows // 2, rows)
            else:
                mine = per_core(bit_at(phases[0]), bit_at(phases[1]))
                held = self.rows_sum(0, rows)
                sent = pick(held, 1 - mine)
                self.held = [pick(held, mine)]
        else:
            kept = self.held[0]
            if spot == 0:
                low = (kept.astype(F32) + got.astype(F32)).astype(LOW)
            elif spot <= len(self.back) - 2:
                phases = self.back[spot - 1]
                flip = per_core(bit_at(phases[0]), bit_at(phases[1])) == 1
                low = jnp.concatenate(
                    [jnp.where(flip, got, kept), jnp.where(flip, kept, got)], axis=0
                )
            elif spot == len(self.back) - 1:
                low = jnp.concatenate([kept, got], axis=0)
                self.partial = self.spread(low, 0)
            else:
                self.results = self.spread(got, 1, self.partial)
                return self.results[0]
            phases = self.back[spot]
            sent = low
            self.held = [low]
        self.got = swap_phase(sent, phases)
        return sent

    def spread(self, half, index, held=None):
        bits = per_core(*[bit_at(self.first[i]) * 2 + bit_at(self.second[i]) for i in range(2)])
        places = (2 * index + lax.iota(jnp.int32, 2)) ^ bits
        size = half.shape[0] // 2
        rows = 4 * size
        width = half.shape[1]
        held = list(held or [])

        def kernel(place_ref, half_ref, *refs):
            values = half_ref[...].astype(F32)
            for ref, (begin, end, turned) in zip(refs[len(held) :], self.outs):
                ref[...] = values[:, begin:end].T if turned else values[:, begin:end]

        shapes = []
        specs = []
        for begin, end, turned in self.outs:
            if turned:
                shapes.append(jax.ShapeDtypeStruct((end - begin, rows), F32))
                specs.append(pl.BlockSpec((end - begin, size), lambda i, t: (0, t[i])))
            else:
                shapes.append(jax.ShapeDtypeStruct((rows, end - begin), F32))
                specs.append(pl.BlockSpec((size, end - begin), lambda i, t: (t[i], 0)))
        return pl.pallas_call(
            kernel,
            grid_spec=pltpu.PrefetchScalarGridSpec(
                num_scalar_prefetch=1,
                grid=(2,),
                in_specs=[pl.BlockSpec((size, width), lambda i, t: (i, 0))]
                + [pl.BlockSpec(memory_space=pl.ANY)] * len(held),
                out_specs=specs,
            ),
            out_shape=shapes,
            input_output_aliases={2 + k: k for k in range(len(held))},
            cost_estimate=BRIEF,
        )(places, half, *held)


ORDERS_DOWN = [[ROW, 1, 0], [0, ROW, 1]]
ORDERS_UP = [[1, 0, ROW], [0, 1, ROW]]
ORDERS_ATTENTION = [[ROW, 0, 1], [1, ROW, 0]]
TAIL = "UWAAxUWAUWUAAAU"


def body(
    layer_input,
    cotangent,
    lengths,
    dealing,
    w_query,
    w_key,
    w_value,
    bias_query,
    bias_value,
    w_out,
    bias_out,
    w_up,
    bias_up,
    w_down,
    bias_down,
    gain_attention_in,
    shift_attention_in,
    gain_attention_out,
    shift_attention_out,
    gain_ffn_in,
    shift_ffn_in,
    gain_ffn_out,
    shift_ffn_out,
):
    row_count = lax.axis_size("row")
    groups = lax.axis_size("dp")
    shard_count = groups * row_count
    row_index = lax.axis_index("row")
    group_index = lax.axis_index("dp")
    rows = layer_input.shape[0]
    local_width = layer_input.shape[2]
    places = rows // shard_count
    group_rows = rows * row_count

    routes, grid_ofs = route_tables(lengths, dealing, groups, rows, shard_count, row_count)
    place = (routes[:, None] == lax.iota(jnp.int32, rows)[None, :]).astype(LOW)

    def deal(values):
        sent = dot(place, values.reshape(rows, local_width)).astype(LOW)
        sent = sent.reshape(places, shard_count, local_width)
        got = lax.all_to_all(sent, ("dp", "row"), split_axis=1, concat_axis=1, tiled=True)
        return got.reshape(rows, local_width)

    def undo_deal(values, sums=None):
        sent = values.reshape(places, shard_count, local_width)
        if sums is not None:
            copies = (sums.shape[0],) + sent.shape[1:]
            spread = jnp.broadcast_to(sums.astype(LOW)[:, None, :], copies)
            sent = jnp.concatenate([sent, spread], axis=0)
        got = lax.all_to_all(sent, ("dp", "row"), split_axis=1, concat_axis=1, tiled=True)
        back = dot_tokens(place, got[:places].reshape(rows, local_width)).astype(LOW)
        back = back.reshape(rows, 1, local_width)
        if sums is None:
            return back
        return back, jnp.sum(got[places:].astype(F32), axis=1)

    own_ofs = jnp.sum(
        jnp.where((lax.iota(jnp.int32, groups) == group_index)[:, None], grid_ofs, 0), axis=0
    )
    positions = row_index * rows + lax.iota(jnp.int32, rows)
    first = row_index * rows
    post = jnp.where(positions[:, None] >= own_ofs[None, :], own_ofs[None, :], 0)
    begin_post = jnp.max(post, axis=1, keepdims=True) - first
    line = jnp.where(positions[None, :] >= own_ofs[:, None], own_ofs[:, None], 0)
    begin = jnp.max(line, axis=0, keepdims=True) - first

    packed = jnp.stack(
        [
            gain_attention_in,
            shift_attention_in,
            gain_attention_out,
            shift_attention_out,
            gain_ffn_in,
            shift_ffn_in,
            gain_ffn_out,
            shift_ffn_out,
            bias_out,
            bias_down,
        ]
    )
    vectors = col_pieces(packed)
    rest = list(bits_of("dp"))[2:]
    orders_up = [head + rest for head in ORDERS_UP]
    orders_down = [head + rest for head in ORDERS_DOWN]
    orders_attention = [head + rest for head in ORDERS_ATTENTION]
    column = lax.axis_index("col").reshape(1)

    tables = [place_table(o) for o in (orders_attention, orders_up, orders_down)]
    scalars = jnp.concatenate([column] + tables)

    x_own = deal(layer_input)
    x_low_own = lax.ppermute(x_own, "row", [(0, 1)])
    g_own = deal(cotangent)
    x = col_pieces(x_own)
    h1, h1_blocks = row_call(
        norm_in_kernel, scalars, vectors, [x], [(D, LOW), (D, LOW)]
    )
    queries = ((dot(h1, w_query) + bias_query) * (1.0 / math.sqrt(DH))).astype(LOW)
    keys = dot(h1, w_key).astype(LOW)
    values = (dot(h1, w_value) + bias_value).astype(LOW)

    width = queries.shape[1]
    x_low = col_pieces(after(x_low_own, queries))
    (h_low,) = row_call(norm_in_kernel, scalars, vectors, [x_low], [(D, LOW)])
    keys_low = dot(h_low, w_key).astype(LOW)
    values_low = (dot(h_low, w_value) + bias_value).astype(LOW)
    attended, log_total = attend_call(
        forward_kernel,
        rows,
        width,
        ["post"] + ["rows"] * 5,
        [("rows", LOW), ("stat", F32)],
        2 * rows,
    )(begin_post, queries, keys_low, values_low, keys, values)

    branch = col_parts(dot(attended, w_out).astype(LOW))
    h2, h2_blocks, y_own = row_call(
        norm_mid_kernel,
        scalars,
        vectors,
        [branch, x],
        [(D, LOW), (D, LOW), (local_width, F32)],
        1,
    )
    pre = dot(h2, w_up) + bias_up
    cube = math.sqrt(2.0 / math.pi)
    bend = jnp.tanh(cube * (pre + 0.044715 * pre * pre * pre))
    hidden = (0.5 * pre * (1.0 + bend)).astype(LOW)
    slope = 0.5 * (1.0 + bend) + 0.5 * pre * (1.0 - bend * bend) * cube * (
        1.0 + 3.0 * 0.044715 * pre * pre
    )
    slope = slope.astype(LOW)
    ffn = col_parts(dot(hidden, w_down).astype(LOW))
    g = col_pieces(g_own)
    d_ffn, d_ffn_blocks, result, sums4 = row_call(
        norm_out_kernel,
        scalars,
        vectors,
        [ffn, g, [y_own]],
        [(D, LOW), (D, LOW), (local_width, LOW), local_width],
        2,
    )

    ff = hidden.shape[1]
    down = GradSum("down", [(d_ffn_blocks, hidden)], orders_down, [(0, ff, True)])
    tip = down.begin()
    d_pre = dot_back(after(d_ffn, tip), w_down) * slope.astype(F32)
    d_pre = d_pre.astype(LOW)
    up = GradSum("up", [(h2_blocks, d_pre)], orders_up, [(0, ff, False)])
    tip = up.begin()
    d_h2 = col_parts(dot_back(after(d_pre, tip), w_up).astype(LOW))
    kept_down = down.keep(d_h2[0])
    d_branch, d_branch_blocks, d_middle, sums3 = row_call(
        norm_back_kernel,
        scalars,
        vectors,
        [d_h2, g, x, branch],
        [(D, LOW), (D, LOW), (local_width, F32), local_width],
    )
    tip = down.advance(d_branch, kept_down)
    d_attended = dot_back(after(d_branch, tip), w_out).astype(LOW)
    back_ins = ["line"] + ["rows"] * 5 + ["stat"]
    dq_low, dkv_low = attend_call(
        functools.partial(backward_kernel, False),
        rows,
        width,
        back_ins,
        [("cols", F32), ("two", LOW)],
        rows,
    )(begin, queries, keys_low, values_low, d_attended, attended, log_total)
    dkv_back = lax.ppermute(dkv_low, "row", [(1, 0)])
    tip = up.keep(dq_low)
    tip = down.advance(tip)
    d_query, dkv_own = attend_call(
        functools.partial(backward_kernel, True),
        rows,
        width,
        back_ins + ["cols"],
        [("rows", LOW), ("two", LOW)],
        rows,
    )(begin, queries, keys, values, after(d_attended, tip), attended, log_total, dq_low)

    tip = up.advance(d_query)
    tip = down.advance(tip)
    dkv = dkv_own.astype(F32) + after(dkv_back, tip).astype(F32)
    d_key, d_value = dkv[0].astype(LOW), dkv[1].astype(LOW)
    attention = GradSum(
        "attention",
        [
            (h1_blocks, d_query),
            (h1_blocks, d_key),
            (h1_blocks, d_value),
            (d_branch_blocks, attended),
        ],
        orders_attention,
        [(k * width, (k + 1) * width, k == 3) for k in range(4)],
    )
    tip = attention.begin()
    output = undo_deal(after(result, tip))
    d_h1 = dot_back(after(d_query, tip), w_query) + dot_back(d_key, w_key)
    d_h1 = col_parts((d_h1 + dot_back(d_value, w_value)).astype(LOW))
    kept = attention.keep(d_h1[0])
    in_grad, sums1 = row_call(
        norm_last_kernel,
        scalars,
        vectors,
        [d_h1, x, [d_middle]],
        [(local_width, LOW), local_width],
    )
    tip = in_grad
    ready = [in_grad, kept]

    def summed(values):
        return jnp.sum(values.astype(F32), axis=0).reshape(-1, local_width)

    small_rows = [sums1[:2], sums3[:5], sums4[:3]]
    small_rows = small_rows + [summed(d_query), summed(d_value), summed(d_pre)]
    packed_sums = jnp.concatenate(small_rows, axis=0)
    chains = {"W": down, "U": up, "A": attention}
    for name in TAIL:
        if name == "x":
            input_grad, smalls = undo_deal(after(in_grad, tip), packed_sums)
        else:
            tip = chains[name].advance(tip, *ready)
            ready = []
    for chain in chains.values():
        while chain.results is None:
            tip = chain.advance(tip)

    grad_query, grad_key, grad_value, grad_out = attention.results
    (grad_up,) = up.results
    (grad_down,) = down.results
    return (
        output,
        input_grad,
        grad_query,
        grad_key,
        grad_value,
        smalls[10],
        smalls[11],
        grad_out,
        smalls[6],
        grad_up,
        smalls[12:].reshape(-1),
        grad_down,
        smalls[9],
        smalls[0],
        smalls[1],
        smalls[4],
        smalls[5],
        smalls[2],
        smalls[3],
        smalls[7],
        smalls[8],
    )


def solution(mesh):
    shards = P(None, ("dp", "row"), "col")
    by_col = P("col")
    vectors = (by_col,) * 8
    return jax.shard_map(
        body,
        mesh=mesh,
        in_specs=(
            shards,
            shards,
            P(),
            P(),
            P(None, "col"),
            P(None, "col"),
            P(None, "col"),
            by_col,
            by_col,
            P("col", None),
            by_col,
            P(None, "col"),
            by_col,
            P("col", None),
            by_col,
            *vectors,
        ),
        out_specs=(
            shards,
            shards,
            P("row", "col"),
            P("row", "col"),
            P("row", "col"),
            by_col,
            by_col,
            P("col", "row"),
            by_col,
            P("row", "col"),
            by_col,
            P("col", "row"),
            by_col,
            *vectors,
        ),
        check_vma=False,
    )
```
